32 devices in a mesh: row: 4 (over y, x), col: 4 (over z), layer: 2 (over core).
Axes of the slice: x: 2, y: 2, z: 4, core: 2. Of those that a mesh axis runs over, the one named last changes fastest.
Arguments:
- earlier_warming_amount: float32 [8, 512, 512], P('layer', 'row', 'col'), may hold values from -2 to 2
- conductive_capability: float32 [8, 512, 512], P('layer', 'row', 'col'), may hold values from 0.5 to 2
- thermal_mass_timewise: float32 [8, 512, 512], P('layer', 'row', 'col'), may hold values from 0.5 to 2
- toggling_wattage_map: bfloat16 [32, 64, 4096], P(('row', 'col', 'layer')), may hold values from 0.049804688 to 1
- baseline_loss_wattage: bfloat16 [32, 64, 4096], P(('row', 'col', 'layer')), may hold values from 0.049804688 to 1
- receiving_panel: int32 [32, 64, 1], P(('row', 'col', 'layer')), may hold values from 0 to 15; in each aligned block of 64 rows (0 to 63, 64 to 127, ..., all dimensions but the last counted through in order) at most 4 rows name the same one
- subsquare_placement: int32 [32, 64], P(('row', 'col', 'layer')), may hold values from 0 to 3
- holder_chip_module: int32 [32, 64], P(('row', 'col', 'layer')), may hold values from 0 to 15, never falling along the last dimension, each value on 1 to 8 neighbouring positions
- module_tier_order: int32 [32, 16], P(('row', 'col', 'layer')), may hold values from 0 to 3
- warming_sensitivity: float32 [32, 16], P(('row', 'col', 'layer')), may hold values from 0.5 to 2
Outputs:
- new_temperature: float32 [8, 512, 512], P('layer', 'row', 'col')
- supplied_wattage_density: float32 [8, 512, 512], P('layer', 'row', 'col')
The draws below stay inside these ranges and needn't reach their ends.
Inputs may be any that keep to these rules, and one draw needn't show every extreme that they name: `receiving_panel`: the tile is numbered row tile times the number of column tiles plus column tile, inside the owning device's layer group; among the slots of one device at most 4 name the same tile, and exactly 4 do on some device in every draw. `subsquare_placement`: row-major over the tile's patch rows and patch columns. `holder_chip_module`: never falls along a device's slots; every block of a device has 1 to 8 slots.
All inputs are finite; a program needn't handle non-finite values.
Results may differ from the reference program's by a relative error of at most 0.0012.
Values may be sent and summed in bfloat16 or wider, within the bound.
A program may use at most 64 MiB of HBM per device.

```python
import math
import jax
import jax.numpy as jnp
import numpy as np
from jax import lax

SUBSQUARE_EXTENT = 64
CR = 128
CC = 128
CL = 4
SWEEPS = 3
S = 64
NB_DEV = 16
CAP = 4
NLAY = 8
NROWS = 512
NCOLS = 512
N_ROW = 4
N_COL = 4
N_LAYER = 2
DEVICES = 32


def draw_earlier_warming_amount(key, part):
    first_key, second_key = jax.random.split(jax.random.fold_in(key, 11))
    coarse_shape = (NLAY, NROWS // SUBSQUARE_EXTENT, NCOLS // SUBSQUARE_EXTENT)
    coarse = jax.random.uniform(first_key, coarse_shape, jnp.float32, -1.0, 1.0)
    fine = 0.3 * jnp.clip(jax.random.normal(second_key, (NLAY, NROWS, NCOLS), jnp.float32), -3.0, 3.0)
    spread_out = jnp.repeat(jnp.repeat(coarse, SUBSQUARE_EXTENT, axis=1), SUBSQUARE_EXTENT, axis=2)
    return spread_out + fine


def touch_ends(values, key, least, top_value):
    shape = values.shape
    place = [jax.random.randint(jax.random.fold_in(key, axis), (), 0, shape[axis]) for axis in range(len(shape))]
    values = values.at[tuple(place)].set(least)
    longest = shape.index(max(shape))
    place[longest] = (place[longest] + 1) % shape[longest]
    return values.at[tuple(place)].set(top_value)


def level_of(rng, shape, cuts, low, high):
    gain = 1.0
    for position, blocks in cuts:
        draws = jax.random.uniform(jax.random.fold_in(jax.random.fold_in(rng, 6), position), (blocks,), jnp.float32, low / len(cuts), high / len(cuts))
        gain = gain * jnp.repeat(jnp.exp(draws), shape[position] // blocks).reshape((-1,) + (1,) * (len(shape) - 1 - position))
    return gain


def split_up(count, total, reach, lean):
    loads = [(1 << 20) // math.isqrt(rank ** lean) + 1 for rank in range(2, count + 1)]
    rest, holding = total - reach - (count - 1), [1] * (count - 1)
    while rest > 0:
        free = [i for i in range(count - 1) if holding[i] < reach]
        mass, budget = sum([loads[i] for i in free]), rest
        for i in free:
            more = min(reach - holding[i], max(1, budget * loads[i] // mass), rest)
            holding[i] = holding[i] + more
            rest = rest - more
    return np.array([reach] + holding)


def ragged_sizes(stream_key, number_of, total, bound, slope):
    if number_of == 2:
        one = jax.random.randint(stream_key, (), max(1, total - bound), min(bound, total - 1) + 1)
        return jnp.stack([one, total - one])
    sizes = jnp.asarray(split_up(number_of, total, bound, slope), jnp.int32)
    pairs = (number_of - 1) // 2
    source_of, taker = sizes[1:1 + 2 * pairs:2], sizes[2:2 + 2 * pairs:2]
    margin = jnp.minimum(source_of - 1, bound - taker)
    shifted = jax.random.randint(jax.random.fold_in(stream_key, 1), (pairs,), 0, 1 << 20) % (margin + 1)
    sizes = sizes.at[1:1 + 2 * pairs:2].set(source_of - shifted).at[2:2 + 2 * pairs:2].set(taker + shifted)
    return sizes[jax.random.permutation(jax.random.fold_in(stream_key, 2), number_of)]


def routed_block(stream_key, own, number, rows, count, top, reach, skew):
    sequence = jax.random.permutation(stream_key, count)
    crowded, common = load_shares(count, rows * top, reach, skew, True), load_shares(count, rows * top, reach, skew, False)
    places = jnp.arange(count)

    def named(lengths, turn):
        used = int((lengths > 0).sum())
        fixed = max(1, used // 4)
        passed = fixed + (places - fixed + turn * (used - fixed)) % max(1, count - fixed)
        return jnp.zeros((count,), jnp.int32).at[sequence[jnp.where(places < fixed, places, passed)]].set(jnp.asarray(lengths, jnp.int32))

    lengths = jnp.where(number % 4 == 0, named(crowded, number // 4), named(common, number - number // 4 - 1))
    mixed = jax.random.permutation(jax.random.fold_in(own, 3), count)
    donor, taker = mixed[0:count // 2 * 2:2], mixed[1:count // 2 * 2:2]
    room = jnp.minimum(lengths[donor] - 1, reach - lengths[taker]) // 2
    room = jnp.where((donor == sequence[0]) | (taker == sequence[0]) | (lengths[taker] == 0), 0, jnp.maximum(room, 0))
    passed = jax.random.randint(jax.random.fold_in(own, 4), (count // 2,), 0, 1 << 20) % (room + 1)
    lengths = lengths.at[donor].add(-passed).at[taker].add(passed)
    members = jnp.searchsorted(jnp.cumsum(lengths), jnp.arange(rows * top), side="right").astype(jnp.int32)
    listing = members.reshape(top, rows).T
    listing = listing[jax.random.permutation(jax.random.fold_in(own, 1), rows)]
    turn = jax.random.randint(jax.random.fold_in(own, 2), (rows, 1), 0, top)
    return jnp.take_along_axis(listing, (jnp.arange(top)[None, :] + turn) % top, axis=1)


def load_shares(amount, total, most, skew, full):
    loads = [(1 << 20) // math.isqrt(rank ** skew) + 1 for rank in range(1, amount + 1)]
    largest = most if full else min(most, max(-(-total // amount), total * loads[0] // sum(loads)))
    least = 1 if total - largest >= amount - 1 else 0
    holding, rest = [largest] + [least] * (amount - 1), total - largest - least * (amount - 1)
    while rest > 0:
        free = [i for i in range(1, amount) if holding[i] < largest] or [i for i in range(1, amount) if holding[i] < most]
        whole, remaining = sum([loads[i] for i in free]), rest
        for i in free:
            more = min(most - holding[i], max(1, remaining * loads[i] // whole), rest)
            holding[i] = holding[i] + more
            rest = rest - more
    return np.array(holding)


def setup_inputs(seed: int = 0) -> dict:
    keys = jax.random.split(jax.random.key(seed), 11)
    earlier_warming_amount = draw_earlier_warming_amount(jax.random.fold_in(keys[10], 71), 0)
    conductive_capability = jnp.clip(jnp.exp(math.log(2.0) - 1.3862944 * jax.random.uniform(keys[1], (NLAY, NROWS, NCOLS), jnp.float32) ** level_of(keys[1], (NLAY, NROWS, NCOLS), ((0, 2), (1, 4), (2, 4)), -0.2, 0.2)), 0.5, 2.0)
    thermal_mass_timewise = jnp.clip(0.5 + 1.5 * jax.random.uniform(keys[2], (NLAY, NROWS, NCOLS), jnp.float32) ** level_of(keys[2], (NLAY, NROWS, NCOLS), ((0, 2), (1, 4), (2, 4)), -0.2, 0.2), 0.5, 2.0)
    toggling_wattage_map = jnp.clip(jnp.exp(math.log(1.0) - 2.9996462 * jax.random.uniform(keys[3], (DEVICES, S, SUBSQUARE_EXTENT * SUBSQUARE_EXTENT), jnp.float32) ** level_of(keys[3], (DEVICES, S, SUBSQUARE_EXTENT * SUBSQUARE_EXTENT), ((0, 32),), -0.2, 0.2)), 0.049804688, 1.0).astype(jnp.bfloat16)
    baseline_loss_wattage = jnp.clip(jnp.exp(math.log(1.0) - 2.9996462 * jax.random.uniform(keys[4], (DEVICES, S, SUBSQUARE_EXTENT * SUBSQUARE_EXTENT), jnp.float32) ** level_of(keys[4], (DEVICES, S, SUBSQUARE_EXTENT * SUBSQUARE_EXTENT), ((0, 32),), -0.2, 0.2)), 0.049804688, 1.0).astype(jnp.bfloat16)
    receiving_panel_keys = jax.random.split(jax.random.fold_in(keys[5], 1), DEVICES * S // S)
    receiving_panel_turns = jax.random.permutation(jax.random.fold_in(keys[5], 3), DEVICES * S // S)
    receiving_panel = jax.vmap(lambda own, number: routed_block(jax.random.fold_in(keys[5], 2), own, number, S, N_ROW * N_COL, 1, CAP, 2))(receiving_panel_keys, receiving_panel_turns).reshape((DEVICES, S, 1))
    subsquare_placement = touch_ends(jax.random.randint(keys[6], (DEVICES, S), 0, (CR // SUBSQUARE_EXTENT) * (CC // SUBSQUARE_EXTENT)), jax.random.fold_in(keys[6], 1), 0, ((CR // SUBSQUARE_EXTENT) * (CC // SUBSQUARE_EXTENT)) - 1).astype(jnp.int32)
    holder_chip_module = jax.vmap(lambda own: jnp.searchsorted(jnp.cumsum(ragged_sizes(own, NB_DEV, S, 2 * S // NB_DEV, 2)), jnp.arange(S), side="right"))(jax.random.split(keys[7], DEVICES)).reshape((DEVICES, S)).astype(jnp.int32)
    module_tier_order = touch_ends(jax.random.randint(keys[8], (DEVICES, NB_DEV), 0, CL), jax.random.fold_in(keys[8], 1), 0, CL - 1).astype(jnp.int32)
    warming_sensitivity = jnp.clip(jnp.exp(math.log(2.0) - 1.3862944 * jax.random.uniform(keys[9], (DEVICES, NB_DEV), jnp.float32) ** level_of(keys[9], (DEVICES, NB_DEV), ((0, 32),), -0.2, 0.2)), 0.5, 2.0)
    return dict(earlier_warming_amount=earlier_warming_amount, conductive_capability=conductive_capability, thermal_mass_timewise=thermal_mass_timewise, toggling_wattage_map=toggling_wattage_map, baseline_loss_wattage=baseline_loss_wattage, receiving_panel=receiving_panel, subsquare_placement=subsquare_placement, holder_chip_module=holder_chip_module, module_tier_order=module_tier_order, warming_sensitivity=warming_sensitivity)


eig_low = 0.1
eig_high = 2.0


def neighbours(padded):
    return [padded[2:, 1:-1, 1:-1], padded[:-2, 1:-1, 1:-1], padded[1:-1, 2:, 1:-1],
            padded[1:-1, :-2, 1:-1], padded[1:-1, 1:-1, 2:], padded[1:-1, 1:-1, :-2]]


def face_terms(padded_cond):
    center = padded_cond[1:-1, 1:-1, 1:-1]
    return [0.5 * (center + beside) for beside in neighbours(padded_cond)]


def diagonal_of(thermal_mass_timewise, nearby_conductance_factors):
    running = thermal_mass_timewise
    for face_term in nearby_conductance_factors:
        running = running + face_term
    return running


def linear_mapping_result(padded, nearby_conductance_factors, linear_pivot_coefficients):
    result = linear_pivot_coefficients * padded[1:-1, 1:-1, 1:-1]
    for face_term, beside in zip(nearby_conductance_factors, neighbours(padded)):
        result = result - face_term * beside
    return result


def reference(earlier_warming_amount, conductive_capability, thermal_mass_timewise, toggling_wattage_map, baseline_loss_wattage, receiving_panel, subsquare_placement, holder_chip_module, module_tier_order, warming_sensitivity):
    third_axis_extent, first_axis_extent, second_axis_extent = earlier_warming_amount.shape
    subsquares_eastward = first_axis_extent // SUBSQUARE_EXTENT
    subsquares_northward = second_axis_extent // SUBSQUARE_EXTENT
    slots_all = DEVICES * S
    owner = jnp.arange(slots_all, dtype=jnp.int32) // S
    owner_group = owner % N_LAYER
    target = receiving_panel.reshape(slots_all).astype(jnp.int32)
    local_block = holder_chip_module.reshape(slots_all).astype(jnp.int32)
    global_block = owner * NB_DEV + local_block
    die_layer = module_tier_order.reshape(DEVICES * NB_DEV)[global_block] + owner_group * CL
    offsets = subsquare_placement.reshape(slots_all)
    patch_row = (target // N_COL) * (CR // SUBSQUARE_EXTENT) + offsets // (CC // SUBSQUARE_EXTENT)
    patch_col = (target % N_COL) * (CC // SUBSQUARE_EXTENT) + offsets % (CC // SUBSQUARE_EXTENT)
    patch_index = ((die_layer * subsquares_eastward + patch_row) * subsquares_northward + patch_col).astype(jnp.int32)
    subsquare_averaged = earlier_warming_amount.reshape(third_axis_extent, subsquares_eastward, SUBSQUARE_EXTENT, subsquares_northward, SUBSQUARE_EXTENT).mean(axis=(2, 4)).reshape(-1)
    slot_means = subsquare_averaged[patch_index]
    blocks_all = DEVICES * NB_DEV
    block_sums = jax.ops.segment_sum(slot_means, global_block, num_segments=blocks_all)
    block_sizes = jax.ops.segment_sum(jnp.ones((slots_all,), jnp.float32), global_block, num_segments=blocks_all)
    factor = jnp.exp(warming_sensitivity.reshape(blocks_all) * (block_sums / block_sizes))
    slot_power = toggling_wattage_map.reshape(slots_all, SUBSQUARE_EXTENT * SUBSQUARE_EXTENT).astype(jnp.float32) + factor[global_block][:, None] * baseline_loss_wattage.reshape(slots_all, SUBSQUARE_EXTENT * SUBSQUARE_EXTENT).astype(jnp.float32)
    slot_power = lax.optimization_barrier(slot_power.astype(jnp.bfloat16)).astype(jnp.float32)
    footprint_wattage = jax.ops.segment_sum(slot_power, patch_index, num_segments=third_axis_extent * subsquares_eastward * subsquares_northward)
    supplied_wattage_density = footprint_wattage.reshape(third_axis_extent, subsquares_eastward, subsquares_northward, SUBSQUARE_EXTENT, SUBSQUARE_EXTENT).transpose(0, 1, 3, 2, 4).reshape(third_axis_extent, first_axis_extent, second_axis_extent)
    nearby_conductance_factors = face_terms(jnp.pad(conductive_capability, 1))
    linear_pivot_coefficients = diagonal_of(thermal_mass_timewise, nearby_conductance_factors)
    middle = (eig_low + eig_high) / 2.0
    spread = (eig_high - eig_low) / 2.0
    ratio_sigma = middle / spread
    weight_now = 1.0 / ratio_sigma
    iterate_guess = earlier_warming_amount
    remaining_imbalance = thermal_mass_timewise * earlier_warming_amount + supplied_wattage_density - linear_mapping_result(jnp.pad(iterate_guess, 1), nearby_conductance_factors, linear_pivot_coefficients)
    direction = remaining_imbalance / (linear_pivot_coefficients * middle)
    for sweep in range(SWEEPS):
        iterate_guess = iterate_guess + direction
        if sweep < SWEEPS - 1:
            remaining_imbalance = remaining_imbalance - linear_mapping_result(jnp.pad(direction, 1), nearby_conductance_factors, linear_pivot_coefficients)
            weight_new = 1.0 / (2.0 * ratio_sigma - weight_now)
            direction = weight_new * weight_now * direction + (2.0 * weight_new / spread) * (remaining_imbalance / linear_pivot_coefficients)
            weight_now = weight_new
    return iterate_guess, supplied_wattage_density
```

```python
import functools
import jax
import jax.numpy as jnp
from jax import lax
from jax.experimental import pallas as pl
from jax.experimental.pallas import tpu as pltpu
from jax.sharding import PartitionSpec as P

SUB = 64
SWEEPS = 3
CAP = 4
EIG_LOW = 0.1
EIG_HIGH = 2.0
LANES = 128
PACK = 16
VMEM_BYTES = 16 << 20

MESH = pl.DeviceIdType.MESH
F32 = jnp.float32
BF16 = jnp.bfloat16


def iota(shape, dim):
    return lax.broadcasted_iota(jnp.int32, shape, dim)


def hi_dot(a, b, dims):
    return lax.dot_general(
        a, b, (dims, ((), ())), precision=lax.Precision.HIGHEST, preferred_element_type=F32
    )


def div(x, n):
    if n & (n - 1):
        return x // n
    return lax.shift_right_logical(x, jnp.int32(n.bit_length() - 1))


def mod(x, n):
    if n & (n - 1):
        return lax.rem(x, n)
    return x & (n - 1)


def two_parts(x, axis):
    head = x.astype(BF16)
    return jnp.concatenate([head, (x - head.astype(F32)).astype(BF16)], axis=axis)


def kernel(
    sizes,
    temp_hbm,
    cond_hbm,
    mass_hbm,
    dyn_hbm,
    leak_hbm,
    panel_hbm,
    place_hbm,
    block_hbm,
    tier_hbm,
    sens_hbm,
    out_ref,
    power_ref,
    panel_ref,
    place_ref,
    block_ref,
    tier_ref,
    sens_ref,
    temp,
    cond,
    mass,
    dyn,
    leak,
    note_send,
    note_recv,
    load_send,
    load_recv,
    dirs,
    faces,
    diag,
    inv,
    resid,
    edge_send,
    edge_recv,
    plane_recv,
    in_sem,
    note_ssem,
    note_rsem,
    load_ssem,
    load_rsem,
    halo_ssem,
    halo_rsem,
):
    n_row, n_col, n_layer = sizes
    tiles = n_row * n_col
    tiers, rows, cols = temp.shape
    slots, cells = dyn.shape
    folds = PACK // CAP
    wide = cells // folds
    note_rows = note_send.shape[0] // tiles
    in_plane = (rows // SUB) * (cols // SUB)
    patches = tiers * in_plane
    bands = tiers * (rows // SUB)
    chunks = tiles * PACK // LANES

    my_row = lax.axis_index("row")
    my_col = lax.axis_index("col")
    my_layer = lax.axis_index("layer")
    me = my_row * n_col + my_col

    loads = [
        pltpu.make_async_copy(src, dst, in_sem.at[i])
        for i, (src, dst) in enumerate(
            (
                (panel_hbm, panel_ref),
                (place_hbm, place_ref),
                (block_hbm, block_ref),
                (tier_hbm, tier_ref),
                (sens_hbm, sens_ref),
                (temp_hbm, temp),
                (cond_hbm, cond),
                (dyn_hbm.at[0], dyn),
                (leak_hbm.at[0], leak),
                (mass_hbm, mass),
            )
        )
    ]
    for load in loads:
        load.start()

    def peer(step):
        other = lax.rem(me + step, tiles)
        return other, {"row": other // n_col, "col": lax.rem(other, n_col)}

    sides = (
        (my_layer > 0, {"layer": my_layer - 1}, 0),
        (my_layer < n_layer - 1, {"layer": my_layer + 1}, 1),
        (my_row > 0, {"row": my_row - 1}, 2),
        (my_row < n_row - 1, {"row": my_row + 1}, 3),
        (my_col > 0, {"col": my_col - 1}, 4),
        (my_col < n_col - 1, {"col": my_col + 1}, 5),
    )

    barrier = pltpu.get_barrier_semaphore()

    @pl.loop(1, tiles)
    def _(step):
        _, where = peer(step)
        pl.semaphore_signal(barrier, inc=1, device_id=where, device_id_type=MESH)

    for exists, where, side in sides[:2]:

        @pl.when(exists)
        def _(where=where):
            pl.semaphore_signal(barrier, inc=1, device_id=where, device_id_type=MESH)

    for turn in range(4):
        for exists, _, side in sides:

            @pl.when(jnp.logical_not(exists))
            def _(turn=turn, side=side):
                if side < 2:
                    plane_recv[turn, side] = jnp.zeros((rows, cols), F32)
                else:
                    edge_recv[turn, side - 2] = jnp.zeros(edge_recv.shape[2:], F32)

    lane_s = iota((slots, slots), 1)
    sub_s = iota((slots, slots), 0)
    eye = lane_s == sub_s

    def to_col(row):
        return jnp.sum(jnp.where(eye, jnp.broadcast_to(row, (slots, slots)), 0.0), axis=1, keepdims=True)

    def to_row(col):
        return jnp.sum(jnp.where(eye, jnp.broadcast_to(col, (slots, slots)), 0.0), axis=0, keepdims=True)

    for load in loads[:5]:
        load.wait()
    tgt_row = panel_ref[...].astype(F32)
    tgt_col = to_col(tgt_row)
    blk_row = block_ref[...].astype(F32)
    blk_col = to_col(blk_row)
    sub_col = to_col(place_ref[...].astype(F32))
    same_tile = tgt_col == tgt_row
    rank_col = jnp.sum(jnp.where(same_tile & (lane_s < sub_s), 1.0, 0.0), axis=1, keepdims=True)
    rank_row = jnp.sum(jnp.where(same_tile & (sub_s < lane_s), 1.0, 0.0), axis=0, keepdims=True)
    blocks = tier_ref.shape[1]
    of_block = blk_col == iota((slots, blocks), 1).astype(F32)
    tier_col = jnp.sum(jnp.where(of_block, tier_ref[...].astype(F32), 0.0), axis=1, keepdims=True)
    sens_col = jnp.sum(jnp.where(of_block, sens_ref[...], 0.0), axis=1, keepdims=True)
    pos_col = tier_col * in_plane + sub_col
    same_block = jnp.where(blk_col == blk_row, 1.0, 0.0)
    block_size = jnp.sum(same_block, axis=1, keepdims=True)

    offset = lax.rem(me * PACK, LANES)
    my_chunk = (me * PACK) // LANES
    rel = iota((slots, LANES), 1) - offset
    fits = (rel >= 0) & (rel < PACK) & ((rel & (CAP - 1)).astype(F32) == rank_col)
    place_lanes = jnp.where(fits, pos_col + 1.0, 0.0)
    note_i = iota((tiles * note_rows, slots), 0)
    to_tile = jnp.where(
        (div(note_i, note_rows).astype(F32) == tgt_row) & (mod(note_i, note_rows) == 1 + my_chunk),
        1.0,
        0.0,
    )
    places = jnp.dot(to_tile.astype(BF16), place_lanes.astype(BF16), preferred_element_type=F32)

    loads[5].wait()
    band_sums = jnp.concatenate(
        [
            jnp.sum(temp[t, b * SUB : (b + 1) * SUB, :], axis=0, keepdims=True)
            for t in range(tiers)
            for b in range(rows // SUB)
        ],
        axis=0,
    )
    lane_b = iota((bands, LANES), 1)
    sub_b = iota((bands, LANES), 0)
    means = jnp.zeros((1, LANES), F32)
    per_band = cols // SUB
    for part in range(per_band):
        total = jnp.sum(jnp.where(div(lane_b, SUB) == part, band_sums, 0.0), axis=1, keepdims=True)
        means = means + jnp.sum(
            jnp.where(lane_b == sub_b * per_band + part, total, 0.0), axis=0, keepdims=True
        )
    means = means * (1.0 / (SUB * SUB))
    note_j = iota((tiles * note_rows, LANES), 0)
    note_send[...] = places + jnp.where(mod(note_j, note_rows) == 0, means, 0.0)

    sub8 = iota((2 * tiers, 2 * cols), 0)
    lane8 = mod(iota((2 * tiers, 2 * cols), 1), cols)
    picks = [
        jnp.where(
            ((sub8 == t) & (lane8 == 0)) | ((sub8 == tiers + t) & (lane8 == cols - 1)), 1.0, 0.0
        ).astype(BF16)
        for t in range(tiers)
    ]

    def halo_copy(turn, field, where, side, lands):
        if side < 2:
            src = field.at[0 if side == 0 else tiers - 1]
            dst = plane_recv.at[turn, lands]
        else:
            src = edge_send.at[turn, (side - 2) // 2]
            dst = edge_recv.at[turn, lands - 2]
        return pltpu.make_async_remote_copy(
            src_ref=src,
            dst_ref=dst,
            send_sem=halo_ssem.at[turn, side],
            recv_sem=halo_rsem.at[turn, lands],
            device_id=where,
            device_id_type=MESH,
        )

    def pack_rows(turn, field):
        for end in range(2):
            at = end * (rows - 1)
            for t in range(tiers):
                edge_send[turn, 0, end * tiers + t : end * tiers + t + 1, :] = field[t, at : at + 1, :]

    def pack_columns(turn, field):
        columns = jnp.zeros((2 * tiers, rows), F32)
        for t in range(tiers):
            columns = columns + lax.dot_general(
                picks[t], two_parts(field[t], 1), (((1,), (1,)), ((), ())), preferred_element_type=F32
            )
        edge_send[turn, 1] = columns

    def each_side(act, which=sides):
        for exists, where, side in which:
            pl.when(exists)(functools.partial(act, where, side))

    def start_halo(turn, field):
        def start(where, side):
            halo_copy(turn, field, where, side, side ^ 1).start()

        pack_rows(turn, field)
        each_side(start, sides[2:4])
        each_side(start, sides[:2])
        pack_columns(turn, field)
        each_side(start, sides[4:])

    def wait_halo(turn, field):
        each_side(lambda where, side: halo_copy(turn, field, where, side, side).wait_recv())

    def end_halo(turn, field):
        each_side(lambda where, side: halo_copy(turn, field, where, side, side ^ 1).wait_send())

    row_i = iota((rows, cols), 0)
    col_i = iota((rows, cols), 1)
    sub16 = mod(iota((8 * tiers, tiers * cols), 0), 4 * tiers)
    lane16 = iota((8 * tiers, tiers * cols), 1)
    put = jnp.where(
        ((mod(lane16, cols) == 0) & (sub16 == tiers + div(lane16, cols)))
        | ((mod(lane16, cols) == cols - 1) & (sub16 == 2 * tiers + div(lane16, cols))),
        1.0,
        0.0,
    ).astype(BF16)

    def inside(field, t):
        v = field[t]
        none = jnp.zeros_like(v)
        low = none if t == 0 else field[t - 1]
        high = none if t == tiers - 1 else field[t + 1]
        north = jnp.where(row_i == 0, 0.0, pltpu.roll(v, 1, 0))
        south = jnp.where(row_i == rows - 1, 0.0, pltpu.roll(v, rows - 1, 0))
        west = jnp.where(col_i == 0, 0.0, pltpu.roll(v, 1, 1))
        east = jnp.where(col_i == cols - 1, 0.0, pltpu.roll(v, cols - 1, 1))
        return v, (low, high, north, south, west, east)

    def rims(turn):
        ends = jnp.concatenate([edge_recv[turn, 2], edge_recv[turn, 3]], axis=0)
        return lax.dot_general(
            two_parts(ends, 0), put, (((0,), (0,)), ((), ())), preferred_element_type=F32
        )

    def apply_inside(field, t):
        v, around = inside(field, t)
        value = diag[t] * v
        for k in range(6):
            if not (k == 0 and t == 0 or k == 1 and t == tiers - 1):
                value = value - faces[k, t] * around[k]
        return value

    def add_beyond(turn):
        rim = rims(turn)
        resid[0] = resid[0] + faces[0, 0] * plane_recv[turn, 0]
        resid[tiers - 1] = resid[tiers - 1] + faces[1, tiers - 1] * plane_recv[turn, 1]
        for t in range(tiers):
            first, last = slice(0, 1), slice(rows - 1, rows)
            resid[t, first, :] = (
                resid[t, first, :] + faces[2, t, first, :] * edge_recv[turn, 0, tiers + t : tiers + t + 1, :]
            )
            resid[t, last, :] = (
                resid[t, last, :] + faces[3, t, last, :] * edge_recv[turn, 1, t : t + 1, :]
            )
            face = jnp.where(col_i == 0, faces[4, t], faces[5, t])
            resid[t] = resid[t] + face * rim[:, t * cols : (t + 1) * cols]

    beyond = (my_layer > 0).astype(jnp.int32) + (my_layer < n_layer - 1).astype(jnp.int32)
    pl.semaphore_wait(barrier, tiles - 1 + beyond)

    def note_copy(step):
        other, where = peer(step)
        return pltpu.make_async_remote_copy(
            src_ref=note_send.at[pl.ds(other * note_rows, note_rows), :],
            dst_ref=note_recv.at[pl.ds(me * note_rows, note_rows), :],
            send_sem=note_ssem.at[step],
            recv_sem=note_rsem.at[step],
            device_id=where,
            device_id_type=MESH,
        )

    def load_copy(other, lands):
        return pltpu.make_async_remote_copy(
            src_ref=load_send.at[pl.ds(other * PACK, PACK), :],
            dst_ref=load_recv.at[pl.ds(me * PACK, PACK), :],
            send_sem=load_ssem.at[other],
            recv_sem=load_rsem.at[lands],
            device_id={"row": div(other, n_col), "col": mod(other, n_col)},
            device_id_type=MESH,
        )

    @pl.loop(1, tiles)
    def _(step):
        note_copy(step).start()

    own_note = pl.ds(pl.multiple_of(me * note_rows, note_rows), note_rows)
    own_copy = pltpu.make_async_copy(note_send.at[own_note, :], note_recv.at[own_note, :], note_rsem.at[0])
    own_copy.start()

    loads[6].wait()
    start_halo(0, temp)
    start_halo(1, cond)
    loads[7].wait()
    loads[8].wait()
    note_k = iota((slots, tiles * note_rows), 1)
    from_tile = jnp.where(
        (div(note_k, note_rows).astype(F32) == tgt_col) & (mod(note_k, note_rows) == 0), 1.0, 0.0
    )
    at_place = iota((slots, LANES), 1).astype(F32) == pos_col
    send_i = iota((tiles * PACK, folds * slots), 0)
    send_j = iota((tiles * PACK, folds * slots), 1)
    slot_place = jnp.concatenate([tgt_row * CAP + rank_row] * folds, axis=1)
    goes = (div(send_i, PACK) * CAP + mod(send_i, CAP)).astype(F32) == slot_place
    pick = jnp.where(goes & (div(mod(send_i, PACK), CAP) == div(send_j, slots)), 1.0, 0.0).astype(BF16)
    own_copy.wait()

    @pl.loop(1, tiles)
    def _(step):
        note_copy(step).wait_recv()

    tile_means = hi_dot(from_tile, note_recv[...], ((1,), (0,)))
    slot_mean = jnp.sum(jnp.where(at_place, tile_means, 0.0), axis=1, keepdims=True)
    block_rise = jnp.sum(same_block * to_row(slot_mean), axis=1, keepdims=True) / block_size
    factor = jnp.exp(sens_col * block_rise)
    half = wide // 2
    for piece in range(2):
        slot_power = jnp.concatenate(
            [
                (
                    dyn[:, fold * wide + piece * half : fold * wide + (piece + 1) * half].astype(F32)
                    + factor
                    * leak[:, fold * wide + piece * half : fold * wide + (piece + 1) * half].astype(F32)
                ).astype(BF16)
                for fold in range(folds)
            ],
            axis=0,
        )
        load_send[:, piece * half : (piece + 1) * half] = jnp.dot(
            pick, slot_power, preferred_element_type=F32
        ).astype(BF16)

    @pl.loop(0, tiles)
    def _(step):
        nth = div(step, n_row)
        far = jnp.where(my_col < n_col // 2, n_col - 1 - nth, nth)
        other = lax.rem(my_row + lax.rem(step, n_row), n_row) * n_col + far

        @pl.when(other != me)
        def _():
            load_copy(other, me).start()

    own_load = pl.ds(pl.multiple_of(me * PACK, PACK), PACK)
    own_move = pltpu.make_async_copy(load_send.at[own_load, :], load_recv.at[own_load, :], load_rsem.at[me])
    own_move.start()

    loads[9].wait()
    wait_halo(0, temp)
    wait_halo(1, cond)
    rim = rims(1)
    for t in range(tiers):
        c, (low, high, north, south, west, east) = inside(cond, t)
        here = rim[:, t * cols : (t + 1) * cols]
        low = plane_recv[1, 0] if t == 0 else low
        high = plane_recv[1, 1] if t == tiers - 1 else high
        north = jnp.where(row_i == 0, edge_recv[1, 0, tiers + t : tiers + t + 1, :], north)
        south = jnp.where(row_i == rows - 1, edge_recv[1, 1, t : t + 1, :], south)
        west = jnp.where(col_i == 0, here, west)
        east = jnp.where(col_i == cols - 1, here, east)
        total = mass[t]
        for k, beside in enumerate((low, high, north, south, west, east)):
            face = 0.5 * (c + beside)
            faces[k, t] = face
            total = total + face
        diag[t] = total
        inv[t] = 1.0 / total
    for t in range(tiers):
        resid[t] = mass[t] * temp[t] - apply_inside(temp, t)
    add_beyond(0)

    middle = (EIG_LOW + EIG_HIGH) / 2.0
    spread = (EIG_HIGH - EIG_LOW) / 2.0
    ratio = middle / spread
    weight = 1.0 / ratio

    sel_i = iota((folds * patches, LANES), 0)
    sel_j = iota((folds * patches, LANES), 1)
    sel_in = mod(sel_i, patches)
    sel_patch = mod(sel_in, bands) * per_band + div(sel_in, bands)
    fold_hit = div(sel_i, patches) == div(mod(sel_j, PACK), CAP)
    notes = note_recv[...]
    pickers = []
    for chunk in range(chunks):
        code = jnp.sum(jnp.where(mod(note_j, note_rows) == 1 + chunk, notes, 0.0), axis=0, keepdims=True)
        pickers.append(
            jnp.where(fold_hit & (code == (sel_patch + 1).astype(F32)), 1.0, 0.0).astype(BF16)
        )

    picker = jnp.concatenate(pickers, axis=1)
    own_move.wait()

    @pl.loop(1, tiles)
    def _(step):
        other, _ = peer(step)
        load_copy(other, other).wait_recv()

    footprint = jnp.dot(picker, load_recv[...], preferred_element_type=F32)
    left = iota((bands, LANES), 1) < SUB
    for fold in range(folds):
        for k in range(wide // LANES):
            lanes = slice(k * LANES, (k + 1) * LANES)
            a = footprint[fold * patches : fold * patches + bands, lanes]
            b = footprint[fold * patches + bands : fold * patches + 2 * bands, lanes]
            at = 2 * (fold * (wide // LANES) + k)
            power_ref[pl.ds(at, bands, stride=SUB), :] = jnp.where(left, a, pltpu.roll(b, SUB, 1))
            power_ref[pl.ds(at + 1, bands, stride=SUB), :] = jnp.where(left, pltpu.roll(a, SUB, 1), b)

    for t in range(tiers):
        r = resid[t] + power_ref[t * rows : (t + 1) * rows, :]
        resid[t] = r
        dirs[0, t] = r * inv[t] * (1.0 / middle)
    for sweep in range(1, SWEEPS):
        field = dirs.at[sweep - 1]
        turn = 1 + sweep
        start_halo(turn, field)
        weight_new = 1.0 / (2.0 * ratio - weight)
        for t in range(tiers):
            base = temp[t] if sweep == 1 else out_ref[t]
            out_ref[t] = base + field[t]
            resid[t] = resid[t] - apply_inside(field, t)
        wait_halo(turn, field)
        add_beyond(turn)
        for t in range(tiers):
            d = weight_new * weight * field[t] + (2.0 * weight_new / spread) * (resid[t] * inv[t])
            if sweep < SWEEPS - 1:
                dirs[sweep, t] = d
            else:
                out_ref[t] = out_ref[t] + d
        weight = weight_new
    end_halo(0, temp)
    end_halo(1, cond)
    for sweep in range(1, SWEEPS):
        end_halo(1 + sweep, dirs.at[sweep - 1])

    @pl.loop(1, tiles)
    def _(step):
        note_copy(step).wait_send()
        other, _ = peer(step)
        load_copy(other, me).wait_send()


def hand_over(new, power, new_out, power_out, sem):
    moves = (pltpu.make_async_copy(power, power_out, sem.at[0]), pltpu.make_async_copy(new, new_out, sem.at[1]))
    for move in moves:
        move.start()
    for move in moves:
        move.wait()


def shards(sizes, temp, cond, mass, dyn, leak, panel, place, block, tier, sens):
    tiers, rows, cols = temp.shape
    slots, cells = dyn.shape[1:]
    tiles = sizes[0] * sizes[1]
    folds = PACK // CAP
    note_rows = -(-(1 + tiles * PACK // LANES) // 8) * 8
    any_spec = pl.BlockSpec(memory_space=pl.ANY)
    vmem_spec = pl.BlockSpec(memory_space=pltpu.VMEM)
    grid = (tiers, rows, cols)
    dma = pltpu.SemaphoreType.DMA
    new, power = pl.pallas_call(
        functools.partial(kernel, sizes),
        out_shape=(
            pltpu.VMEM(grid, F32),
            pltpu.VMEM((tiers * rows, cols), F32),
        ),
        in_specs=[any_spec] * 10,
        out_specs=(vmem_spec, vmem_spec),
        scratch_shapes=[
            pltpu.VMEM((1, slots), jnp.int32),
            pltpu.VMEM((1, slots), jnp.int32),
            pltpu.VMEM((1, slots), jnp.int32),
            pltpu.VMEM(tier.shape, jnp.int32),
            pltpu.VMEM(sens.shape, F32),
            pltpu.VMEM(grid, F32),
            pltpu.VMEM(grid, F32),
            pltpu.VMEM(grid, F32),
            pltpu.VMEM((slots, cells), BF16),
            pltpu.VMEM((slots, cells), BF16),
            pltpu.VMEM((tiles * note_rows, LANES), F32),
            pltpu.VMEM((tiles * note_rows, LANES), F32),
            pltpu.VMEM((tiles * PACK, cells // folds), BF16),
            pltpu.VMEM((tiles * PACK, cells // folds), BF16),
            pltpu.VMEM((SWEEPS - 1,) + grid, F32),
            pltpu.VMEM((6,) + grid, F32),
            pltpu.VMEM(grid, F32),
            pltpu.VMEM(grid, F32),
            pltpu.VMEM(grid, F32),
            pltpu.VMEM((SWEEPS + 1, 2, 2 * tiers, cols), F32),
            pltpu.VMEM((SWEEPS + 1, 4, 2 * tiers, cols), F32),
            pltpu.VMEM((SWEEPS + 1, 2, rows, cols), F32),
            dma((10,)),
            dma((tiles,)),
            dma((tiles,)),
            dma((tiles,)),
            dma((tiles,)),
            dma((SWEEPS + 1, 6)),
            dma((SWEEPS + 1, 6)),
        ],
        compiler_params=pltpu.CompilerParams(
            collective_id=0, has_side_effects=True, vmem_limit_bytes=VMEM_BYTES
        ),
    )(
        *(
            pltpu.with_memory_space_constraint(given, pltpu.HBM)
            for given in (temp, cond, mass, dyn, leak, panel.reshape(1, slots), place, block, tier, sens)
        )
    )
    return pl.pallas_call(
        hand_over,
        out_shape=(jax.ShapeDtypeStruct(grid, F32),) * 2,
        in_specs=[vmem_spec] * 2,
        out_specs=(any_spec, any_spec),
        scratch_shapes=[dma((2,))],
        compiler_params=pltpu.CompilerParams(vmem_limit_bytes=VMEM_BYTES),
    )(new, power.reshape(grid))


def solution(mesh):
    sizes = (mesh.shape["row"], mesh.shape["col"], mesh.shape["layer"])
    owner = ("row", "col", "layer")
    return jax.shard_map(
        functools.partial(shards, sizes),
        mesh=mesh,
        in_specs=(P("layer", "row", "col"),) * 3
        + (P(owner, None, None),) * 3
        + (P(owner, None),) * 4,
        out_specs=(P("layer", "row", "col"), P("layer", "row", "col")),
        check_vma=False,
    )
```

```python
import functools
import jax
import jax.numpy as jnp
from jax import lax
from jax.experimental import pallas as pl
from jax.experimental.pallas import tpu as pltpu
from jax.sharding import PartitionSpec as P

SUB = 64
SWEEPS = 3
CAP = 4
EIG_LOW = 0.1
EIG_HIGH = 2.0
LANES = 128
FOLDS = 16
VMEM_BYTES = 40 << 20

MESH = pl.DeviceIdType.MESH
F32 = jnp.float32
BF16 = jnp.bfloat16


def iota(shape, dim):
    return lax.broadcasted_iota(jnp.int32, shape, dim)


def div(x, n):
    if n & (n - 1):
        return x // n
    return lax.shift_right_logical(x, jnp.int32(n.bit_length() - 1))


def mod(x, n):
    if n & (n - 1):
        return lax.rem(x, n)
    return x & (n - 1)


def three_parts(x, axis):
    head = x.astype(BF16)
    rest = x - head.astype(F32)
    body = rest.astype(BF16)
    return jnp.concatenate([head, body, (rest - body.astype(F32)).astype(BF16)], axis=axis)


def two_parts(x, axis):
    head = x.astype(BF16)
    return jnp.concatenate([head, (x - head.astype(F32)).astype(BF16)], axis=axis)


def kernel(
    sizes,
    temp_hbm,
    cond_hbm,
    mass_hbm,
    dyn_hbm,
    leak_hbm,
    panel_hbm,
    place_hbm,
    block_hbm,
    tier_hbm,
    sens_hbm,
    out_ref,
    power_ref,
    panel_ref,
    place_ref,
    block_ref,
    tier_ref,
    sens_ref,
    temp,
    cond,
    mass,
    dyn,
    leak,
    dyn_pick,
    leak_pick,
    note_send,
    note_recv,
    place_send,
    place_recv,
    fac,
    load_send,
    load_recv,
    dirs,
    faces,
    diag,
    inv,
    resid,
    edge_send,
    edge_recv,
    plane_recv,
    nothing,
    waste,
    in_sem,
    note_ssem,
    note_rsem,
    place_ssem,
    place_rsem,
    load_ssem,
    load_rsem,
    halo_ssem,
    halo_rsem,
):
    n_row, n_col, n_layer = sizes
    tiles = n_row * n_col
    tiers, rows, cols = temp.shape
    slots, cells = dyn.shape
    wide = cells // FOLDS
    halves = wide // LANES
    named = 8 * tiles
    in_plane = (rows // SUB) * (cols // SUB)
    patches = tiers * in_plane
    bands = tiers * (rows // SUB)
    my_row = lax.axis_index("row")
    my_col = lax.axis_index("col")
    my_layer = lax.axis_index("layer")
    me = my_row * n_col + my_col

    loads = [
        pltpu.make_async_copy(src, dst, in_sem.at[i])
        for i, (src, dst) in enumerate(
            (
                (temp_hbm, temp),
                (panel_hbm, panel_ref),
                (place_hbm, place_ref),
                (block_hbm, block_ref),
                (tier_hbm, tier_ref),
                (sens_hbm, sens_ref),
                (dyn_hbm.at[0], dyn),
                (leak_hbm.at[0], leak),
                (cond_hbm, cond),
                (mass_hbm, mass),
            )
        )
    ]
    for load in loads:
        load.start()

    def far_first(step):
        if n_row & (n_row - 1) or n_col & (n_col - 1) or n_col == 1:
            return lax.rem(me + step, tiles)
        near = n_col // 2
        turn = mod(step, tiles // 2)
        over_row = n_row - 1 - div(turn, near)
        over_col = n_col - 1 - mod(turn, near) - near * div(step, tiles // 2)
        return lax.bitwise_xor(my_row, over_row) * n_col + lax.bitwise_xor(my_col, over_col)

    def each_peer(act):
        @pl.loop(0, tiles)
        def _(step):
            other = far_first(step)
            pl.when(other != me)(lambda: act(other))

    def device(other):
        return {"row": div(other, n_col), "col": mod(other, n_col)}

    sides = (
        (my_layer > 0, {"layer": my_layer - 1}, 0),
        (my_layer < n_layer - 1, {"layer": my_layer + 1}, 1),
        (my_row > 0, {"row": my_row - 1}, 2),
        (my_row < n_row - 1, {"row": my_row + 1}, 3),
        (my_col > 0, {"col": my_col - 1}, 4),
        (my_col < n_col - 1, {"col": my_col + 1}, 5),
    )

    nothing[...] = jnp.zeros_like(nothing)
    barrier = pltpu.get_barrier_semaphore()

    each_peer(
        lambda other: pl.semaphore_signal(barrier, inc=1, device_id=device(other), device_id_type=MESH)
    )

    for exists, where, side in sides[:2]:

        @pl.when(exists)
        def _(where=where):
            pl.semaphore_signal(barrier, inc=1, device_id=where, device_id_type=MESH)

    def remote(src, dst, ssem, rsem, other):
        return pltpu.make_async_remote_copy(
            src_ref=src,
            dst_ref=dst,
            send_sem=ssem,
            recv_sem=rsem,
            device_id=device(other),
            device_id_type=MESH,
        )

    def eight(tile):
        return pl.ds(pl.multiple_of(tile * 8, 8), 8)

    def note_copy(other):
        return remote(note_send, note_recv.at[me], note_ssem, note_rsem, other)

    def place_copy(other):
        return remote(place_send.at[eight(other), :], place_recv.at[eight(me), :], place_ssem, place_rsem, other)

    def load_copy(other):
        return remote(load_send.at[other], load_recv.at[me], load_ssem, load_rsem, other)

    def bytes_of(ref, sem):
        return pltpu.make_async_copy(ref, ref, sem)

    def keep(src, dst, sem):
        pltpu.make_async_copy(src, dst, sem).start()

    loads[0].wait()
    band_sums = jnp.concatenate(
        [
            jnp.sum(temp[t, b * SUB : (b + 1) * SUB, :], axis=0, keepdims=True)
            for t in range(tiers)
            for b in range(rows // SUB)
        ],
        axis=0,
    )
    lane_b = iota((bands, LANES), 1)
    sub_b = iota((bands, LANES), 0)
    means = jnp.zeros((1, LANES), F32)
    per_band = cols // SUB
    for part in range(per_band):
        total = jnp.sum(jnp.where(div(lane_b, SUB) == part, band_sums, 0.0), axis=1, keepdims=True)
        means = means + jnp.sum(
            jnp.where(lane_b == sub_b * per_band + part, total, 0.0), axis=0, keepdims=True
        )
    means = means * (1.0 / (SUB * SUB))
    note_send[...] = means
    beyond = (my_layer > 0).astype(jnp.int32) + (my_layer < n_layer - 1).astype(jnp.int32)
    pl.semaphore_wait(barrier, tiles - 1 + beyond)

    each_peer(lambda other: note_copy(other).start())
    keep(note_send, note_recv.at[me], note_rsem)
    lane_s = iota((slots, slots), 1)
    sub_s = iota((slots, slots), 0)
    eye = lane_s == sub_s

    def to_col(row):
        return jnp.sum(jnp.where(eye, jnp.broadcast_to(row, (slots, slots)), 0.0), axis=1, keepdims=True)

    def to_row(col):
        return jnp.sum(jnp.where(eye, jnp.broadcast_to(col, (slots, slots)), 0.0), axis=0, keepdims=True)

    for load in loads[1:6]:
        load.wait()
    tgt_row = panel_ref[...].astype(F32)
    tgt_col = to_col(tgt_row)
    blk_row = block_ref[...].astype(F32)
    blk_col = to_col(blk_row)
    sub_col = to_col(place_ref[...].astype(F32))
    same_tile = tgt_col == tgt_row
    rank_col = jnp.sum(jnp.where(same_tile & (lane_s < sub_s), 1.0, 0.0), axis=1, keepdims=True)
    rank_row = jnp.sum(jnp.where(same_tile & (sub_s < lane_s), 1.0, 0.0), axis=0, keepdims=True)
    blocks = tier_ref.shape[1]
    of_block = blk_col == iota((slots, blocks), 1).astype(F32)
    tier_col = jnp.sum(jnp.where(of_block, tier_ref[...].astype(F32), 0.0), axis=1, keepdims=True)
    sens_col = jnp.sum(jnp.where(of_block, sens_ref[...], 0.0), axis=1, keepdims=True)
    pos_col = tier_col * in_plane + sub_col
    goes = (tgt_row * CAP + rank_row) == iota((tiles * CAP, slots), 0).astype(F32)
    pick = jnp.where(goes, 1.0, 0.0).astype(BF16)
    sub8 = iota((2 * tiers, 2 * cols), 0)
    lane8 = mod(iota((2 * tiers, 2 * cols), 1), cols)
    picks = [
        jnp.where(
            ((sub8 == t) & (lane8 == 0)) | ((sub8 == tiers + t) & (lane8 == cols - 1)), 1.0, 0.0
        ).astype(BF16)
        for t in range(tiers)
    ]

    def halo_ends(turn, field, side, lands):
        if side < 2:
            return field.at[0 if side == 0 else tiers - 1], plane_recv.at[turn, lands], 0
        return edge_send.at[turn, (side - 2) // 2], edge_recv.at[turn, lands - 2], 1

    def halo_start(turn, field, exists, where, side):
        @pl.when(exists)
        def _():
            src, dst, kind = halo_ends(turn, field, side, side ^ 1)
            pltpu.make_async_remote_copy(
                src_ref=src,
                dst_ref=dst,
                send_sem=halo_ssem.at[kind],
                recv_sem=halo_rsem.at[turn, kind],
                device_id=where,
                device_id_type=MESH,
            ).start()

        @pl.when(jnp.logical_not(exists))
        def _():
            _, dst, kind = halo_ends(turn, field, side, side)
            none = nothing.at[...] if kind == 0 else nothing.at[: 2 * tiers, :]
            spare = waste.at[turn, side]
            spare = spare if kind == 0 else spare.at[: 2 * tiers, :]
            keep(none, dst, halo_rsem.at[turn, kind])
            keep(none, spare, halo_ssem.at[kind])

    def pack_rows(turn, field):
        for end in range(2):
            at = end * (rows - 1)
            for t in range(tiers):
                edge_send[turn, 0, end * tiers + t : end * tiers + t + 1, :] = field[t, at : at + 1, :]

    def pack_columns(turn, field):
        columns = jnp.zeros((2 * tiers, rows), F32)
        for t in range(tiers):
            columns = columns + lax.dot_general(
                picks[t], two_parts(field[t], 1), (((1,), (1,)), ((), ())), preferred_element_type=F32
            )
        edge_send[turn, 1] = columns

    def start_halo(turn, field):
        def start(which):
            for exists, where, side in which:
                halo_start(turn, field, exists, where, side)

        pack_rows(turn, field)
        start(sides[2:4])
        start(sides[:2])
        pack_columns(turn, field)
        start(sides[4:])

    def wait_halo(turn):
        bytes_of(plane_recv.at[turn], halo_rsem.at[turn, 0]).wait()
        bytes_of(edge_recv.at[turn], halo_rsem.at[turn, 1]).wait()

    row_i = iota((rows, cols), 0)
    col_i = iota((rows, cols), 1)
    sub16 = mod(iota((8 * tiers, tiers * cols), 0), 4 * tiers)
    lane16 = iota((8 * tiers, tiers * cols), 1)
    put = jnp.where(
        ((mod(lane16, cols) == 0) & (sub16 == tiers + div(lane16, cols)))
        | ((mod(lane16, cols) == cols - 1) & (sub16 == 2 * tiers + div(lane16, cols))),
        1.0,
        0.0,
    ).astype(BF16)

    def inside(field, t):
        v = field[t]
        none = jnp.zeros_like(v)
        low = none if t == 0 else field[t - 1]
        high = none if t == tiers - 1 else field[t + 1]
        north = jnp.where(row_i == 0, 0.0, pltpu.roll(v, 1, 0))
        south = jnp.where(row_i == rows - 1, 0.0, pltpu.roll(v, rows - 1, 0))
        west = jnp.where(col_i == 0, 0.0, pltpu.roll(v, 1, 1))
        east = jnp.where(col_i == cols - 1, 0.0, pltpu.roll(v, cols - 1, 1))
        return v, (low, high, north, south, west, east)

    def rims(turn):
        ends = jnp.concatenate([edge_recv[turn, 2], edge_recv[turn, 3]], axis=0)
        return lax.dot_general(
            two_parts(ends, 0), put, (((0,), (0,)), ((), ())), preferred_element_type=F32
        )

    def apply_inside(field, t):
        v, around = inside(field, t)
        value = diag[t] * v
        for k in range(6):
            if not (k == 0 and t == 0 or k == 1 and t == tiers - 1):
                value = value - faces[k, t] * around[k]
        return value

    def add_beyond(turn):
        rim = rims(turn)
        resid[0] = resid[0] + faces[0, 0] * plane_recv[turn, 0]
        resid[tiers - 1] = resid[tiers - 1] + faces[1, tiers - 1] * plane_recv[turn, 1]
        for t in range(tiers):
            first, last = slice(0, 1), slice(rows - 1, rows)
            resid[t, first, :] = (
                resid[t, first, :] + faces[2, t, first, :] * edge_recv[turn, 0, tiers + t : tiers + t + 1, :]
            )
            resid[t, last, :] = (
                resid[t, last, :] + faces[3, t, last, :] * edge_recv[turn, 1, t : t + 1, :]
            )
            face = jnp.where(col_i == 0, faces[4, t], faces[5, t])
            resid[t] = resid[t] + face * rim[:, t * cols : (t + 1) * cols]

    name_r = iota((named, slots), 0).astype(F32)
    named_row = tgt_row * 8.0 + rank_row
    named_col = tgt_col * 8.0 + rank_col
    by_name = name_r == named_row

    def rename(row):
        return jnp.sum(jnp.where(by_name, row, 0.0), axis=1, keepdims=True)

    pos_r = rename(to_row(pos_col) + 1.0)
    blk_r = rename(blk_row + 1.0)
    sens_r = rename(to_row(sens_col))
    blk_n = jnp.sum(
        jnp.where(named_col == iota((slots, named), 1).astype(F32), blk_col + 1.0, 0.0), axis=0, keepdims=True
    )
    same_block = jnp.where((blk_r == blk_n) & (blk_r > 0.0), 1.0, 0.0)
    block_size = jnp.maximum(jnp.sum(same_block, axis=1, keepdims=True), 1.0)
    same_three = jnp.concatenate([same_block.astype(BF16)] * 3, axis=1)
    at_place = (iota((named, LANES), 1) + 1).astype(F32) == pos_r
    place_send[...] = jnp.broadcast_to(pos_r, place_send.shape)
    each_peer(lambda other: place_copy(other).start())
    keep(place_send.at[eight(me), :], place_recv.at[eight(me), :], place_rsem)

    loads[8].wait()
    start_halo(0, temp)
    start_halo(1, cond)

    loads[6].wait()
    loads[7].wait()
    for src, dst in ((dyn, dyn_pick), (leak, leak_pick)):
        for fold in range(FOLDS):
            taken = jnp.dot(pick, src[:, fold * wide : (fold + 1) * wide], preferred_element_type=F32)
            for half in range(halves):
                dst[half, pl.ds(fold, tiles * CAP, stride=FOLDS), :] = taken[
                    :, half * LANES : (half + 1) * LANES
                ]

    bytes_of(note_recv, note_rsem).wait()
    tile_means = jnp.concatenate([jnp.broadcast_to(note_recv[tile], (8, LANES)) for tile in range(tiles)], axis=0)
    at_slots = three_parts(jnp.where(at_place, tile_means, 0.0), 0)
    block_sum = jnp.sum(
        jnp.dot(same_three, at_slots, preferred_element_type=F32), axis=1, keepdims=True
    )
    fac[...] = jnp.broadcast_to(jnp.exp(sens_r * (block_sum / block_size)), (named, LANES))

    @pl.loop(0, tiles)
    def _(step):
        other = far_first(step)
        for rank in range(CAP):
            by = fac[pl.ds(other * 8 + rank, 8, stride=0), :]
            by = jnp.concatenate([by] * (FOLDS // 8), axis=0)
            at = pl.ds(pl.multiple_of((other * CAP + rank) * FOLDS, FOLDS), FOLDS)
            for half in range(halves):
                load_send[other, rank * FOLDS : (rank + 1) * FOLDS, half * LANES : (half + 1) * LANES] = (
                    dyn_pick[half, at, :] + by * leak_pick[half, at, :]
                ).astype(BF16)

        @pl.when(other != me)
        def _():
            load_copy(other).start()

    keep(load_send.at[me], load_recv.at[me], load_rsem)

    loads[9].wait()
    wait_halo(0)
    wait_halo(1)
    rim = rims(1)
    for t in range(tiers):
        c, (low, high, north, south, west, east) = inside(cond, t)
        here = rim[:, t * cols : (t + 1) * cols]
        low = plane_recv[1, 0] if t == 0 else low
        high = plane_recv[1, 1] if t == tiers - 1 else high
        north = jnp.where(row_i == 0, edge_recv[1, 0, tiers + t : tiers + t + 1, :], north)
        south = jnp.where(row_i == rows - 1, edge_recv[1, 1, t : t + 1, :], south)
        west = jnp.where(col_i == 0, here, west)
        east = jnp.where(col_i == cols - 1, here, east)
        total = mass[t]
        for k, beside in enumerate((low, high, north, south, west, east)):
            face = 0.5 * (c + beside)
            faces[k, t] = face
            total = total + face
        diag[t] = total
        inv[t] = 1.0 / total
    for t in range(tiers):
        resid[t] = mass[t] * temp[t] - apply_inside(temp, t)
    add_beyond(0)

    middle = (EIG_LOW + EIG_HIGH) / 2.0
    spread = (EIG_HIGH - EIG_LOW) / 2.0
    ratio = middle / spread
    weight = 1.0 / ratio

    sources = tiles * CAP * FOLDS
    sel_i = iota((FOLDS * patches, sources), 0)
    sel_j = iota((FOLDS * patches, sources), 1)
    sel_in = mod(sel_i, patches)
    sel_patch = mod(sel_in, bands) * per_band + div(sel_in, bands)
    fold_hit = div(sel_i, patches) == mod(sel_j, FOLDS)
    bytes_of(place_recv, place_rsem).wait()
    place_i = iota((named, sources), 0)
    place_j = div(iota((named, sources), 1), FOLDS)
    place_j = div(place_j, CAP) * 8 + mod(place_j, CAP)
    places = jnp.concatenate([place_recv[...]] * (sources // LANES), axis=1)
    code = jnp.sum(jnp.where(place_i == place_j, places, 0.0), axis=0, keepdims=True)
    picker = jnp.where(fold_hit & (code == (sel_patch + 1).astype(F32)), 1.0, 0.0).astype(BF16)
    bytes_of(load_recv, load_rsem).wait()
    footprint = jnp.dot(picker, load_recv[...].reshape(sources, wide), preferred_element_type=F32)
    left = iota((bands, LANES), 1) < SUB
    for fold in range(FOLDS):
        for k in range(wide // LANES):
            lanes = slice(k * LANES, (k + 1) * LANES)
            a = footprint[fold * patches : fold * patches + bands, lanes]
            b = footprint[fold * patches + bands : fold * patches + 2 * bands, lanes]
            at = 2 * (fold * (wide // LANES) + k)
            power_ref[pl.ds(at, bands, stride=SUB), :] = jnp.where(left, a, pltpu.roll(b, SUB, 1))
            power_ref[pl.ds(at + 1, bands, stride=SUB), :] = jnp.where(left, pltpu.roll(a, SUB, 1), b)

    for t in range(tiers):
        r = resid[t] + power_ref[t * rows : (t + 1) * rows, :]
        resid[t] = r
        dirs[0, t] = r * inv[t] * (1.0 / middle)
    for sweep in range(1, SWEEPS):
        field = dirs.at[sweep - 1]
        turn = 1 + sweep
        start_halo(turn, field)
        weight_new = 1.0 / (2.0 * ratio - weight)
        for t in range(tiers):
            base = temp[t] if sweep == 1 else out_ref[t]
            out_ref[t] = base + field[t]
            resid[t] = resid[t] - apply_inside(field, t)
        wait_halo(turn)
        add_beyond(turn)
        for t in range(tiers):
            d = weight_new * weight * field[t] + (2.0 * weight_new / spread) * (resid[t] * inv[t])
            if sweep < SWEEPS - 1:
                dirs[sweep, t] = d
            else:
                out_ref[t] = out_ref[t] + d
        weight = weight_new
    bytes_of(plane_recv, halo_ssem.at[0]).wait()
    bytes_of(edge_recv, halo_ssem.at[1]).wait()
    bytes_of(note_recv.at[1:], note_ssem).wait()
    bytes_of(place_recv.at[8:, :], place_ssem).wait()
    bytes_of(load_recv.at[1:], load_ssem).wait()


def hand_over(new, power, new_out, power_out, sem):
    moves = (pltpu.make_async_copy(power, power_out, sem.at[0]), pltpu.make_async_copy(new, new_out, sem.at[1]))
    for move in moves:
        move.start()
    for move in moves:
        move.wait()


def shards(sizes, temp, cond, mass, dyn, leak, panel, place, block, tier, sens):
    tiers, rows, cols = temp.shape
    slots, cells = dyn.shape[1:]
    tiles = sizes[0] * sizes[1]
    any_spec = pl.BlockSpec(memory_space=pl.ANY)
    vmem_spec = pl.BlockSpec(memory_space=pltpu.VMEM)
    grid = (tiers, rows, cols)
    dma = pltpu.SemaphoreType.DMA
    new, power = pl.pallas_call(
        functools.partial(kernel, sizes),
        out_shape=(
            pltpu.VMEM(grid, F32),
            pltpu.VMEM((tiers * rows, cols), F32),
        ),
        in_specs=[any_spec] * 10,
        out_specs=(vmem_spec, vmem_spec),
        scratch_shapes=[
            pltpu.VMEM((1, slots), jnp.int32),
            pltpu.VMEM((1, slots), jnp.int32),
            pltpu.VMEM((1, slots), jnp.int32),
            pltpu.VMEM(tier.shape, jnp.int32),
            pltpu.VMEM(sens.shape, F32),
            pltpu.VMEM(grid, F32),
            pltpu.VMEM(grid, F32),
            pltpu.VMEM(grid, F32),
            pltpu.VMEM((slots, cells), BF16),
            pltpu.VMEM((slots, cells), BF16),
            pltpu.VMEM((cells // FOLDS // LANES, tiles * CAP * FOLDS, LANES), F32),
            pltpu.VMEM((cells // FOLDS // LANES, tiles * CAP * FOLDS, LANES), F32),
            pltpu.VMEM((1, LANES), F32),
            pltpu.VMEM((tiles, 1, LANES), F32),
            pltpu.VMEM((8 * tiles, LANES), F32),
            pltpu.VMEM((8 * tiles, LANES), F32),
            pltpu.VMEM((8 * tiles, LANES), F32),
            pltpu.VMEM((tiles, CAP * FOLDS, cells // FOLDS), BF16),
            pltpu.VMEM((tiles, CAP * FOLDS, cells // FOLDS), BF16),
            pltpu.VMEM((SWEEPS - 1,) + grid, F32),
            pltpu.VMEM((6,) + grid, F32),
            pltpu.VMEM(grid, F32),
            pltpu.VMEM(grid, F32),
            pltpu.VMEM(grid, F32),
            pltpu.VMEM((SWEEPS + 1, 2, 2 * tiers, cols), F32),
            pltpu.VMEM((SWEEPS + 1, 4, 2 * tiers, cols), F32),
            pltpu.VMEM((SWEEPS + 1, 2, rows, cols), F32),
            pltpu.VMEM((rows, cols), F32),
            pltpu.VMEM((SWEEPS + 1, 6, rows, cols), F32),
            dma((10,)),
            dma(()),
            dma(()),
            dma(()),
            dma(()),
            dma(()),
            dma(()),
            dma((2,)),
            dma((SWEEPS + 1, 2)),
        ],
        compiler_params=pltpu.CompilerParams(
            collective_id=0, has_side_effects=True, vmem_limit_bytes=VMEM_BYTES
        ),
    )(
        *(
            pltpu.with_memory_space_constraint(given, pltpu.HBM)
            for given in (temp, cond, mass, dyn, leak, panel.reshape(1, slots), place, block, tier, sens)
        )
    )
    return pl.pallas_call(
        hand_over,
        out_shape=(jax.ShapeDtypeStruct(grid, F32),) * 2,
        in_specs=[vmem_spec] * 2,
        out_specs=(any_spec, any_spec),
        scratch_shapes=[dma((2,))],
        compiler_params=pltpu.CompilerParams(vmem_limit_bytes=VMEM_BYTES),
    )(new, power.reshape(grid))


def solution(mesh):
    sizes = (mesh.shape["row"], mesh.shape["col"], mesh.shape["layer"])
    owner = ("row", "col", "layer")
    return jax.shard_map(
        functools.partial(shards, sizes),
        mesh=mesh,
        in_specs=(P("layer", "row", "col"),) * 3
        + (P(owner, None, None),) * 3
        + (P(owner, None),) * 4,
        out_specs=(P("layer", "row", "col"), P("layer", "row", "col")),
        check_vma=False,
    )
```

```python
import functools
import jax
import jax.numpy as jnp
from jax import lax
from jax.experimental import pallas as pl
from jax.experimental.pallas import tpu as pltpu
from jax.sharding import PartitionSpec as P

SUB = 64
SWEEPS = 3
CAP = 4
EIG_LOW = 0.1
EIG_HIGH = 2.0
LANES = 128
FOLDS = 16
VMEM_BYTES = 40 << 20

MESH = pl.DeviceIdType.MESH
F32 = jnp.float32
BF16 = jnp.bfloat16


def iota(shape, dim):
    return lax.broadcasted_iota(jnp.int32, shape, dim)


def div(x, n):
    if n & (n - 1):
        return x // n
    return lax.shift_right_logical(x, jnp.int32(n.bit_length() - 1))


def mod(x, n):
    if n & (n - 1):
        return lax.rem(x, n)
    return x & (n - 1)


def three_parts(x, axis):
    head = x.astype(BF16)
    rest = x - head.astype(F32)
    body = rest.astype(BF16)
    return jnp.concatenate([head, body, (rest - body.astype(F32)).astype(BF16)], axis=axis)


def two_parts(x, axis):
    head = x.astype(BF16)
    return jnp.concatenate([head, (x - head.astype(F32)).astype(BF16)], axis=axis)


def kernel(
    sizes,
    temp_hbm,
    cond_hbm,
    mass_hbm,
    dyn_hbm,
    leak_hbm,
    panel_hbm,
    place_hbm,
    block_hbm,
    tier_hbm,
    sens_hbm,
    out_ref,
    power_ref,
    panel_ref,
    place_ref,
    block_ref,
    tier_ref,
    sens_ref,
    temp,
    cond,
    mass,
    dyn,
    leak,
    dyn_pick,
    leak_pick,
    note_send,
    note_recv,
    place_send,
    place_recv,
    fac,
    load_send,
    load_recv,
    dirs,
    faces,
    diag,
    inv,
    resid,
    edge_send,
    edge_recv,
    edge_spare,
    plane_recv,
    plane_spare,
    rim_send,
    rim_recv,
    rim_spare,
    gain_send,
    gain_recv,
    gain_spare,
    nothing,
    in_sem,
    note_ssem,
    note_rsem,
    place_ssem,
    place_rsem,
    load_ssem,
    load_rsem,
    halo_ssem,
    halo_rsem,
    rim_ssem,
    rim_rsem,
    gain_ssem,
    gain_rsem,
):
    n_row, n_col, n_layer = sizes
    tiles = n_row * n_col
    tiers, rows, cols = temp.shape
    slots, cells = dyn.shape
    wide = cells // FOLDS
    halves = wide // LANES
    named = 8 * tiles
    in_plane = (rows // SUB) * (cols // SUB)
    patches = tiers * in_plane
    bands = tiers * (rows // SUB)
    my_row = lax.axis_index("row")
    my_col = lax.axis_index("col")
    my_layer = lax.axis_index("layer")
    me = my_row * n_col + my_col

    loads = [
        pltpu.make_async_copy(src, dst, in_sem.at[i])
        for i, (src, dst) in enumerate(
            (
                (temp_hbm, temp),
                (panel_hbm, panel_ref),
                (place_hbm, place_ref),
                (block_hbm, block_ref),
                (tier_hbm, tier_ref),
                (sens_hbm, sens_ref),
                (dyn_hbm.at[0], dyn),
                (leak_hbm.at[0], leak),
                (cond_hbm, cond),
                (mass_hbm, mass),
            )
        )
    ]
    for load in loads:
        load.start()

    def far_first(step):
        if n_row & (n_row - 1) or n_col & (n_col - 1) or n_col == 1:
            return lax.rem(me + step, tiles)
        near = n_col // 2
        turn = mod(step, tiles // 2)
        over_row = n_row - 1 - div(turn, near)
        over_col = n_col - 1 - mod(turn, near) - near * div(step, tiles // 2)
        return lax.bitwise_xor(my_row, over_row) * n_col + lax.bitwise_xor(my_col, over_col)

    def each_peer(act):
        @pl.loop(0, tiles)
        def _(step):
            other = far_first(step)
            pl.when(other != me)(lambda: act(other))

    def device(other):
        return {"row": div(other, n_col), "col": mod(other, n_col)}

    sides = (
        (my_layer > 0, {"layer": my_layer - 1}, 0),
        (my_layer < n_layer - 1, {"layer": my_layer + 1}, 1),
        (my_row > 0, {"row": my_row - 1}, 2),
        (my_row < n_row - 1, {"row": my_row + 1}, 3),
        (my_col > 0, {"col": my_col - 1}, 4),
        (my_col < n_col - 1, {"col": my_col + 1}, 5),
    )

    def neighbour(d_row, d_col, d_layer):
        exists, where = [], {}
        for axis, mine, count, d in (
            ("row", my_row, n_row, d_row),
            ("col", my_col, n_col, d_col),
            ("layer", my_layer, n_layer, d_layer),
        ):
            if d:
                exists.append(mine > 0 if d < 0 else mine < count - 1)
                where[axis] = mine + d
        return functools.reduce(jnp.logical_and, exists), where

    rims_of = (
        [((a, b, 0), 0, 1, 8 + i) for i, (a, b) in enumerate(((-1, -1), (-1, 1), (1, -1), (1, 1)))]
        + [((a, 0, c), 0, 1, 12 + i) for i, (a, c) in enumerate(((-1, -1), (-1, 1), (1, -1), (1, 1)))]
        + [((0, b, c), 2, 1, 16 + i) for i, (b, c) in enumerate(((-1, -1), (-1, 1), (1, -1), (1, 1)))]
        + [((-1, 0, 0), 0, 2, 0), ((1, 0, 0), 0, 2, 2), ((0, -1, 0), 2, 2, 4), ((0, 1, 0), 2, 2, 6)]
    )
    slot_of = {step: slot for step, _, _, slot in rims_of}

    nothing[...] = jnp.zeros_like(nothing)
    barrier = pltpu.get_barrier_semaphore()

    each_peer(
        lambda other: pl.semaphore_signal(barrier, inc=1, device_id=device(other), device_id_type=MESH)
    )

    across = [neighbour(*step) for step, _, _, _ in rims_of if step[2]] + [neighbour(0, 0, -1), neighbour(0, 0, 1)]
    for exists, where in across:

        @pl.when(exists)
        def _(where=where):
            pl.semaphore_signal(barrier, inc=1, device_id=where, device_id_type=MESH)

    def remote(src, dst, ssem, rsem, other):
        return pltpu.make_async_remote_copy(
            src_ref=src,
            dst_ref=dst,
            send_sem=ssem,
            recv_sem=rsem,
            device_id=device(other),
            device_id_type=MESH,
        )

    def eight(tile):
        return pl.ds(pl.multiple_of(tile * 8, 8), 8)

    def note_copy(other):
        return remote(note_send, note_recv.at[me], note_ssem, note_rsem, other)

    def place_copy(other):
        return remote(place_send.at[eight(other), :], place_recv.at[eight(me), :], place_ssem, place_rsem, other)

    def load_copy(other):
        return remote(load_send.at[other], load_recv.at[me], load_ssem, load_rsem, other)

    def send(src, dst, ssem, rsem, where):
        pltpu.make_async_remote_copy(
            src_ref=src, dst_ref=dst, send_sem=ssem, recv_sem=rsem, device_id=where, device_id_type=MESH
        ).start()

    def bytes_of(ref, sem):
        return pltpu.make_async_copy(ref, ref, sem)

    def keep(src, dst, sem):
        pltpu.make_async_copy(src, dst, sem).start()

    loads[0].wait()
    band_sums = jnp.concatenate(
        [
            jnp.sum(temp[t, b * SUB : (b + 1) * SUB, :], axis=0, keepdims=True)
            for t in range(tiers)
            for b in range(rows // SUB)
        ],
        axis=0,
    )
    lane_b = iota((bands, LANES), 1)
    sub_b = iota((bands, LANES), 0)
    means = jnp.zeros((1, LANES), F32)
    per_band = cols // SUB
    for part in range(per_band):
        total = jnp.sum(jnp.where(div(lane_b, SUB) == part, band_sums, 0.0), axis=1, keepdims=True)
        means = means + jnp.sum(
            jnp.where(lane_b == sub_b * per_band + part, total, 0.0), axis=0, keepdims=True
        )
    means = means * (1.0 / (SUB * SUB))
    note_send[...] = means
    beyond = sum(exists.astype(jnp.int32) for exists, _ in across)
    pl.semaphore_wait(barrier, tiles - 1 + beyond)

    each_peer(lambda other: note_copy(other).start())
    keep(note_send, note_recv.at[me], note_rsem)

    def missing(exists, blocks):
        @pl.when(jnp.logical_not(exists))
        def _():
            for recv, spare, at, ssem, rsem, none in blocks:
                keep(none, recv.at[at], rsem)
                keep(none, spare.at[at], ssem)

    none8 = nothing.at[:8, :]
    for exists, _, side in sides[:2]:
        missing(
            exists,
            [
                (plane_recv.at[turn], plane_spare.at[turn], side, halo_ssem.at[0], halo_rsem.at[turn, 0], nothing)
                for turn in range(4)
            ],
        )
    for exists, _, side in sides[2:]:
        missing(
            exists,
            [
                (edge_recv.at[turn], edge_spare.at[turn], side - 2, halo_ssem.at[1], halo_rsem.at[turn, 1], none8)
                for turn in range(2)
            ]
            + [(gain_recv, gain_spare, 3 * (side - 2) + k, gain_ssem, gain_rsem, none8) for k in range(3)],
        )
    for step, _, count, slot in rims_of:
        missing(
            neighbour(*step)[0],
            [(rim_recv, rim_spare, slot + k, rim_ssem, rim_rsem, none8) for k in range(count)],
        )
    lane_s = iota((slots, slots), 1)
    sub_s = iota((slots, slots), 0)
    eye = lane_s == sub_s

    def to_col(row):
        return jnp.sum(jnp.where(eye, jnp.broadcast_to(row, (slots, slots)), 0.0), axis=1, keepdims=True)

    def to_row(col):
        return jnp.sum(jnp.where(eye, jnp.broadcast_to(col, (slots, slots)), 0.0), axis=0, keepdims=True)

    for load in loads[1:6]:
        load.wait()
    tgt_row = panel_ref[...].astype(F32)
    tgt_col = to_col(tgt_row)
    blk_row = block_ref[...].astype(F32)
    blk_col = to_col(blk_row)
    sub_col = to_col(place_ref[...].astype(F32))
    same_tile = tgt_col == tgt_row
    rank_col = jnp.sum(jnp.where(same_tile & (lane_s < sub_s), 1.0, 0.0), axis=1, keepdims=True)
    rank_row = jnp.sum(jnp.where(same_tile & (sub_s < lane_s), 1.0, 0.0), axis=0, keepdims=True)
    blocks = tier_ref.shape[1]
    of_block = blk_col == iota((slots, blocks), 1).astype(F32)
    tier_col = jnp.sum(jnp.where(of_block, tier_ref[...].astype(F32), 0.0), axis=1, keepdims=True)
    sens_col = jnp.sum(jnp.where(of_block, sens_ref[...], 0.0), axis=1, keepdims=True)
    pos_col = tier_col * in_plane + sub_col
    goes = (tgt_row * CAP + rank_row) == iota((tiles * CAP, slots), 0).astype(F32)
    pick = jnp.where(goes, 1.0, 0.0).astype(BF16)
    sub8 = iota((2 * tiers, 2 * cols), 0)
    lane8 = mod(iota((2 * tiers, 2 * cols), 1), cols)
    picks = [
        jnp.where(
            ((sub8 == t) & (lane8 == 0)) | ((sub8 == tiers + t) & (lane8 == cols - 1)), 1.0, 0.0
        ).astype(BF16)
        for t in range(tiers)
    ]

    def halo_ends(turn, field, side, lands):
        if side < 2:
            return field.at[0 if side == 0 else tiers - 1], plane_recv.at[turn, lands], 0
        return edge_send.at[turn, (side - 2) // 2], edge_recv.at[turn, lands - 2], 1

    def halo_start(turn, field, exists, where, side):
        @pl.when(exists)
        def _():
            src, dst, kind = halo_ends(turn, field, side, side ^ 1)
            send(src, dst, halo_ssem.at[kind], halo_rsem.at[turn, kind], where)

    def pack_rows(turn, field):
        for end in range(2):
            at = end * (rows - 1)
            for t in range(tiers):
                edge_send[turn, 0, end * tiers + t : end * tiers + t + 1, :] = field[t, at : at + 1, :]

    def columns_of(field):
        columns = jnp.zeros((2 * tiers, rows), F32)
        for t in range(tiers):
            columns = columns + lax.dot_general(
                picks[t], two_parts(field(t), 1), (((1,), (1,)), ((), ())), preferred_element_type=F32
            )
        return columns

    def rows_of(first, last):
        return jnp.concatenate([first(t) for t in range(tiers)] + [last(t) for t in range(tiers)], axis=0)

    def start_halo(turn, field):
        def start(which):
            for exists, where, side in which:
                halo_start(turn, field, exists, where, side)

        pack_rows(turn, field)
        start(sides[2:4])
        start(sides[:2])
        edge_send[turn, 1] = columns_of(lambda t: field[t])
        start(sides[4:])

    def wait_plane(turn):
        bytes_of(plane_recv.at[turn], halo_rsem.at[turn, 0]).wait()

    def wait_halo(turn):
        wait_plane(turn)
        bytes_of(edge_recv.at[turn], halo_rsem.at[turn, 1]).wait()

    row_i = iota((rows, cols), 0)
    col_i = iota((rows, cols), 1)
    sub16 = mod(iota((8 * tiers, tiers * cols), 0), 4 * tiers)
    lane16 = iota((8 * tiers, tiers * cols), 1)
    put = jnp.where(
        ((mod(lane16, cols) == 0) & (sub16 == tiers + div(lane16, cols)))
        | ((mod(lane16, cols) == cols - 1) & (sub16 == 2 * tiers + div(lane16, cols))),
        1.0,
        0.0,
    ).astype(BF16)

    def inside(field, t):
        v = field[t]
        none = jnp.zeros_like(v)
        low = none if t == 0 else field[t - 1]
        high = none if t == tiers - 1 else field[t + 1]
        north = jnp.where(row_i == 0, 0.0, pltpu.roll(v, 1, 0))
        south = jnp.where(row_i == rows - 1, 0.0, pltpu.roll(v, rows - 1, 0))
        west = jnp.where(col_i == 0, 0.0, pltpu.roll(v, 1, 1))
        east = jnp.where(col_i == cols - 1, 0.0, pltpu.roll(v, cols - 1, 1))
        return v, (low, high, north, south, west, east)

    def rims(west, east):
        ends = jnp.concatenate([west, east], axis=0)
        return lax.dot_general(
            two_parts(ends, 0), put, (((0,), (0,)), ((), ())), preferred_element_type=F32
        )

    def apply_inside(field, t):
        v, around = inside(field, t)
        value = diag[t] * v
        for k in range(6):
            if not (k == 0 and t == 0 or k == 1 and t == tiers - 1):
                value = value - faces[k, t] * around[k]
        return value

    def add_beyond(turn):
        rim = rims(edge_recv[turn, 2], edge_recv[turn, 3])
        resid[0] = resid[0] + faces[0, 0] * plane_recv[turn, 0]
        resid[tiers - 1] = resid[tiers - 1] + faces[1, tiers - 1] * plane_recv[turn, 1]
        for t in range(tiers):
            first, last = slice(0, 1), slice(rows - 1, rows)
            resid[t, first, :] = (
                resid[t, first, :] + faces[2, t, first, :] * edge_recv[turn, 0, tiers + t : tiers + t + 1, :]
            )
            resid[t, last, :] = (
                resid[t, last, :] + faces[3, t, last, :] * edge_recv[turn, 1, t : t + 1, :]
            )
            face = jnp.where(col_i == 0, faces[4, t], faces[5, t])
            resid[t] = resid[t] + face * rim[:, t * cols : (t + 1) * cols]

    name_r = iota((named, slots), 0).astype(F32)
    named_row = tgt_row * 8.0 + rank_row
    named_col = tgt_col * 8.0 + rank_col
    by_name = name_r == named_row

    def rename(row):
        return jnp.sum(jnp.where(by_name, row, 0.0), axis=1, keepdims=True)

    pos_r = rename(to_row(pos_col) + 1.0)
    blk_r = rename(blk_row + 1.0)
    sens_r = rename(to_row(sens_col))
    blk_n = jnp.sum(
        jnp.where(named_col == iota((slots, named), 1).astype(F32), blk_col + 1.0, 0.0), axis=0, keepdims=True
    )
    same_block = jnp.where((blk_r == blk_n) & (blk_r > 0.0), 1.0, 0.0)
    block_size = jnp.maximum(jnp.sum(same_block, axis=1, keepdims=True), 1.0)
    same_three = jnp.concatenate([same_block.astype(BF16)] * 3, axis=1)
    at_place = (iota((named, LANES), 1) + 1).astype(F32) == pos_r
    place_send[...] = jnp.broadcast_to(pos_r, place_send.shape)
    each_peer(lambda other: place_copy(other).start())
    keep(place_send.at[eight(me), :], place_recv.at[eight(me), :], place_rsem)

    loads[8].wait()
    start_halo(0, temp)
    start_halo(1, cond)

    loads[6].wait()
    loads[7].wait()
    for src, dst in ((dyn, dyn_pick), (leak, leak_pick)):
        for fold in range(FOLDS):
            taken = jnp.dot(pick, src[:, fold * wide : (fold + 1) * wide], preferred_element_type=F32)
            for half in range(halves):
                dst[half, pl.ds(fold, tiles * CAP, stride=FOLDS), :] = taken[
                    :, half * LANES : (half + 1) * LANES
                ]

    bytes_of(note_recv, note_rsem).wait()
    tile_means = jnp.concatenate([jnp.broadcast_to(note_recv[tile], (8, LANES)) for tile in range(tiles)], axis=0)
    at_slots = three_parts(jnp.where(at_place, tile_means, 0.0), 0)
    block_sum = jnp.sum(
        jnp.dot(same_three, at_slots, preferred_element_type=F32), axis=1, keepdims=True
    )
    fac[...] = jnp.broadcast_to(jnp.exp(sens_r * (block_sum / block_size)), (named, LANES))

    @pl.loop(0, tiles)
    def _(step):
        other = far_first(step)
        for rank in range(CAP):
            by = fac[pl.ds(other * 8 + rank, 8, stride=0), :]
            by = jnp.concatenate([by] * (FOLDS // 8), axis=0)
            at = pl.ds(pl.multiple_of((other * CAP + rank) * FOLDS, FOLDS), FOLDS)
            for half in range(halves):
                load_send[other, rank * FOLDS : (rank + 1) * FOLDS, half * LANES : (half + 1) * LANES] = (
                    dyn_pick[half, at, :] + by * leak_pick[half, at, :]
                ).astype(BF16)

        @pl.when(other != me)
        def _():
            load_copy(other).start()

    keep(load_send.at[me], load_recv.at[me], load_rsem)

    loads[9].wait()
    wait_halo(0)
    wait_halo(1)
    rim = rims(edge_recv[1, 2], edge_recv[1, 3])
    for t in range(tiers):
        c, (low, high, north, south, west, east) = inside(cond, t)
        here = rim[:, t * cols : (t + 1) * cols]
        low = plane_recv[1, 0] if t == 0 else low
        high = plane_recv[1, 1] if t == tiers - 1 else high
        north = jnp.where(row_i == 0, edge_recv[1, 0, tiers + t : tiers + t + 1, :], north)
        south = jnp.where(row_i == rows - 1, edge_recv[1, 1, t : t + 1, :], south)
        west = jnp.where(col_i == 0, here, west)
        east = jnp.where(col_i == cols - 1, here, east)
        total = mass[t]
        for k, beside in enumerate((low, high, north, south, west, east)):
            face = 0.5 * (c + beside)
            faces[k, t] = face
            total = total + face
        diag[t] = total
        inv[t] = 1.0 / total
    for t in range(tiers):
        resid[t] = mass[t] * temp[t] - apply_inside(temp, t)
    add_beyond(0)

    middle = (EIG_LOW + EIG_HIGH) / 2.0
    spread = (EIG_HIGH - EIG_LOW) / 2.0
    ratio = middle / spread
    weight_a = 1.0 / ratio
    weight_b = 1.0 / (2.0 * ratio - weight_a)
    weight_c = 1.0 / (2.0 * ratio - weight_b)
    keep_b, push_b = weight_b * weight_a, 2.0 * weight_b / spread
    keep_c, push_c = weight_c * weight_b, 2.0 * weight_c / spread

    for t in range(tiers):
        scaled = push_b * inv[t]
        for k in range(6):
            faces[k, t] = scaled * faces[k, t]

    def layer_face(t):
        if t == 0 and t == tiers - 1:
            raise ValueError("one tier")
        return faces[0, t] if t == 0 else faces[1, t] if t == tiers - 1 else jnp.zeros((rows, cols), F32)

    first, last = slice(0, 1), slice(rows - 1, rows)
    side_face = [jnp.where(col_i == 0, faces[4, t], jnp.where(col_i == cols - 1, faces[5, t], 0.0)) for t in range(tiers)]
    ends_face = [jnp.where(row_i == 0, faces[2, t], jnp.where(row_i == rows - 1, faces[3, t], 0.0)) for t in range(tiers)]
    gain_send[0] = rows_of(lambda t: faces[2, t, first, :], lambda t: faces[3, t, last, :])
    gain_send[1] = rows_of(lambda t: layer_face(t)[first, :], lambda t: layer_face(t)[last, :])
    gain_send[2] = rows_of(lambda t: side_face[t][first, :], lambda t: side_face[t][last, :])
    gain_send[3] = columns_of(lambda t: side_face[t])
    gain_send[4] = columns_of(layer_face)
    gain_send[5] = columns_of(lambda t: ends_face[t])
    for exists, where, side in sides[2:]:
        lands = (side - 2) ^ 1

        @pl.when(exists)
        def _(where=where, side=side, lands=lands):
            send(
                gain_send.at[0:3] if side < 4 else gain_send.at[3:6],
                gain_recv.at[3 * lands : 3 * lands + 3],
                gain_ssem,
                gain_rsem,
                where,
            )

    sources = tiles * CAP * FOLDS
    sel_i = iota((FOLDS * patches, sources), 0)
    sel_j = iota((FOLDS * patches, sources), 1)
    sel_in = mod(sel_i, patches)
    sel_patch = mod(sel_in, bands) * per_band + div(sel_in, bands)
    fold_hit = div(sel_i, patches) == mod(sel_j, FOLDS)
    bytes_of(place_recv, place_rsem).wait()
    place_i = iota((named, sources), 0)
    place_j = div(iota((named, sources), 1), FOLDS)
    place_j = div(place_j, CAP) * 8 + mod(place_j, CAP)
    places = jnp.concatenate([place_recv[...]] * (sources // LANES), axis=1)
    code = jnp.sum(jnp.where(place_i == place_j, places, 0.0), axis=0, keepdims=True)
    picker = jnp.where(fold_hit & (code == (sel_patch + 1).astype(F32)), 1.0, 0.0).astype(BF16)
    bytes_of(load_recv, load_rsem).wait()
    footprint = jnp.dot(picker, load_recv[...].reshape(sources, wide), preferred_element_type=F32)
    left = iota((bands, LANES), 1) < SUB
    for fold in range(FOLDS):
        for k in range(wide // LANES):
            lanes = slice(k * LANES, (k + 1) * LANES)
            a = footprint[fold * patches : fold * patches + bands, lanes]
            b = footprint[fold * patches + bands : fold * patches + 2 * bands, lanes]
            at = 2 * (fold * (wide // LANES) + k)
            power_ref[pl.ds(at, bands, stride=SUB), :] = jnp.where(left, a, pltpu.roll(b, SUB, 1))
            power_ref[pl.ds(at + 1, bands, stride=SUB), :] = jnp.where(left, pltpu.roll(a, SUB, 1), b)

    for t in range(tiers):
        r = resid[t] + power_ref[t * rows : (t + 1) * rows, :]
        resid[t] = r
        dirs[0, t] = r * inv[t] * (1.0 / middle)
    start, after = dirs.at[0], dirs.at[1]

    def send_rims(which):
        for step, block, count, _ in which:
            exists, where = neighbour(*step)
            lands = slot_of[tuple(-d for d in step)]

            @pl.when(exists)
            def _(where=where, block=block, count=count, lands=lands):
                send(
                    rim_send.at[block : block + count],
                    rim_recv.at[lands : lands + count],
                    rim_ssem,
                    rim_rsem,
                    where,
                )

    def send_planes(turn, field):
        for exists, where, side in sides[:2]:
            halo_start(turn, field, exists, where, side)

    def around_sum(field, t):
        v, around = inside(field, t)
        value = None
        for k in range(6):
            if not (k == 0 and t == 0 or k == 1 and t == tiers - 1):
                term = faces[k, t] * around[k]
                value = term if value is None else value + term
        return v, value

    own_rows = rows_of(lambda t: start[t, first, :], lambda t: start[t, last, :])
    rim_send[0] = own_rows
    send_rims(rims_of[:8])
    own_columns = columns_of(lambda t: start[t])
    rim_send[2] = own_columns
    send_rims(rims_of[8:12])
    stay = keep_b + push_b * (middle - 1.0)
    for t in range(tiers):
        v, value = around_sum(start, t)
        after[t] = stay * v + value
    rim_send[1] = rows_of(lambda t: after[t, first, :], lambda t: after[t, last, :])
    send_rims(rims_of[12:14])
    rim_send[3] = columns_of(lambda t: after[t])
    send_rims(rims_of[14:])
    send_planes(2, start)
    bytes_of(gain_recv, gain_rsem).wait()
    wait_plane(2)
    bytes_of(rim_recv, rim_rsem).wait()

    eight_s = iota((2 * tiers, cols), 0)
    eight_l = iota((2 * tiers, cols), 1)
    upper = eight_s >= tiers
    tier_s = mod(eight_s, tiers)

    def pair(a, b):
        return jnp.where(upper, a, b)

    def swap(x):
        return pltpu.roll(x, tiers, 0)

    def layer_part(down, up):
        return jnp.where(
            tier_s == 0, pltpu.roll(down, tiers + 1, 0), jnp.where(tier_s == tiers - 1, pltpu.roll(up, tiers - 1, 0), 0.0)
        )

    north_west, north_east, south_west, south_east = (rim_recv[8 + i] for i in range(4))

    def shell(own, at, layer_at, gain_at, side_part):
        return (
            pair(rim_recv[at + 1], rim_recv[at + 3])
            + pair(gain_recv[gain_at], gain_recv[gain_at + 3]) * swap(own)
            + pair(gain_recv[gain_at + 1], gain_recv[gain_at + 4])
            * layer_part(
                pair(rim_recv[layer_at], rim_recv[layer_at + 2]), pair(rim_recv[layer_at + 1], rim_recv[layer_at + 3])
            )
            + pair(gain_recv[gain_at + 2], gain_recv[gain_at + 5]) * side_part
        )

    row_shell = shell(
        own_rows,
        0,
        12,
        0,
        jnp.where(
            eight_l == 0,
            pltpu.roll(pair(north_west, south_west), 1, 1),
            pltpu.roll(pair(north_east, south_east), cols - 1, 1),
        ),
    )
    col_shell = shell(
        own_columns,
        4,
        16,
        6,
        jnp.where(
            eight_l == 0,
            pair(pltpu.roll(north_west, 1, 1), swap(north_east)),
            pair(swap(south_west), pltpu.roll(south_east, cols - 1, 1)),
        ),
    )
    rim_a = rims(rim_recv[4], rim_recv[6])
    rim_b = rims(col_shell, col_shell)

    def beyond_rows(ref, t, scale, north, south, rim):
        ref[t, first, :] = ref[t, first, :] + scale * faces[2, t, first, :] * north
        ref[t, last, :] = ref[t, last, :] + scale * faces[3, t, last, :] * south
        face = jnp.where(col_i == 0, faces[4, t], faces[5, t])
        ref[t] = ref[t] + scale * face * rim[:, t * cols : (t + 1) * cols]

    outer = sorted(range(tiers), key=lambda t: 0 < t < tiers - 1)
    for t in outer:
        if t == 0:
            after[t] = after[t] + faces[0, t] * plane_recv[2, 0]
        if t == tiers - 1:
            after[t] = after[t] + faces[1, t] * plane_recv[2, 1]
        beyond_rows(
            after, t, 1.0, rim_recv[0, tiers + t : tiers + t + 1, :], rim_recv[2, t : t + 1, :], rim_a
        )
        if t == outer[min(1, tiers - 1)]:
            send_planes(3, after)
    lift = push_c / push_b
    old = 1.0 - lift * keep_b
    now = 1.0 + keep_c + lift - push_c
    for t in range(tiers):
        v, value = around_sum(after, t)
        out_ref[t] = temp[t] + old * start[t] + now * v + lift * value
        beyond_rows(
            out_ref, t, lift, row_shell[tiers + t : tiers + t + 1, :], row_shell[t : t + 1, :], rim_b
        )
    wait_plane(3)
    out_ref[0] = out_ref[0] + lift * faces[0, 0] * plane_recv[3, 0]
    out_ref[tiers - 1] = out_ref[tiers - 1] + lift * faces[1, tiers - 1] * plane_recv[3, 1]

    bytes_of(plane_recv, halo_ssem.at[0]).wait()
    bytes_of(edge_recv, halo_ssem.at[1]).wait()
    bytes_of(rim_recv, rim_ssem).wait()
    bytes_of(gain_recv, gain_ssem).wait()
    bytes_of(note_recv.at[1:], note_ssem).wait()
    bytes_of(place_recv.at[8:, :], place_ssem).wait()
    bytes_of(load_recv.at[1:], load_ssem).wait()


def hand_over(new, power, new_out, power_out, sem):
    moves = (pltpu.make_async_copy(power, power_out, sem.at[0]), pltpu.make_async_copy(new, new_out, sem.at[1]))
    for move in moves:
        move.start()
    for move in moves:
        move.wait()


def shards(sizes, temp, cond, mass, dyn, leak, panel, place, block, tier, sens):
    tiers, rows, cols = temp.shape
    slots, cells = dyn.shape[1:]
    tiles = sizes[0] * sizes[1]
    any_spec = pl.BlockSpec(memory_space=pl.ANY)
    vmem_spec = pl.BlockSpec(memory_space=pltpu.VMEM)
    grid = (tiers, rows, cols)
    dma = pltpu.SemaphoreType.DMA
    new, power = pl.pallas_call(
        functools.partial(kernel, sizes),
        out_shape=(
            pltpu.VMEM(grid, F32),
            pltpu.VMEM((tiers * rows, cols), F32),
        ),
        in_specs=[any_spec] * 10,
        out_specs=(vmem_spec, vmem_spec),
        scratch_shapes=[
            pltpu.VMEM((1, slots), jnp.int32),
            pltpu.VMEM((1, slots), jnp.int32),
            pltpu.VMEM((1, slots), jnp.int32),
            pltpu.VMEM(tier.shape, jnp.int32),
            pltpu.VMEM(sens.shape, F32),
            pltpu.VMEM(grid, F32),
            pltpu.VMEM(grid, F32),
            pltpu.VMEM(grid, F32),
            pltpu.VMEM((slots, cells), BF16),
            pltpu.VMEM((slots, cells), BF16),
            pltpu.VMEM((cells // FOLDS // LANES, tiles * CAP * FOLDS, LANES), F32),
            pltpu.VMEM((cells // FOLDS // LANES, tiles * CAP * FOLDS, LANES), F32),
            pltpu.VMEM((1, LANES), F32),
            pltpu.VMEM((tiles, 1, LANES), F32),
            pltpu.VMEM((8 * tiles, LANES), F32),
            pltpu.VMEM((8 * tiles, LANES), F32),
            pltpu.VMEM((8 * tiles, LANES), F32),
            pltpu.VMEM((tiles, CAP * FOLDS, cells // FOLDS), BF16),
            pltpu.VMEM((tiles, CAP * FOLDS, cells // FOLDS), BF16),
            pltpu.VMEM((SWEEPS - 1,) + grid, F32),
            pltpu.VMEM((6,) + grid, F32),
            pltpu.VMEM(grid, F32),
            pltpu.VMEM(grid, F32),
            pltpu.VMEM(grid, F32),
            pltpu.VMEM((2, 2, 2 * tiers, cols), F32),
            pltpu.VMEM((2, 4, 2 * tiers, cols), F32),
            pltpu.VMEM((2, 4, 2 * tiers, cols), F32),
            pltpu.VMEM((4, 2, rows, cols), F32),
            pltpu.VMEM((4, 2, rows, cols), F32),
            pltpu.VMEM((4, 2 * tiers, cols), F32),
            pltpu.VMEM((20, 2 * tiers, cols), F32),
            pltpu.VMEM((20, 2 * tiers, cols), F32),
            pltpu.VMEM((6, 2 * tiers, cols), F32),
            pltpu.VMEM((12, 2 * tiers, cols), F32),
            pltpu.VMEM((12, 2 * tiers, cols), F32),
            pltpu.VMEM((rows, cols), F32),
            dma((10,)),
            dma(()),
            dma(()),
            dma(()),
            dma(()),
            dma(()),
            dma(()),
            dma((2,)),
            dma((4, 2)),
            dma(()),
            dma(()),
            dma(()),
            dma(()),
        ],
        compiler_params=pltpu.CompilerParams(
            collective_id=0, has_side_effects=True, vmem_limit_bytes=VMEM_BYTES
        ),
    )(
        *(
            pltpu.with_memory_space_constraint(given, pltpu.HBM)
            for given in (temp, cond, mass, dyn, leak, panel.reshape(1, slots), place, block, tier, sens)
        )
    )
    return pl.pallas_call(
        hand_over,
        out_shape=(jax.ShapeDtypeStruct(grid, F32),) * 2,
        in_specs=[vmem_spec] * 2,
        out_specs=(any_spec, any_spec),
        scratch_shapes=[dma((2,))],
        compiler_params=pltpu.CompilerParams(vmem_limit_bytes=VMEM_BYTES),
    )(new, power.reshape(grid))


def solution(mesh):
    sizes = (mesh.shape["row"], mesh.shape["col"], mesh.shape["layer"])
    owner = ("row", "col", "layer")
    return jax.shard_map(
        functools.partial(shards, sizes),
        mesh=mesh,
        in_specs=(P("layer", "row", "col"),) * 3
        + (P(owner, None, None),) * 3
        + (P(owner, None),) * 4,
        out_specs=(P("layer", "row", "col"), P("layer", "row", "col")),
        check_vma=False,
    )
```

```python
import functools
import jax
import jax.numpy as jnp
from jax import lax
from jax.experimental import pallas as pl
from jax.experimental.pallas import tpu as pltpu
from jax.sharding import PartitionSpec as P

SUB = 64
SWEEPS = 3
CAP = 4
EIG_LOW = 0.1
EIG_HIGH = 2.0
LANES = 128
FOLDS = 4
EARLY = 1
VMEM_BYTES = 40 << 20

MESH = pl.DeviceIdType.MESH
F32 = jnp.float32
BF16 = jnp.bfloat16


def iota(shape, dim):
    return lax.broadcasted_iota(jnp.int32, shape, dim)


def div(x, n):
    if n & (n - 1):
        return x // n
    return lax.shift_right_logical(x, jnp.int32(n.bit_length() - 1))


def mod(x, n):
    if n & (n - 1):
        return lax.rem(x, n)
    return x & (n - 1)


def three_parts(x, axis):
    head = x.astype(BF16)
    rest = x - head.astype(F32)
    body = rest.astype(BF16)
    return jnp.concatenate([head, body, (rest - body.astype(F32)).astype(BF16)], axis=axis)


def two_parts(x, axis):
    head = x.astype(BF16)
    return jnp.concatenate([head, (x - head.astype(F32)).astype(BF16)], axis=axis)


def kernel(
    sizes,
    temp_hbm,
    cond_hbm,
    mass_hbm,
    dyn_hbm,
    leak_hbm,
    panel_hbm,
    place_hbm,
    block_hbm,
    tier_hbm,
    sens_hbm,
    out_ref,
    power_ref,
    panel_ref,
    place_ref,
    block_ref,
    tier_ref,
    sens_ref,
    temp,
    cond,
    mass,
    dyn,
    leak,
    dyn_pick,
    leak_pick,
    note_send,
    note_recv,
    place_send,
    place_recv,
    fac,
    fac_send,
    fac_recv,
    early_send,
    early_recv,
    early_power,
    load_send,
    load_recv,
    dirs,
    faces,
    diag,
    inv,
    resid,
    edge_send,
    edge_recv,
    edge_spare,
    plane_recv,
    plane_spare,
    rim_send,
    rim_recv,
    rim_spare,
    gain_send,
    gain_recv,
    gain_spare,
    nothing,
    in_sem,
    note_ssem,
    note_rsem,
    place_ssem,
    place_rsem,
    fac_ssem,
    fac_rsem,
    early_ssem,
    early_rsem,
    load_ssem,
    load_rsem,
    halo_ssem,
    halo_rsem,
    rim_ssem,
    rim_rsem,
    gain_ssem,
    gain_rsem,
):
    n_row, n_col, n_layer = sizes
    tiles = n_row * n_col
    tiers, rows, cols = temp.shape
    slots, cells = dyn.shape
    wide = cells // FOLDS
    halves = wide // LANES
    rows_of_tile = CAP * FOLDS
    named = 8 * tiles
    in_plane = (rows // SUB) * (cols // SUB)
    patches = tiers * in_plane
    bands = tiers * (rows // SUB)
    my_row = lax.axis_index("row")
    my_col = lax.axis_index("col")
    my_layer = lax.axis_index("layer")
    me = my_row * n_col + my_col

    loads = [
        pltpu.make_async_copy(src, dst, in_sem.at[i])
        for i, (src, dst) in enumerate(
            (
                (temp_hbm, temp),
                (panel_hbm, panel_ref),
                (place_hbm, place_ref),
                (block_hbm, block_ref),
                (tier_hbm, tier_ref),
                (sens_hbm, sens_ref),
                (dyn_hbm.at[0], dyn),
                (leak_hbm.at[0], leak),
                (cond_hbm, cond),
                (mass_hbm, mass),
            )
        )
    ]
    for load in loads:
        load.start()

    def far_first(step):
        if n_row & (n_row - 1) or n_col & (n_col - 1) or n_col == 1:
            return lax.rem(me + step, tiles)
        near = n_col // 2
        turn = mod(step, tiles // 2)
        over_row = n_row - 1 - div(turn, near)
        over_col = n_col - 1 - mod(turn, near) - near * div(step, tiles // 2)
        return lax.bitwise_xor(my_row, over_row) * n_col + lax.bitwise_xor(my_col, over_col)

    def each_peer(act):
        @pl.loop(0, tiles)
        def _(step):
            other = far_first(step)
            pl.when(other != me)(lambda: act(other))

    def device(other):
        return {"row": div(other, n_col), "col": mod(other, n_col)}

    sides = (
        (my_layer > 0, {"layer": my_layer - 1}, 0),
        (my_layer < n_layer - 1, {"layer": my_layer + 1}, 1),
        (my_row > 0, {"row": my_row - 1}, 2),
        (my_row < n_row - 1, {"row": my_row + 1}, 3),
        (my_col > 0, {"col": my_col - 1}, 4),
        (my_col < n_col - 1, {"col": my_col + 1}, 5),
    )

    def neighbour(d_row, d_col, d_layer):
        exists, where = [], {}
        for axis, mine, count, d in (
            ("row", my_row, n_row, d_row),
            ("col", my_col, n_col, d_col),
            ("layer", my_layer, n_layer, d_layer),
        ):
            if d:
                exists.append(mine > 0 if d < 0 else mine < count - 1)
                where[axis] = mine + d
        return functools.reduce(jnp.logical_and, exists), where

    rims_of = (
        [((a, b, 0), 0, 1, 8 + i) for i, (a, b) in enumerate(((-1, -1), (-1, 1), (1, -1), (1, 1)))]
        + [((a, 0, c), 0, 1, 12 + i) for i, (a, c) in enumerate(((-1, -1), (-1, 1), (1, -1), (1, 1)))]
        + [((0, b, c), 2, 1, 16 + i) for i, (b, c) in enumerate(((-1, -1), (-1, 1), (1, -1), (1, 1)))]
        + [((-1, 0, 0), 0, 2, 0), ((1, 0, 0), 0, 2, 2), ((0, -1, 0), 2, 2, 4), ((0, 1, 0), 2, 2, 6)]
    )
    slot_of = {step: slot for step, _, _, slot in rims_of}

    nothing[...] = jnp.zeros_like(nothing)
    barrier = pltpu.get_barrier_semaphore()

    each_peer(
        lambda other: pl.semaphore_signal(barrier, inc=1, device_id=device(other), device_id_type=MESH)
    )

    across = [neighbour(*step) for step, _, _, _ in rims_of if step[2]] + [neighbour(0, 0, -1), neighbour(0, 0, 1)]
    for exists, where in across:

        @pl.when(exists)
        def _(where=where):
            pl.semaphore_signal(barrier, inc=1, device_id=where, device_id_type=MESH)

    def remote(src, dst, ssem, rsem, other):
        return pltpu.make_async_remote_copy(
            src_ref=src,
            dst_ref=dst,
            send_sem=ssem,
            recv_sem=rsem,
            device_id=device(other),
            device_id_type=MESH,
        )

    def note_copy(other):
        return remote(note_send, note_recv.at[me], note_ssem, note_rsem, other)

    def place_copy(other):
        return remote(place_send.at[other], place_recv.at[me], place_ssem, place_rsem, other)

    def fac_copy(other):
        return remote(fac_send.at[other], fac_recv.at[me], fac_ssem, fac_rsem, other)

    def early_copy(other):
        return remote(early_send.at[other], early_recv.at[me], early_ssem, early_rsem, other)

    def load_copy(other):
        return remote(load_send.at[other], load_recv.at[me], load_ssem, load_rsem, other)

    def send(src, dst, ssem, rsem, where):
        pltpu.make_async_remote_copy(
            src_ref=src, dst_ref=dst, send_sem=ssem, recv_sem=rsem, device_id=where, device_id_type=MESH
        ).start()

    def bytes_of(ref, sem):
        return pltpu.make_async_copy(ref, ref, sem)

    def keep(src, dst, sem):
        pltpu.make_async_copy(src, dst, sem).start()

    loads[0].wait()
    band_sums = jnp.concatenate(
        [
            jnp.sum(temp[t, b * SUB : (b + 1) * SUB, :], axis=0, keepdims=True)
            for t in range(tiers)
            for b in range(rows // SUB)
        ],
        axis=0,
    )
    lane_b = iota((bands, LANES), 1)
    sub_b = iota((bands, LANES), 0)
    means = jnp.zeros((1, LANES), F32)
    per_band = cols // SUB
    for part in range(per_band):
        total = jnp.sum(jnp.where(div(lane_b, SUB) == part, band_sums, 0.0), axis=1, keepdims=True)
        means = means + jnp.sum(
            jnp.where(lane_b == sub_b * per_band + part, total, 0.0), axis=0, keepdims=True
        )
    means = means * (1.0 / (SUB * SUB))
    note_send[...] = means
    lane_s = iota((slots, slots), 1)
    sub_s = iota((slots, slots), 0)
    eye = lane_s == sub_s

    def to_col(row):
        return jnp.sum(jnp.where(eye, jnp.broadcast_to(row, (slots, slots)), 0.0), axis=1, keepdims=True)

    def to_row(col):
        return jnp.sum(jnp.where(eye, jnp.broadcast_to(col, (slots, slots)), 0.0), axis=0, keepdims=True)

    for load in loads[1:6]:
        load.wait()
    tgt_row = panel_ref[...].astype(F32)
    tgt_col = to_col(tgt_row)
    blk_row = block_ref[...].astype(F32)
    blk_col = to_col(blk_row)
    sub_col = to_col(place_ref[...].astype(F32))
    same_tile = tgt_col == tgt_row
    rank_col = jnp.sum(jnp.where(same_tile & (lane_s < sub_s), 1.0, 0.0), axis=1, keepdims=True)
    rank_row = jnp.sum(jnp.where(same_tile & (sub_s < lane_s), 1.0, 0.0), axis=0, keepdims=True)
    blocks = tier_ref.shape[1]
    of_block = blk_col == iota((slots, blocks), 1).astype(F32)
    tier_col = jnp.sum(jnp.where(of_block, tier_ref[...].astype(F32), 0.0), axis=1, keepdims=True)
    sens_col = jnp.sum(jnp.where(of_block, sens_ref[...], 0.0), axis=1, keepdims=True)
    pos_col = tier_col * in_plane + sub_col
    goes = (tgt_row * CAP + rank_row) == iota((tiles * CAP, slots), 0).astype(F32)
    pick = jnp.where(goes, 1.0, 0.0).astype(BF16)
    loads[6].wait()
    loads[7].wait()
    for src, dst in ((dyn, dyn_pick), (leak, leak_pick)):
        for fold in range(FOLDS):
            taken = jnp.dot(pick, src[:, fold * wide : (fold + 1) * wide], preferred_element_type=F32)
            for half in range(halves):
                dst[half, pl.ds(fold, tiles * CAP, stride=FOLDS), :] = taken[
                    :, half * LANES : (half + 1) * LANES
                ]
    for tile in range(tiles):
        for half in range(EARLY):
            at, lanes = slice(tile * rows_of_tile, (tile + 1) * rows_of_tile), slice(half * LANES, (half + 1) * LANES)
            early_send[tile, 0, :, lanes] = dyn_pick[half, at, :].astype(BF16)
            early_send[tile, 1, :, lanes] = leak_pick[half, at, :].astype(BF16)

    beyond = sum(exists.astype(jnp.int32) for exists, _ in across)
    pl.semaphore_wait(barrier, tiles - 1 + beyond)

    each_peer(lambda other: note_copy(other).start())
    keep(note_send, note_recv.at[me], note_rsem)
    each_peer(lambda other: early_copy(other).start())
    keep(early_send.at[me], early_recv.at[me], early_rsem)

    sub8 = iota((2 * tiers, 2 * cols), 0)
    lane8 = mod(iota((2 * tiers, 2 * cols), 1), cols)
    picks = [
        jnp.where(
            ((sub8 == t) & (lane8 == 0)) | ((sub8 == tiers + t) & (lane8 == cols - 1)), 1.0, 0.0
        ).astype(BF16)
        for t in range(tiers)
    ]

    def halo_ends(turn, field, side, lands):
        if side < 2:
            return field.at[0 if side == 0 else tiers - 1], plane_recv.at[turn, lands], 0
        return edge_send.at[turn, (side - 2) // 2], edge_recv.at[turn, lands - 2], 1

    def halo_start(turn, field, exists, where, side):
        @pl.when(exists)
        def _():
            src, dst, kind = halo_ends(turn, field, side, side ^ 1)
            send(src, dst, halo_ssem.at[kind], halo_rsem.at[turn, kind], where)

    def pack_rows(turn, field):
        for end in range(2):
            at = end * (rows - 1)
            for t in range(tiers):
                edge_send[turn, 0, end * tiers + t : end * tiers + t + 1, :] = field[t, at : at + 1, :]

    def columns_of(field):
        columns = jnp.zeros((2 * tiers, rows), F32)
        for t in range(tiers):
            columns = columns + lax.dot_general(
                picks[t], two_parts(field(t), 1), (((1,), (1,)), ((), ())), preferred_element_type=F32
            )
        return columns

    def rows_of(first, last):
        return jnp.concatenate([first(t) for t in range(tiers)] + [last(t) for t in range(tiers)], axis=0)

    def start_halo(turn, field):
        def start(which):
            for exists, where, side in which:
                halo_start(turn, field, exists, where, side)

        pack_rows(turn, field)
        start(sides[2:4])
        start(sides[:2])
        edge_send[turn, 1] = columns_of(lambda t: field[t])
        start(sides[4:])

    def wait_plane(turn):
        bytes_of(plane_recv.at[turn], halo_rsem.at[turn, 0]).wait()

    def wait_halo(turn):
        wait_plane(turn)
        bytes_of(edge_recv.at[turn], halo_rsem.at[turn, 1]).wait()

    row_i = iota((rows, cols), 0)
    col_i = iota((rows, cols), 1)
    sub16 = mod(iota((8 * tiers, tiers * cols), 0), 4 * tiers)
    lane16 = iota((8 * tiers, tiers * cols), 1)
    put = jnp.where(
        ((mod(lane16, cols) == 0) & (sub16 == tiers + div(lane16, cols)))
        | ((mod(lane16, cols) == cols - 1) & (sub16 == 2 * tiers + div(lane16, cols))),
        1.0,
        0.0,
    ).astype(BF16)

    def inside(field, t):
        v = field[t]
        none = jnp.zeros_like(v)
        low = none if t == 0 else field[t - 1]
        high = none if t == tiers - 1 else field[t + 1]
        north = jnp.where(row_i == 0, 0.0, pltpu.roll(v, 1, 0))
        south = jnp.where(row_i == rows - 1, 0.0, pltpu.roll(v, rows - 1, 0))
        west = jnp.where(col_i == 0, 0.0, pltpu.roll(v, 1, 1))
        east = jnp.where(col_i == cols - 1, 0.0, pltpu.roll(v, cols - 1, 1))
        return v, (low, high, north, south, west, east)

    def rims(west, east):
        ends = jnp.concatenate([west, east], axis=0)
        return lax.dot_general(
            two_parts(ends, 0), put, (((0,), (0,)), ((), ())), preferred_element_type=F32
        )

    def apply_inside(field, t):
        v, around = inside(field, t)
        value = diag[t] * v
        for k in range(6):
            if not (k == 0 and t == 0 or k == 1 and t == tiers - 1):
                value = value - faces[k, t] * around[k]
        return value

    def add_beyond(turn):
        rim = rims(edge_recv[turn, 2], edge_recv[turn, 3])
        resid[0] = resid[0] + faces[0, 0] * plane_recv[turn, 0]
        resid[tiers - 1] = resid[tiers - 1] + faces[1, tiers - 1] * plane_recv[turn, 1]
        for t in range(tiers):
            first, last = slice(0, 1), slice(rows - 1, rows)
            resid[t, first, :] = (
                resid[t, first, :] + faces[2, t, first, :] * edge_recv[turn, 0, tiers + t : tiers + t + 1, :]
            )
            resid[t, last, :] = (
                resid[t, last, :] + faces[3, t, last, :] * edge_recv[turn, 1, t : t + 1, :]
            )
            face = jnp.where(col_i == 0, faces[4, t], faces[5, t])
            resid[t] = resid[t] + face * rim[:, t * cols : (t + 1) * cols]

    name_r = iota((named, slots), 0).astype(F32)
    named_row = tgt_row * 8.0 + rank_row
    named_col = tgt_col * 8.0 + rank_col
    by_name = name_r == named_row

    def rename(row):
        return jnp.sum(jnp.where(by_name, row, 0.0), axis=1, keepdims=True)

    pos_r = rename(to_row(pos_col) + 1.0)
    blk_r = rename(blk_row + 1.0)
    sens_r = rename(to_row(sens_col))
    blk_n = jnp.sum(
        jnp.where(named_col == iota((slots, named), 1).astype(F32), blk_col + 1.0, 0.0), axis=0, keepdims=True
    )
    same_block = jnp.where((blk_r == blk_n) & (blk_r > 0.0), 1.0, 0.0)
    block_size = jnp.maximum(jnp.sum(same_block, axis=1, keepdims=True), 1.0)
    same_three = jnp.concatenate([same_block.astype(BF16)] * 3, axis=1)
    at_place = (iota((named, LANES), 1) + 1).astype(F32) == pos_r
    group = div(iota((8, LANES), 1), LANES // CAP) == iota((8, LANES), 0)

    def one_row(block):
        return jnp.sum(jnp.where(group, block, 0.0), axis=0, keepdims=True)

    for tile in range(tiles):
        place_send[tile] = one_row(jnp.broadcast_to(pos_r[tile * 8 : (tile + 1) * 8], (8, LANES)))
    each_peer(lambda other: place_copy(other).start())
    keep(place_send.at[me], place_recv.at[me], place_rsem)

    loads[8].wait()
    start_halo(0, temp)
    start_halo(1, cond)

    bytes_of(note_recv, note_rsem).wait()
    tile_means = jnp.concatenate([jnp.broadcast_to(note_recv[tile], (8, LANES)) for tile in range(tiles)], axis=0)
    at_slots = three_parts(jnp.where(at_place, tile_means, 0.0), 0)
    block_sum = jnp.sum(
        jnp.dot(same_three, at_slots, preferred_element_type=F32), axis=1, keepdims=True
    )
    fac[...] = jnp.broadcast_to(jnp.exp(sens_r * (block_sum / block_size)), (named, LANES))

    upper_rank = iota((8, LANES), 0) >= FOLDS
    for tile in range(tiles):
        fac_send[tile] = one_row(fac[tile * 8 : (tile + 1) * 8, :])
    each_peer(lambda other: fac_copy(other).start())
    keep(fac_send.at[me], fac_recv.at[me], fac_rsem)


    @pl.loop(0, tiles)
    def _(step):
        other = far_first(step)

        def factor_of(rank):
            return fac[pl.ds(other * 8 + rank, 8, stride=0), :]

        by = jnp.concatenate(
            [jnp.where(upper_rank, factor_of(rank + 1), factor_of(rank)) for rank in range(0, CAP, 2)], axis=0
        )
        at = pl.ds(pl.multiple_of(other * rows_of_tile, rows_of_tile), rows_of_tile)
        for half in range(EARLY, halves):
            load_send[other, :, (half - EARLY) * LANES : (half - EARLY + 1) * LANES] = (
                dyn_pick[half, at, :] + by * leak_pick[half, at, :]
            ).astype(BF16)

        @pl.when(other != me)
        def _():
            load_copy(other).start()

    keep(load_send.at[me], load_recv.at[me], load_rsem)
    def missing(exists, blocks):
        @pl.when(jnp.logical_not(exists))
        def _():
            for recv, spare, at, ssem, rsem, none in blocks:
                keep(none, recv.at[at], rsem)
                keep(none, spare.at[at], ssem)

    none8 = nothing.at[:8, :]
    for exists, _, side in sides[:2]:
        missing(
            exists,
            [
                (plane_recv.at[turn], plane_spare.at[turn], side, halo_ssem.at[0], halo_rsem.at[turn, 0], nothing)
                for turn in range(4)
            ],
        )
    for exists, _, side in sides[2:]:
        missing(
            exists,
            [
                (edge_recv.at[turn], edge_spare.at[turn], side - 2, halo_ssem.at[1], halo_rsem.at[turn, 1], none8)
                for turn in range(2)
            ]
            + [(gain_recv, gain_spare, 3 * (side - 2) + k, gain_ssem, gain_rsem, none8) for k in range(3)],
        )
    for step, _, count, slot in rims_of:
        missing(
            neighbour(*step)[0],
            [(rim_recv, rim_spare, slot + k, rim_ssem, rim_rsem, none8) for k in range(count)],
        )
    loads[9].wait()
    wait_halo(0)
    wait_halo(1)
    rim = rims(edge_recv[1, 2], edge_recv[1, 3])
    for t in range(tiers):
        c, (low, high, north, south, west, east) = inside(cond, t)
        here = rim[:, t * cols : (t + 1) * cols]
        low = plane_recv[1, 0] if t == 0 else low
        high = plane_recv[1, 1] if t == tiers - 1 else high
        north = jnp.where(row_i == 0, edge_recv[1, 0, tiers + t : tiers + t + 1, :], north)
        south = jnp.where(row_i == rows - 1, edge_recv[1, 1, t : t + 1, :], south)
        west = jnp.where(col_i == 0, here, west)
        east = jnp.where(col_i == cols - 1, here, east)
        total = mass[t]
        for k, beside in enumerate((low, high, north, south, west, east)):
            face = 0.5 * (c + beside)
            faces[k, t] = face
            total = total + face
        diag[t] = total
        inv[t] = 1.0 / total
    for t in range(tiers):
        resid[t] = mass[t] * temp[t] - apply_inside(temp, t)
    add_beyond(0)

    middle = (EIG_LOW + EIG_HIGH) / 2.0
    spread = (EIG_HIGH - EIG_LOW) / 2.0
    ratio = middle / spread
    weight_a = 1.0 / ratio
    weight_b = 1.0 / (2.0 * ratio - weight_a)
    weight_c = 1.0 / (2.0 * ratio - weight_b)
    keep_b, push_b = weight_b * weight_a, 2.0 * weight_b / spread
    keep_c, push_c = weight_c * weight_b, 2.0 * weight_c / spread

    for t in range(tiers):
        scaled = push_b * inv[t]
        for k in range(6):
            faces[k, t] = scaled * faces[k, t]

    def layer_face(t):
        if t == 0 and t == tiers - 1:
            raise ValueError("one tier")
        return faces[0, t] if t == 0 else faces[1, t] if t == tiers - 1 else jnp.zeros((rows, cols), F32)

    first, last = slice(0, 1), slice(rows - 1, rows)
    side_face = [jnp.where(col_i == 0, faces[4, t], jnp.where(col_i == cols - 1, faces[5, t], 0.0)) for t in range(tiers)]
    ends_face = [jnp.where(row_i == 0, faces[2, t], jnp.where(row_i == rows - 1, faces[3, t], 0.0)) for t in range(tiers)]
    gain_send[0] = rows_of(lambda t: faces[2, t, first, :], lambda t: faces[3, t, last, :])
    gain_send[1] = rows_of(lambda t: layer_face(t)[first, :], lambda t: layer_face(t)[last, :])
    gain_send[2] = rows_of(lambda t: side_face[t][first, :], lambda t: side_face[t][last, :])
    gain_send[3] = columns_of(lambda t: side_face[t])
    gain_send[4] = columns_of(layer_face)
    gain_send[5] = columns_of(lambda t: ends_face[t])
    for exists, where, side in sides[2:]:
        lands = (side - 2) ^ 1

        @pl.when(exists)
        def _(where=where, side=side, lands=lands):
            send(
                gain_send.at[0:3] if side < 4 else gain_send.at[3:6],
                gain_recv.at[3 * lands : 3 * lands + 3],
                gain_ssem,
                gain_rsem,
                where,
            )

    sources = tiles * CAP * FOLDS
    sel_i = iota((FOLDS * patches, sources), 0)
    sel_j = iota((FOLDS * patches, sources), 1)
    sel_in = mod(sel_i, patches)
    sel_patch = mod(sel_in, bands) * per_band + div(sel_in, bands)
    fold_hit = div(sel_i, patches) == mod(sel_j, FOLDS)
    bytes_of(place_recv, place_rsem).wait()
    def by_source(ref):
        taken = jnp.concatenate([jnp.broadcast_to(ref[tile], (rows_of_tile, LANES)) for tile in range(tiles)], axis=0)
        rank = div(mod(iota(taken.shape, 0), rows_of_tile), FOLDS)
        return jnp.sum(jnp.where(iota(taken.shape, 1) == rank * (LANES // CAP), taken, 0.0), axis=1, keepdims=True)

    same = iota((sources, sources), 0) == iota((sources, sources), 1)
    code = jnp.sum(jnp.where(same, by_source(place_recv), 0.0), axis=0, keepdims=True)
    picker = jnp.where(fold_hit & (code == (sel_patch + 1).astype(F32)), 1.0, 0.0).astype(BF16)
    left = iota((bands, LANES), 1) < SUB

    def deposit(footprint, begin, end):
        for fold in range(FOLDS):
            for k in range(begin, end):
                lanes = slice((k - begin) * LANES, (k - begin + 1) * LANES)
                a = footprint[fold * patches : fold * patches + bands, lanes]
                b = footprint[fold * patches + bands : fold * patches + 2 * bands, lanes]
                at = 2 * (fold * halves + k)
                power_ref[pl.ds(at, bands, stride=SUB), :] = jnp.where(left, a, pltpu.roll(b, SUB, 1))
                power_ref[pl.ds(at + 1, bands, stride=SUB), :] = jnp.where(left, pltpu.roll(a, SUB, 1), b)

    bytes_of(fac_recv, fac_rsem).wait()
    factors = by_source(fac_recv)
    bytes_of(early_recv, early_rsem).wait()
    for half in range(EARLY):
        lanes = slice(half * LANES, (half + 1) * LANES)
        for tile in range(tiles):
            early_power[tile * rows_of_tile : (tile + 1) * rows_of_tile, lanes] = (
                early_recv[tile, 0, :, lanes].astype(F32)
                + factors[tile * rows_of_tile : (tile + 1) * rows_of_tile] * early_recv[tile, 1, :, lanes].astype(F32)
            ).astype(BF16)
    deposit(jnp.dot(picker, early_power[...], preferred_element_type=F32), 0, EARLY)
    bytes_of(load_recv, load_rsem).wait()
    deposit(
        jnp.dot(picker, load_recv[...].reshape(sources, wide - EARLY * LANES), preferred_element_type=F32), EARLY, halves
    )
    for t in range(tiers):
        r = resid[t] + power_ref[t * rows : (t + 1) * rows, :]
        resid[t] = r
        dirs[0, t] = r * inv[t] * (1.0 / middle)
    start, after = dirs.at[0], dirs.at[1]

    def send_rims(which):
        for step, block, count, _ in which:
            exists, where = neighbour(*step)
            lands = slot_of[tuple(-d for d in step)]

            @pl.when(exists)
            def _(where=where, block=block, count=count, lands=lands):
                send(
                    rim_send.at[block : block + count],
                    rim_recv.at[lands : lands + count],
                    rim_ssem,
                    rim_rsem,
                    where,
                )

    def send_planes(turn, field):
        for exists, where, side in sides[:2]:
            halo_start(turn, field, exists, where, side)

    def around_sum(field, t):
        v, around = inside(field, t)
        value = None
        for k in range(6):
            if not (k == 0 and t == 0 or k == 1 and t == tiers - 1):
                term = faces[k, t] * around[k]
                value = term if value is None else value + term
        return v, value

    own_rows = rows_of(lambda t: start[t, first, :], lambda t: start[t, last, :])
    rim_send[0] = own_rows
    send_rims(rims_of[:8])
    own_columns = columns_of(lambda t: start[t])
    rim_send[2] = own_columns
    send_rims(rims_of[8:12])
    stay = keep_b + push_b * (middle - 1.0)
    for t in range(tiers):
        v, value = around_sum(start, t)
        after[t] = stay * v + value
    rim_send[1] = rows_of(lambda t: after[t, first, :], lambda t: after[t, last, :])
    send_rims(rims_of[12:14])
    rim_send[3] = columns_of(lambda t: after[t])
    send_rims(rims_of[14:])
    send_planes(2, start)
    bytes_of(gain_recv, gain_rsem).wait()
    wait_plane(2)
    bytes_of(rim_recv, rim_rsem).wait()

    eight_s = iota((2 * tiers, cols), 0)
    eight_l = iota((2 * tiers, cols), 1)
    upper = eight_s >= tiers
    tier_s = mod(eight_s, tiers)

    def pair(a, b):
        return jnp.where(upper, a, b)

    def swap(x):
        return pltpu.roll(x, tiers, 0)

    def layer_part(down, up):
        return jnp.where(
            tier_s == 0, pltpu.roll(down, tiers + 1, 0), jnp.where(tier_s == tiers - 1, pltpu.roll(up, tiers - 1, 0), 0.0)
        )

    north_west, north_east, south_west, south_east = (rim_recv[8 + i] for i in range(4))

    def shell(own, at, layer_at, gain_at, side_part):
        return (
            pair(rim_recv[at + 1], rim_recv[at + 3])
            + pair(gain_recv[gain_at], gain_recv[gain_at + 3]) * swap(own)
            + pair(gain_recv[gain_at + 1], gain_recv[gain_at + 4])
            * layer_part(
                pair(rim_recv[layer_at], rim_recv[layer_at + 2]), pair(rim_recv[layer_at + 1], rim_recv[layer_at + 3])
            )
            + pair(gain_recv[gain_at + 2], gain_recv[gain_at + 5]) * side_part
        )

    row_shell = shell(
        own_rows,
        0,
        12,
        0,
        jnp.where(
            eight_l == 0,
            pltpu.roll(pair(north_west, south_west), 1, 1),
            pltpu.roll(pair(north_east, south_east), cols - 1, 1),
        ),
    )
    col_shell = shell(
        own_columns,
        4,
        16,
        6,
        jnp.where(
            eight_l == 0,
            pair(pltpu.roll(north_west, 1, 1), swap(north_east)),
            pair(swap(south_west), pltpu.roll(south_east, cols - 1, 1)),
        ),
    )
    rim_a = rims(rim_recv[4], rim_recv[6])
    rim_b = rims(col_shell, col_shell)

    def beyond_rows(ref, t, scale, north, south, rim):
        ref[t, first, :] = ref[t, first, :] + scale * faces[2, t, first, :] * north
        ref[t, last, :] = ref[t, last, :] + scale * faces[3, t, last, :] * south
        face = jnp.where(col_i == 0, faces[4, t], faces[5, t])
        ref[t] = ref[t] + scale * face * rim[:, t * cols : (t + 1) * cols]

    outer = sorted(range(tiers), key=lambda t: 0 < t < tiers - 1)
    for t in outer:
        if t == 0:
            after[t] = after[t] + faces[0, t] * plane_recv[2, 0]
        if t == tiers - 1:
            after[t] = after[t] + faces[1, t] * plane_recv[2, 1]
        beyond_rows(
            after, t, 1.0, rim_recv[0, tiers + t : tiers + t + 1, :], rim_recv[2, t : t + 1, :], rim_a
        )
        if t == outer[min(1, tiers - 1)]:
            send_planes(3, after)
    lift = push_c / push_b
    old = 1.0 - lift * keep_b
    now = 1.0 + keep_c + lift - push_c
    for t in range(tiers):
        v, value = around_sum(after, t)
        out_ref[t] = temp[t] + old * start[t] + now * v + lift * value
        beyond_rows(
            out_ref, t, lift, row_shell[tiers + t : tiers + t + 1, :], row_shell[t : t + 1, :], rim_b
        )
    wait_plane(3)
    out_ref[0] = out_ref[0] + lift * faces[0, 0] * plane_recv[3, 0]
    out_ref[tiers - 1] = out_ref[tiers - 1] + lift * faces[1, tiers - 1] * plane_recv[3, 1]

    bytes_of(plane_recv, halo_ssem.at[0]).wait()
    bytes_of(edge_recv, halo_ssem.at[1]).wait()
    bytes_of(rim_recv, rim_ssem).wait()
    bytes_of(gain_recv, gain_ssem).wait()
    bytes_of(note_recv.at[1:], note_ssem).wait()
    bytes_of(place_recv.at[1:], place_ssem).wait()
    bytes_of(fac_recv.at[1:], fac_ssem).wait()
    bytes_of(early_recv.at[1:], early_ssem).wait()
    bytes_of(load_recv.at[1:], load_ssem).wait()


def hand_over(new, power, new_out, power_out, sem):
    moves = (pltpu.make_async_copy(power, power_out, sem.at[0]), pltpu.make_async_copy(new, new_out, sem.at[1]))
    for move in moves:
        move.start()
    for move in moves:
        move.wait()


def shards(sizes, temp, cond, mass, dyn, leak, panel, place, block, tier, sens):
    tiers, rows, cols = temp.shape
    slots, cells = dyn.shape[1:]
    tiles = sizes[0] * sizes[1]
    any_spec = pl.BlockSpec(memory_space=pl.ANY)
    vmem_spec = pl.BlockSpec(memory_space=pltpu.VMEM)
    grid = (tiers, rows, cols)
    dma = pltpu.SemaphoreType.DMA
    new, power = pl.pallas_call(
        functools.partial(kernel, sizes),
        out_shape=(
            pltpu.VMEM(grid, F32),
            pltpu.VMEM((tiers * rows, cols), F32),
        ),
        in_specs=[any_spec] * 10,
        out_specs=(vmem_spec, vmem_spec),
        scratch_shapes=[
            pltpu.VMEM((1, slots), jnp.int32),
            pltpu.VMEM((1, slots), jnp.int32),
            pltpu.VMEM((1, slots), jnp.int32),
            pltpu.VMEM(tier.shape, jnp.int32),
            pltpu.VMEM(sens.shape, F32),
            pltpu.VMEM(grid, F32),
            pltpu.VMEM(grid, F32),
            pltpu.VMEM(grid, F32),
            pltpu.VMEM((slots, cells), BF16),
            pltpu.VMEM((slots, cells), BF16),
            pltpu.VMEM((cells // FOLDS // LANES, tiles * CAP * FOLDS, LANES), F32),
            pltpu.VMEM((cells // FOLDS // LANES, tiles * CAP * FOLDS, LANES), F32),
            pltpu.VMEM((1, LANES), F32),
            pltpu.VMEM((tiles, 1, LANES), F32),
            pltpu.VMEM((tiles, 1, LANES), F32),
            pltpu.VMEM((tiles, 1, LANES), F32),
            pltpu.VMEM((8 * tiles, LANES), F32),
            pltpu.VMEM((tiles, 1, LANES), F32),
            pltpu.VMEM((tiles, 1, LANES), F32),
            pltpu.VMEM((tiles, 2, CAP * FOLDS, EARLY * LANES), BF16),
            pltpu.VMEM((tiles, 2, CAP * FOLDS, EARLY * LANES), BF16),
            pltpu.VMEM((tiles * CAP * FOLDS, EARLY * LANES), BF16),
            pltpu.VMEM((tiles, CAP * FOLDS, cells // FOLDS - EARLY * LANES), BF16),
            pltpu.VMEM((tiles, CAP * FOLDS, cells // FOLDS - EARLY * LANES), BF16),
            pltpu.VMEM((SWEEPS - 1,) + grid, F32),
            pltpu.VMEM((6,) + grid, F32),
            pltpu.VMEM(grid, F32),
            pltpu.VMEM(grid, F32),
            pltpu.VMEM(grid, F32),
            pltpu.VMEM((2, 2, 2 * tiers, cols), F32),
            pltpu.VMEM((2, 4, 2 * tiers, cols), F32),
            pltpu.VMEM((2, 4, 2 * tiers, cols), F32),
            pltpu.VMEM((4, 2, rows, cols), F32),
            pltpu.VMEM((4, 2, rows, cols), F32),
            pltpu.VMEM((4, 2 * tiers, cols), F32),
            pltpu.VMEM((20, 2 * tiers, cols), F32),
            pltpu.VMEM((20, 2 * tiers, cols), F32),
            pltpu.VMEM((6, 2 * tiers, cols), F32),
            pltpu.VMEM((12, 2 * tiers, cols), F32),
            pltpu.VMEM((12, 2 * tiers, cols), F32),
            pltpu.VMEM((rows, cols), F32),
            dma((10,)),
            dma(()),
            dma(()),
            dma(()),
            dma(()),
            dma(()),
            dma(()),
            dma(()),
            dma(()),
            dma(()),
            dma(()),
            dma((2,)),
            dma((4, 2)),
            dma(()),
            dma(()),
            dma(()),
            dma(()),
        ],
        compiler_params=pltpu.CompilerParams(
            collective_id=0, has_side_effects=True, vmem_limit_bytes=VMEM_BYTES
        ),
    )(
        *(
            pltpu.with_memory_space_constraint(given, pltpu.HBM)
            for given in (temp, cond, mass, dyn, leak, panel.reshape(1, slots), place, block, tier, sens)
        )
    )
    return pl.pallas_call(
        hand_over,
        out_shape=(jax.ShapeDtypeStruct(grid, F32),) * 2,
        in_specs=[vmem_spec] * 2,
        out_specs=(any_spec, any_spec),
        scratch_shapes=[dma((2,))],
        compiler_params=pltpu.CompilerParams(vmem_limit_bytes=VMEM_BYTES),
    )(new, power.reshape(grid))


def solution(mesh):
    sizes = (mesh.shape["row"], mesh.shape["col"], mesh.shape["layer"])
    owner = ("row", "col", "layer")
    return jax.shard_map(
        functools.partial(shards, sizes),
        mesh=mesh,
        in_specs=(P("layer", "row", "col"),) * 3
        + (P(owner, None, None),) * 3
        + (P(owner, None),) * 4,
        out_specs=(P("layer", "row", "col"), P("layer", "row", "col")),
        check_vma=False,
    )
```

```python
import functools
import jax
import jax.numpy as jnp
from jax import lax
from jax.experimental import pallas as pl
from jax.experimental.pallas import tpu as pltpu
from jax.sharding import PartitionSpec as P

SUB = 64
SWEEPS = 3
CAP = 4
EIG_LOW = 0.1
EIG_HIGH = 2.0
LANES = 128
FOLDS = 4
EARLY = 1
VMEM_BYTES = 40 << 20

MESH = pl.DeviceIdType.MESH
F32 = jnp.float32
BF16 = jnp.bfloat16


def iota(shape, dim):
    return lax.broadcasted_iota(jnp.int32, shape, dim)


def div(x, n):
    if n & (n - 1):
        return x // n
    return lax.shift_right_logical(x, jnp.int32(n.bit_length() - 1))


def mod(x, n):
    if n & (n - 1):
        return lax.rem(x, n)
    return x & (n - 1)


def three_parts(x, axis):
    head = x.astype(BF16)
    rest = x - head.astype(F32)
    body = rest.astype(BF16)
    return jnp.concatenate([head, body, (rest - body.astype(F32)).astype(BF16)], axis=axis)


def two_parts(x, axis):
    head = x.astype(BF16)
    return jnp.concatenate([head, (x - head.astype(F32)).astype(BF16)], axis=axis)


def kernel(
    sizes,
    temp_hbm,
    cond_hbm,
    mass_hbm,
    dyn_hbm,
    leak_hbm,
    panel_hbm,
    place_hbm,
    block_hbm,
    tier_hbm,
    sens_hbm,
    out_ref,
    power_ref,
    panel_ref,
    place_ref,
    block_ref,
    tier_ref,
    sens_ref,
    temp,
    cond,
    mass,
    dyn,
    leak,
    dyn_pick,
    leak_pick,
    note_send,
    note_recv,
    place_send,
    place_recv,
    fac,
    fac_send,
    fac_recv,
    early_send,
    early_recv,
    early_power,
    load_send,
    load_recv,
    dirs,
    faces,
    diag,
    inv,
    resid,
    edge_send,
    edge_recv,
    edge_spare,
    plane_recv,
    plane_spare,
    rim_send,
    rim_recv,
    rim_spare,
    gain_send,
    gain_recv,
    gain_spare,
    face_send,
    face_recv,
    face_spare,
    nothing,
    in_sem,
    note_ssem,
    note_rsem,
    place_ssem,
    place_rsem,
    fac_ssem,
    fac_rsem,
    early_ssem,
    early_rsem,
    load_ssem,
    load_rsem,
    halo_ssem,
    halo_rsem,
    rim_ssem,
    rim_rsem,
    gain_ssem,
    gain_rsem,
    face_ssem,
    face_rsem,
):
    n_row, n_col, n_layer = sizes
    tiles = n_row * n_col
    tiers, rows, cols = temp.shape
    slots, cells = dyn.shape
    wide = cells // FOLDS
    halves = wide // LANES
    rows_of_tile = CAP * FOLDS
    named = 8 * tiles
    in_plane = (rows // SUB) * (cols // SUB)
    patches = tiers * in_plane
    bands = tiers * (rows // SUB)
    my_row = lax.axis_index("row")
    my_col = lax.axis_index("col")
    my_layer = lax.axis_index("layer")
    me = my_row * n_col + my_col

    loads = [
        pltpu.make_async_copy(src, dst, in_sem.at[i])
        for i, (src, dst) in enumerate(
            (
                (temp_hbm, temp),
                (panel_hbm, panel_ref),
                (place_hbm, place_ref),
                (block_hbm, block_ref),
                (tier_hbm, tier_ref),
                (sens_hbm, sens_ref),
                (dyn_hbm.at[0], dyn),
                (leak_hbm.at[0], leak),
                (cond_hbm, cond),
                (mass_hbm, mass),
            )
        )
    ]
    for load in loads:
        load.start()

    def far_first(step):
        if n_row & (n_row - 1) or n_col & (n_col - 1) or n_col == 1:
            return lax.rem(me + step, tiles)
        near = n_col // 2
        turn = mod(step, tiles // 2)
        over_row = n_row - 1 - div(turn, near)
        over_col = n_col - 1 - mod(turn, near) - near * div(step, tiles // 2)
        return lax.bitwise_xor(my_row, over_row) * n_col + lax.bitwise_xor(my_col, over_col)

    def each_peer(act):
        @pl.loop(0, tiles)
        def _(step):
            other = far_first(step)
            pl.when(other != me)(lambda: act(other))

    def device(other):
        return {"row": div(other, n_col), "col": mod(other, n_col)}

    sides = (
        (my_layer > 0, {"layer": my_layer - 1}, 0),
        (my_layer < n_layer - 1, {"layer": my_layer + 1}, 1),
        (my_row > 0, {"row": my_row - 1}, 2),
        (my_row < n_row - 1, {"row": my_row + 1}, 3),
        (my_col > 0, {"col": my_col - 1}, 4),
        (my_col < n_col - 1, {"col": my_col + 1}, 5),
    )

    def neighbour(d_row, d_col, d_layer):
        exists, where = [], {}
        for axis, mine, count, d in (
            ("row", my_row, n_row, d_row),
            ("col", my_col, n_col, d_col),
            ("layer", my_layer, n_layer, d_layer),
        ):
            if d:
                exists.append(mine > 0 if d < 0 else mine < count - 1)
                where[axis] = mine + d
        return functools.reduce(jnp.logical_and, exists), where

    rims_of = (
        [((a, b, 0), 0, 1, 8 + i) for i, (a, b) in enumerate(((-1, -1), (-1, 1), (1, -1), (1, 1)))]
        + [((a, 0, c), 0, 1, 12 + i) for i, (a, c) in enumerate(((-1, -1), (-1, 1), (1, -1), (1, 1)))]
        + [((0, b, c), 2, 1, 16 + i) for i, (b, c) in enumerate(((-1, -1), (-1, 1), (1, -1), (1, 1)))]
        + [((-1, 0, 0), 0, 2, 0), ((1, 0, 0), 0, 2, 2), ((0, -1, 0), 2, 2, 4), ((0, 1, 0), 2, 2, 6)]
    )
    slot_of = {step: slot for step, _, _, slot in rims_of}

    nothing[...] = jnp.zeros_like(nothing)
    barrier = pltpu.get_barrier_semaphore()

    each_peer(
        lambda other: pl.semaphore_signal(barrier, inc=1, device_id=device(other), device_id_type=MESH)
    )

    across = [neighbour(*step) for step, _, _, _ in rims_of if step[2]] + [neighbour(0, 0, -1), neighbour(0, 0, 1)]
    for exists, where in across:

        @pl.when(exists)
        def _(where=where):
            pl.semaphore_signal(barrier, inc=1, device_id=where, device_id_type=MESH)

    def remote(src, dst, ssem, rsem, other):
        return pltpu.make_async_remote_copy(
            src_ref=src,
            dst_ref=dst,
            send_sem=ssem,
            recv_sem=rsem,
            device_id=device(other),
            device_id_type=MESH,
        )

    def note_copy(other):
        return remote(note_send, note_recv.at[me], note_ssem, note_rsem, other)

    def place_copy(other):
        return remote(place_send.at[other], place_recv.at[me], place_ssem, place_rsem, other)

    def fac_copy(other):
        return remote(fac_send.at[other], fac_recv.at[me], fac_ssem, fac_rsem, other)

    def early_copy(other):
        return remote(early_send.at[other], early_recv.at[me], early_ssem, early_rsem, other)

    def load_copy(other):
        return remote(load_send.at[other], load_recv.at[me], load_ssem, load_rsem, other)

    def send(src, dst, ssem, rsem, where):
        pltpu.make_async_remote_copy(
            src_ref=src, dst_ref=dst, send_sem=ssem, recv_sem=rsem, device_id=where, device_id_type=MESH
        ).start()

    def bytes_of(ref, sem):
        return pltpu.make_async_copy(ref, ref, sem)

    def keep(src, dst, sem):
        pltpu.make_async_copy(src, dst, sem).start()

    loads[0].wait()
    band_sums = jnp.concatenate(
        [
            jnp.sum(temp[t, b * SUB : (b + 1) * SUB, :], axis=0, keepdims=True)
            for t in range(tiers)
            for b in range(rows // SUB)
        ],
        axis=0,
    )
    lane_b = iota((bands, LANES), 1)
    sub_b = iota((bands, LANES), 0)
    means = jnp.zeros((1, LANES), F32)
    per_band = cols // SUB
    for part in range(per_band):
        total = jnp.sum(jnp.where(div(lane_b, SUB) == part, band_sums, 0.0), axis=1, keepdims=True)
        means = means + jnp.sum(
            jnp.where(lane_b == sub_b * per_band + part, total, 0.0), axis=0, keepdims=True
        )
    means = means * (1.0 / (SUB * SUB))
    note_send[...] = means
    lane_s = iota((slots, slots), 1)
    sub_s = iota((slots, slots), 0)
    eye = lane_s == sub_s

    def to_col(row):
        return jnp.sum(jnp.where(eye, jnp.broadcast_to(row, (slots, slots)), 0.0), axis=1, keepdims=True)

    def to_row(col):
        return jnp.sum(jnp.where(eye, jnp.broadcast_to(col, (slots, slots)), 0.0), axis=0, keepdims=True)

    for load in loads[1:6]:
        load.wait()
    tgt_row = panel_ref[...].astype(F32)
    tgt_col = to_col(tgt_row)
    blk_row = block_ref[...].astype(F32)
    blk_col = to_col(blk_row)
    sub_col = to_col(place_ref[...].astype(F32))
    same_tile = tgt_col == tgt_row
    rank_col = jnp.sum(jnp.where(same_tile & (lane_s < sub_s), 1.0, 0.0), axis=1, keepdims=True)
    rank_row = jnp.sum(jnp.where(same_tile & (sub_s < lane_s), 1.0, 0.0), axis=0, keepdims=True)
    blocks = tier_ref.shape[1]
    of_block = blk_col == iota((slots, blocks), 1).astype(F32)
    tier_col = jnp.sum(jnp.where(of_block, tier_ref[...].astype(F32), 0.0), axis=1, keepdims=True)
    sens_col = jnp.sum(jnp.where(of_block, sens_ref[...], 0.0), axis=1, keepdims=True)
    pos_col = tier_col * in_plane + sub_col
    goes = (tgt_row * CAP + rank_row) == iota((tiles * CAP, slots), 0).astype(F32)
    pick = jnp.where(goes, 1.0, 0.0).astype(BF16)
    loads[6].wait()
    loads[7].wait()
    for src, dst in ((dyn, dyn_pick), (leak, leak_pick)):
        for fold in range(FOLDS):
            taken = jnp.dot(pick, src[:, fold * wide : (fold + 1) * wide], preferred_element_type=F32)
            for half in range(halves):
                dst[half, pl.ds(fold, tiles * CAP, stride=FOLDS), :] = taken[
                    :, half * LANES : (half + 1) * LANES
                ]
    for tile in range(tiles):
        for half in range(EARLY):
            at, lanes = slice(tile * rows_of_tile, (tile + 1) * rows_of_tile), slice(half * LANES, (half + 1) * LANES)
            early_send[tile, 0, :, lanes] = dyn_pick[half, at, :].astype(BF16)
            early_send[tile, 1, :, lanes] = leak_pick[half, at, :].astype(BF16)

    beyond = sum(exists.astype(jnp.int32) for exists, _ in across)
    pl.semaphore_wait(barrier, tiles - 1 + beyond)

    each_peer(lambda other: note_copy(other).start())
    keep(note_send, note_recv.at[me], note_rsem)
    each_peer(lambda other: early_copy(other).start())
    keep(early_send.at[me], early_recv.at[me], early_rsem)

    sub8 = iota((2 * tiers, 2 * cols), 0)
    lane8 = mod(iota((2 * tiers, 2 * cols), 1), cols)
    picks = [
        jnp.where(
            ((sub8 == t) & (lane8 == 0)) | ((sub8 == tiers + t) & (lane8 == cols - 1)), 1.0, 0.0
        ).astype(BF16)
        for t in range(tiers)
    ]

    def halo_ends(turn, field, side, lands):
        if side < 2:
            return field.at[0 if side == 0 else tiers - 1], plane_recv.at[turn, lands], 0
        return edge_send.at[turn, (side - 2) // 2], edge_recv.at[turn, lands - 2], 1

    def halo_start(turn, field, exists, where, side):
        @pl.when(exists)
        def _():
            src, dst, kind = halo_ends(turn, field, side, side ^ 1)
            send(src, dst, halo_ssem.at[kind], halo_rsem.at[turn, kind], where)

    def pack_rows(turn, field):
        for end in range(2):
            at = end * (rows - 1)
            for t in range(tiers):
                edge_send[turn, 0, end * tiers + t : end * tiers + t + 1, :] = field[t, at : at + 1, :]

    def columns_of(field):
        columns = jnp.zeros((2 * tiers, rows), F32)
        for t in range(tiers):
            columns = columns + lax.dot_general(
                picks[t], two_parts(field(t), 1), (((1,), (1,)), ((), ())), preferred_element_type=F32
            )
        return columns

    def rows_of(first, last):
        return jnp.concatenate([first(t) for t in range(tiers)] + [last(t) for t in range(tiers)], axis=0)

    def start_halo(turn, field):
        def start(which):
            for exists, where, side in which:
                halo_start(turn, field, exists, where, side)

        pack_rows(turn, field)
        start(sides[2:4])
        start(sides[:2])
        edge_send[turn, 1] = columns_of(lambda t: field[t])
        start(sides[4:])

    def wait_plane(turn):
        bytes_of(plane_recv.at[turn], halo_rsem.at[turn, 0]).wait()

    def wait_halo(turn):
        wait_plane(turn)
        bytes_of(edge_recv.at[turn], halo_rsem.at[turn, 1]).wait()

    row_i = iota((rows, cols), 0)
    col_i = iota((rows, cols), 1)
    sub16 = mod(iota((8 * tiers, tiers * cols), 0), 4 * tiers)
    lane16 = iota((8 * tiers, tiers * cols), 1)
    put = jnp.where(
        ((mod(lane16, cols) == 0) & (sub16 == tiers + div(lane16, cols)))
        | ((mod(lane16, cols) == cols - 1) & (sub16 == 2 * tiers + div(lane16, cols))),
        1.0,
        0.0,
    ).astype(BF16)

    def inside(field, t):
        v = field[t]
        none = jnp.zeros_like(v)
        low = none if t == 0 else field[t - 1]
        high = none if t == tiers - 1 else field[t + 1]
        north = jnp.where(row_i == 0, 0.0, pltpu.roll(v, 1, 0))
        south = jnp.where(row_i == rows - 1, 0.0, pltpu.roll(v, rows - 1, 0))
        west = jnp.where(col_i == 0, 0.0, pltpu.roll(v, 1, 1))
        east = jnp.where(col_i == cols - 1, 0.0, pltpu.roll(v, cols - 1, 1))
        return v, (low, high, north, south, west, east)

    def rims(west, east, t=None):
        ends = jnp.concatenate([west, east], axis=0)
        into = put if t is None else put[:, t * cols : (t + 1) * cols]
        return lax.dot_general(
            two_parts(ends, 0), into, (((0,), (0,)), ((), ())), preferred_element_type=F32
        )

    def apply_inside(field, t):
        v, around = inside(field, t)
        value = diag[t] * v
        for k in range(6):
            if not (k == 0 and t == 0 or k == 1 and t == tiers - 1):
                value = value - faces[k, t] * around[k]
        return value

    def add_beyond(turn):
        rim = rims(edge_recv[turn, 2], edge_recv[turn, 3])
        resid[0] = resid[0] + faces[0, 0] * plane_recv[turn, 0]
        resid[tiers - 1] = resid[tiers - 1] + faces[1, tiers - 1] * plane_recv[turn, 1]
        for t in range(tiers):
            first, last = slice(0, 1), slice(rows - 1, rows)
            resid[t, first, :] = (
                resid[t, first, :] + faces[2, t, first, :] * edge_recv[turn, 0, tiers + t : tiers + t + 1, :]
            )
            resid[t, last, :] = (
                resid[t, last, :] + faces[3, t, last, :] * edge_recv[turn, 1, t : t + 1, :]
            )
            face = jnp.where(col_i == 0, faces[4, t], faces[5, t])
            resid[t] = resid[t] + face * rim[:, t * cols : (t + 1) * cols]

    name_r = iota((named, slots), 0).astype(F32)
    named_row = tgt_row * 8.0 + rank_row
    named_col = tgt_col * 8.0 + rank_col
    by_name = name_r == named_row

    def rename(row):
        return jnp.sum(jnp.where(by_name, row, 0.0), axis=1, keepdims=True)

    pos_r = rename(to_row(pos_col) + 1.0)
    blk_r = rename(blk_row + 1.0)
    sens_r = rename(to_row(sens_col))
    blk_n = jnp.sum(
        jnp.where(named_col == iota((slots, named), 1).astype(F32), blk_col + 1.0, 0.0), axis=0, keepdims=True
    )
    same_block = jnp.where((blk_r == blk_n) & (blk_r > 0.0), 1.0, 0.0)
    block_size = jnp.maximum(jnp.sum(same_block, axis=1, keepdims=True), 1.0)
    same_three = jnp.concatenate([same_block.astype(BF16)] * 3, axis=1)
    at_place = (iota((named, LANES), 1) + 1).astype(F32) == pos_r
    group = div(iota((8, LANES), 1), LANES // CAP) == iota((8, LANES), 0)

    def one_row(block):
        return jnp.sum(jnp.where(group, block, 0.0), axis=0, keepdims=True)

    for tile in range(tiles):
        place_send[tile] = one_row(jnp.broadcast_to(pos_r[tile * 8 : (tile + 1) * 8], (8, LANES)))
    each_peer(lambda other: place_copy(other).start())
    keep(place_send.at[me], place_recv.at[me], place_rsem)

    loads[8].wait()
    start_halo(0, temp)
    start_halo(1, cond)

    bytes_of(note_recv, note_rsem).wait()
    tile_means = jnp.concatenate([jnp.broadcast_to(note_recv[tile], (8, LANES)) for tile in range(tiles)], axis=0)
    at_slots = three_parts(jnp.where(at_place, tile_means, 0.0), 0)
    block_sum = jnp.sum(
        jnp.dot(same_three, at_slots, preferred_element_type=F32), axis=1, keepdims=True
    )
    fac[...] = jnp.broadcast_to(jnp.exp(sens_r * (block_sum / block_size)), (named, LANES))

    upper_rank = iota((8, LANES), 0) >= FOLDS
    for tile in range(tiles):
        fac_send[tile] = one_row(fac[tile * 8 : (tile + 1) * 8, :])
    each_peer(lambda other: fac_copy(other).start())
    keep(fac_send.at[me], fac_recv.at[me], fac_rsem)


    @pl.loop(0, tiles)
    def _(step):
        other = far_first(step)

        def factor_of(rank):
            return fac[pl.ds(other * 8 + rank, 8, stride=0), :]

        by = jnp.concatenate(
            [jnp.where(upper_rank, factor_of(rank + 1), factor_of(rank)) for rank in range(0, CAP, 2)], axis=0
        )
        at = pl.ds(pl.multiple_of(other * rows_of_tile, rows_of_tile), rows_of_tile)
        for half in range(EARLY, halves):
            load_send[other, :, (half - EARLY) * LANES : (half - EARLY + 1) * LANES] = (
                dyn_pick[half, at, :] + by * leak_pick[half, at, :]
            ).astype(BF16)

        @pl.when(other != me)
        def _():
            load_copy(other).start()

    keep(load_send.at[me], load_recv.at[me], load_rsem)
    def missing(exists, blocks):
        @pl.when(jnp.logical_not(exists))
        def _():
            for recv, spare, at, ssem, rsem, none in blocks:
                keep(none, recv.at[at], rsem)
                keep(none, spare.at[at], ssem)

    none8 = nothing.at[:8, :]
    for exists, _, side in sides[:2]:
        missing(
            exists,
            [
                (plane_recv.at[turn], plane_spare.at[turn], side, halo_ssem.at[0], halo_rsem.at[turn, 0], nothing)
                for turn in range(4)
            ]
            + [(face_recv.at[side], face_spare.at[side], k, face_ssem, face_rsem, nothing) for k in range(3)],
        )
    for exists, _, side in sides[2:]:
        missing(
            exists,
            [
                (edge_recv.at[turn], edge_spare.at[turn], side - 2, halo_ssem.at[1], halo_rsem.at[turn, 1], none8)
                for turn in range(2)
            ]
            + [(gain_recv, gain_spare, 3 * (side - 2) + k, gain_ssem, gain_rsem, none8) for k in range(3)],
        )
    for step, _, count, slot in rims_of:
        missing(
            neighbour(*step)[0],
            [(rim_recv, rim_spare, slot + k, rim_ssem, rim_rsem, none8) for k in range(count)],
        )
    loads[9].wait()
    wait_halo(0)
    wait_halo(1)
    rim = rims(edge_recv[1, 2], edge_recv[1, 3])
    for t in range(tiers):
        c, (low, high, north, south, west, east) = inside(cond, t)
        here = rim[:, t * cols : (t + 1) * cols]
        low = plane_recv[1, 0] if t == 0 else low
        high = plane_recv[1, 1] if t == tiers - 1 else high
        north = jnp.where(row_i == 0, edge_recv[1, 0, tiers + t : tiers + t + 1, :], north)
        south = jnp.where(row_i == rows - 1, edge_recv[1, 1, t : t + 1, :], south)
        west = jnp.where(col_i == 0, here, west)
        east = jnp.where(col_i == cols - 1, here, east)
        total = mass[t]
        for k, beside in enumerate((low, high, north, south, west, east)):
            face = 0.5 * (c + beside)
            faces[k, t] = face
            total = total + face
        diag[t] = total
        inv[t] = 1.0 / total
    for t in range(tiers):
        resid[t] = mass[t] * temp[t] - apply_inside(temp, t)
    add_beyond(0)

    middle = (EIG_LOW + EIG_HIGH) / 2.0
    spread = (EIG_HIGH - EIG_LOW) / 2.0
    ratio = middle / spread
    weight_a = 1.0 / ratio
    weight_b = 1.0 / (2.0 * ratio - weight_a)
    weight_c = 1.0 / (2.0 * ratio - weight_b)
    keep_b, push_b = weight_b * weight_a, 2.0 * weight_b / spread
    keep_c, push_c = weight_c * weight_b, 2.0 * weight_c / spread

    for t in range(tiers):
        scaled = push_b * inv[t]
        for k in range(6):
            faces[k, t] = scaled * faces[k, t]

    def layer_face(t):
        if t == 0 and t == tiers - 1:
            raise ValueError("one tier")
        return faces[0, t] if t == 0 else faces[1, t] if t == tiers - 1 else jnp.zeros((rows, cols), F32)

    first, last = slice(0, 1), slice(rows - 1, rows)
    side_face = [jnp.where(col_i == 0, faces[4, t], jnp.where(col_i == cols - 1, faces[5, t], 0.0)) for t in range(tiers)]
    ends_face = [jnp.where(row_i == 0, faces[2, t], jnp.where(row_i == rows - 1, faces[3, t], 0.0)) for t in range(tiers)]
    gain_send[0] = rows_of(lambda t: faces[2, t, first, :], lambda t: faces[3, t, last, :])
    gain_send[1] = rows_of(lambda t: layer_face(t)[first, :], lambda t: layer_face(t)[last, :])
    gain_send[2] = rows_of(lambda t: side_face[t][first, :], lambda t: side_face[t][last, :])
    gain_send[3] = columns_of(lambda t: side_face[t])
    gain_send[4] = columns_of(layer_face)
    gain_send[5] = columns_of(lambda t: ends_face[t])
    for exists, where, side in sides[:2]:
        t = 0 if side == 0 else tiers - 1
        face_send[side, 0] = faces[side, t]
        face_send[side, 1] = ends_face[t]
        face_send[side, 2] = side_face[t]

        @pl.when(exists)
        def _(where=where, side=side):
            send(face_send.at[side], face_recv.at[side ^ 1], face_ssem, face_rsem, where)

    for exists, where, side in sides[2:]:
        lands = (side - 2) ^ 1

        @pl.when(exists)
        def _(where=where, side=side, lands=lands):
            send(
                gain_send.at[0:3] if side < 4 else gain_send.at[3:6],
                gain_recv.at[3 * lands : 3 * lands + 3],
                gain_ssem,
                gain_rsem,
                where,
            )

    sources = tiles * CAP * FOLDS
    sel_i = iota((FOLDS * patches, sources), 0)
    sel_j = iota((FOLDS * patches, sources), 1)
    sel_in = mod(sel_i, patches)
    sel_patch = mod(sel_in, bands) * per_band + div(sel_in, bands)
    fold_hit = div(sel_i, patches) == mod(sel_j, FOLDS)
    bytes_of(place_recv, place_rsem).wait()
    def by_source(ref):
        taken = jnp.concatenate([jnp.broadcast_to(ref[tile], (rows_of_tile, LANES)) for tile in range(tiles)], axis=0)
        rank = div(mod(iota(taken.shape, 0), rows_of_tile), FOLDS)
        return jnp.sum(jnp.where(iota(taken.shape, 1) == rank * (LANES // CAP), taken, 0.0), axis=1, keepdims=True)

    same = iota((sources, sources), 0) == iota((sources, sources), 1)
    code = jnp.sum(jnp.where(same, by_source(place_recv), 0.0), axis=0, keepdims=True)
    picker = jnp.where(fold_hit & (code == (sel_patch + 1).astype(F32)), 1.0, 0.0).astype(BF16)
    left = iota((bands, LANES), 1) < SUB

    def deposit(footprint, begin, end):
        for fold in range(FOLDS):
            for k in range(begin, end):
                lanes = slice((k - begin) * LANES, (k - begin + 1) * LANES)
                a = footprint[fold * patches : fold * patches + bands, lanes]
                b = footprint[fold * patches + bands : fold * patches + 2 * bands, lanes]
                at = 2 * (fold * halves + k)
                power_ref[pl.ds(at, bands, stride=SUB), :] = jnp.where(left, a, pltpu.roll(b, SUB, 1))
                power_ref[pl.ds(at + 1, bands, stride=SUB), :] = jnp.where(left, pltpu.roll(a, SUB, 1), b)

    bytes_of(fac_recv, fac_rsem).wait()
    factors = by_source(fac_recv)
    bytes_of(early_recv, early_rsem).wait()
    for half in range(EARLY):
        lanes = slice(half * LANES, (half + 1) * LANES)
        for tile in range(tiles):
            early_power[tile * rows_of_tile : (tile + 1) * rows_of_tile, lanes] = (
                early_recv[tile, 0, :, lanes].astype(F32)
                + factors[tile * rows_of_tile : (tile + 1) * rows_of_tile] * early_recv[tile, 1, :, lanes].astype(F32)
            ).astype(BF16)
    deposit(jnp.dot(picker, early_power[...], preferred_element_type=F32), 0, EARLY)
    bytes_of(load_recv, load_rsem).wait()
    deposit(
        jnp.dot(picker, load_recv[...].reshape(sources, wide - EARLY * LANES), preferred_element_type=F32), EARLY, halves
    )
    for t in range(tiers):
        r = resid[t] + power_ref[t * rows : (t + 1) * rows, :]
        resid[t] = r
        dirs[0, t] = r * inv[t] * (1.0 / middle)
    start, after = dirs.at[0], dirs.at[1]

    def send_rims(which):
        for step, block, count, _ in which:
            exists, where = neighbour(*step)
            lands = slot_of[tuple(-d for d in step)]

            @pl.when(exists)
            def _(where=where, block=block, count=count, lands=lands):
                send(
                    rim_send.at[block : block + count],
                    rim_recv.at[lands : lands + count],
                    rim_ssem,
                    rim_rsem,
                    where,
                )

    def send_planes(turn, field):
        for exists, where, side in sides[:2]:
            halo_start(turn, field, exists, where, side)

    def around_sum(field, t):
        v, around = inside(field, t)
        value = None
        for k in range(6):
            if not (k == 0 and t == 0 or k == 1 and t == tiers - 1):
                term = faces[k, t] * around[k]
                value = term if value is None else value + term
        return v, value

    own_rows = rows_of(lambda t: start[t, first, :], lambda t: start[t, last, :])
    rim_send[0] = own_rows
    send_rims(rims_of[:8])
    send_planes(2, start)
    stay = keep_b + push_b * (middle - 1.0)
    slab_lane = iota((8, cols), 1)

    def slab_row(t, begin, row, inward, shift):
        slab = slice(begin, begin + 8)
        v = start[t, slab, :]
        value = stay * v + faces[inward, t, slab, :] * pltpu.roll(v, shift, 0)
        value = value + faces[4, t, slab, :] * jnp.where(slab_lane == 0, 0.0, pltpu.roll(v, 1, 1))
        value = value + faces[5, t, slab, :] * jnp.where(slab_lane == cols - 1, 0.0, pltpu.roll(v, cols - 1, 1))
        if t > 0:
            value = value + faces[0, t, slab, :] * start[t - 1, slab, :]
        if t < tiers - 1:
            value = value + faces[1, t, slab, :] * start[t + 1, slab, :]
        return value[row : row + 1, :]

    rim_send[1] = rows_of(lambda t: slab_row(t, 0, 0, 3, 7), lambda t: slab_row(t, rows - 8, 7, 2, 1))
    send_rims(rims_of[12:14])
    own_columns = columns_of(lambda t: start[t])
    rim_send[2] = own_columns
    send_rims(rims_of[8:12])
    for t in range(tiers):
        v, value = around_sum(start, t)
        after[t] = stay * v + value
    send_planes(3, after)
    rim_send[3] = columns_of(lambda t: after[t])
    send_rims(rims_of[14:])
    bytes_of(gain_recv, gain_rsem).wait()
    wait_plane(2)
    wait_plane(3)
    bytes_of(face_recv, face_rsem).wait()
    bytes_of(rim_recv, rim_rsem).wait()

    rim_a = rims(rim_recv[4], rim_recv[6])

    def beyond_rows(ref, t, scale, north, south, rim):
        ref[t, first, :] = ref[t, first, :] + scale * faces[2, t, first, :] * north
        ref[t, last, :] = ref[t, last, :] + scale * faces[3, t, last, :] * south
        face = jnp.where(col_i == 0, faces[4, t], faces[5, t])
        ref[t] = ref[t] + scale * face * rim[:, t * cols : (t + 1) * cols]

    second = resid
    for t in range(tiers):
        value = after[t]
        if t == 0:
            value = value + faces[0, t] * plane_recv[2, 0]
        if t == tiers - 1:
            value = value + faces[1, t] * plane_recv[2, 1]
        second[t] = value
        beyond_rows(
            second, t, 1.0, rim_recv[0, tiers + t : tiers + t + 1, :], rim_recv[2, t : t + 1, :], rim_a
        )

    for side, t in ((0, tiers - 1), (1, 0)):
        plane = plane_recv.at[3, side]
        rim = rims(rim_recv[16 + side], rim_recv[18 + side], t)
        plane[...] = (
            plane[...] + face_recv[side, 0] * start[0 if side == 0 else tiers - 1] + face_recv[side, 2] * rim
        )
        plane[first, :] = (
            plane[first, :] + face_recv[side, 1, first, :] * rim_recv[12 + side, tiers + t : tiers + t + 1, :]
        )
        plane[last, :] = plane[last, :] + face_recv[side, 1, last, :] * rim_recv[14 + side, t : t + 1, :]

    eight_s = iota((2 * tiers, cols), 0)
    eight_l = iota((2 * tiers, cols), 1)
    upper = eight_s >= tiers
    tier_s = mod(eight_s, tiers)

    def pair(a, b):
        return jnp.where(upper, a, b)

    def swap(x):
        return pltpu.roll(x, tiers, 0)

    def layer_part(down, up):
        return jnp.where(
            tier_s == 0, pltpu.roll(down, tiers + 1, 0), jnp.where(tier_s == tiers - 1, pltpu.roll(up, tiers - 1, 0), 0.0)
        )

    north_west, north_east, south_west, south_east = (rim_recv[8 + i] for i in range(4))

    def shell(own, at, layer_at, gain_at, side_part):
        return (
            pair(rim_recv[at + 1], rim_recv[at + 3])
            + pair(gain_recv[gain_at], gain_recv[gain_at + 3]) * swap(own)
            + pair(gain_recv[gain_at + 1], gain_recv[gain_at + 4])
            * layer_part(
                pair(rim_recv[layer_at], rim_recv[layer_at + 2]), pair(rim_recv[layer_at + 1], rim_recv[layer_at + 3])
            )
            + pair(gain_recv[gain_at + 2], gain_recv[gain_at + 5]) * side_part
        )

    row_shell = shell(
        own_rows,
        0,
        12,
        0,
        jnp.where(
            eight_l == 0,
            pltpu.roll(pair(north_west, south_west), 1, 1),
            pltpu.roll(pair(north_east, south_east), cols - 1, 1),
        ),
    )
    col_shell = shell(
        own_columns,
        4,
        16,
        6,
        jnp.where(
            eight_l == 0,
            pair(pltpu.roll(north_west, 1, 1), swap(north_east)),
            pair(swap(south_west), pltpu.roll(south_east, cols - 1, 1)),
        ),
    )
    rim_b = rims(col_shell, col_shell)

    lift = push_c / push_b
    old = 1.0 - lift * keep_b
    now = 1.0 + keep_c + lift - push_c
    for t in range(tiers):
        v, value = around_sum(second, t)
        if t == 0:
            value = value + faces[0, t] * plane_recv[3, 0]
        if t == tiers - 1:
            value = value + faces[1, t] * plane_recv[3, 1]
        out_ref[t] = temp[t] + old * start[t] + now * v + lift * value
        beyond_rows(
            out_ref, t, lift, row_shell[tiers + t : tiers + t + 1, :], row_shell[t : t + 1, :], rim_b
        )
    bytes_of(plane_recv, halo_ssem.at[0]).wait()
    bytes_of(edge_recv, halo_ssem.at[1]).wait()
    bytes_of(rim_recv, rim_ssem).wait()
    bytes_of(gain_recv, gain_ssem).wait()
    bytes_of(face_recv, face_ssem).wait()
    bytes_of(note_recv.at[1:], note_ssem).wait()
    bytes_of(place_recv.at[1:], place_ssem).wait()
    bytes_of(fac_recv.at[1:], fac_ssem).wait()
    bytes_of(early_recv.at[1:], early_ssem).wait()
    bytes_of(load_recv.at[1:], load_ssem).wait()


def hand_over(new, power, new_out, power_out, sem):
    moves = (pltpu.make_async_copy(power, power_out, sem.at[0]), pltpu.make_async_copy(new, new_out, sem.at[1]))
    for move in moves:
        move.start()
    for move in moves:
        move.wait()


def shards(sizes, temp, cond, mass, dyn, leak, panel, place, block, tier, sens):
    tiers, rows, cols = temp.shape
    slots, cells = dyn.shape[1:]
    tiles = sizes[0] * sizes[1]
    any_spec = pl.BlockSpec(memory_space=pl.ANY)
    vmem_spec = pl.BlockSpec(memory_space=pltpu.VMEM)
    grid = (tiers, rows, cols)
    dma = pltpu.SemaphoreType.DMA
    new, power = pl.pallas_call(
        functools.partial(kernel, sizes),
        out_shape=(
            pltpu.VMEM(grid, F32),
            pltpu.VMEM((tiers * rows, cols), F32),
        ),
        in_specs=[any_spec] * 10,
        out_specs=(vmem_spec, vmem_spec),
        scratch_shapes=[
            pltpu.VMEM((1, slots), jnp.int32),
            pltpu.VMEM((1, slots), jnp.int32),
            pltpu.VMEM((1, slots), jnp.int32),
            pltpu.VMEM(tier.shape, jnp.int32),
            pltpu.VMEM(sens.shape, F32),
            pltpu.VMEM(grid, F32),
            pltpu.VMEM(grid, F32),
            pltpu.VMEM(grid, F32),
            pltpu.VMEM((slots, cells), BF16),
            pltpu.VMEM((slots, cells), BF16),
            pltpu.VMEM((cells // FOLDS // LANES, tiles * CAP * FOLDS, LANES), F32),
            pltpu.VMEM((cells // FOLDS // LANES, tiles * CAP * FOLDS, LANES), F32),
            pltpu.VMEM((1, LANES), F32),
            pltpu.VMEM((tiles, 1, LANES), F32),
            pltpu.VMEM((tiles, 1, LANES), F32),
            pltpu.VMEM((tiles, 1, LANES), F32),
            pltpu.VMEM((8 * tiles, LANES), F32),
            pltpu.VMEM((tiles, 1, LANES), F32),
            pltpu.VMEM((tiles, 1, LANES), F32),
            pltpu.VMEM((tiles, 2, CAP * FOLDS, EARLY * LANES), BF16),
            pltpu.VMEM((tiles, 2, CAP * FOLDS, EARLY * LANES), BF16),
            pltpu.VMEM((tiles * CAP * FOLDS, EARLY * LANES), BF16),
            pltpu.VMEM((tiles, CAP * FOLDS, cells // FOLDS - EARLY * LANES), BF16),
            pltpu.VMEM((tiles, CAP * FOLDS, cells // FOLDS - EARLY * LANES), BF16),
            pltpu.VMEM((SWEEPS - 1,) + grid, F32),
            pltpu.VMEM((6,) + grid, F32),
            pltpu.VMEM(grid, F32),
            pltpu.VMEM(grid, F32),
            pltpu.VMEM(grid, F32),
            pltpu.VMEM((2, 2, 2 * tiers, cols), F32),
            pltpu.VMEM((2, 4, 2 * tiers, cols), F32),
            pltpu.VMEM((2, 4, 2 * tiers, cols), F32),
            pltpu.VMEM((4, 2, rows, cols), F32),
            pltpu.VMEM((4, 2, rows, cols), F32),
            pltpu.VMEM((4, 2 * tiers, cols), F32),
            pltpu.VMEM((20, 2 * tiers, cols), F32),
            pltpu.VMEM((20, 2 * tiers, cols), F32),
            pltpu.VMEM((6, 2 * tiers, cols), F32),
            pltpu.VMEM((12, 2 * tiers, cols), F32),
            pltpu.VMEM((12, 2 * tiers, cols), F32),
            pltpu.VMEM((2, 3, rows, cols), F32),
            pltpu.VMEM((2, 3, rows, cols), F32),
            pltpu.VMEM((2, 3, rows, cols), F32),
            pltpu.VMEM((rows, cols), F32),
            dma((10,)),
            dma(()),
            dma(()),
            dma(()),
            dma(()),
            dma(()),
            dma(()),
            dma(()),
            dma(()),
            dma(()),
            dma(()),
            dma((2,)),
            dma((4, 2)),
            dma(()),
            dma(()),
            dma(()),
            dma(()),
            dma(()),
            dma(()),
        ],
        compiler_params=pltpu.CompilerParams(
            collective_id=0, has_side_effects=True, vmem_limit_bytes=VMEM_BYTES
        ),
    )(
        *(
            pltpu.with_memory_space_constraint(given, pltpu.HBM)
            for given in (temp, cond, mass, dyn, leak, panel.reshape(1, slots), place, block, tier, sens)
        )
    )
    return pl.pallas_call(
        hand_over,
        out_shape=(jax.ShapeDtypeStruct(grid, F32),) * 2,
        in_specs=[vmem_spec] * 2,
        out_specs=(any_spec, any_spec),
        scratch_shapes=[dma((2,))],
        compiler_params=pltpu.CompilerParams(vmem_limit_bytes=VMEM_BYTES),
    )(new, power.reshape(grid))


def solution(mesh):
    sizes = (mesh.shape["row"], mesh.shape["col"], mesh.shape["layer"])
    owner = ("row", "col", "layer")
    return jax.shard_map(
        functools.partial(shards, sizes),
        mesh=mesh,
        in_specs=(P("layer", "row", "col"),) * 3
        + (P(owner, None, None),) * 3
        + (P(owner, None),) * 4,
        out_specs=(P("layer", "row", "col"), P("layer", "row", "col")),
        check_vma=False,
    )
```

```python
import functools
import jax
import jax.numpy as jnp
from jax import lax
from jax.experimental import pallas as pl
from jax.experimental.pallas import tpu as pltpu
from jax.sharding import PartitionSpec as P

SUB = 64
SWEEPS = 3
CAP = 4
EIG_LOW = 0.1
EIG_HIGH = 2.0
LANES = 128
FOLDS = 4
EARLY = 1
VMEM_BYTES = 40 << 20

MESH = pl.DeviceIdType.MESH
F32 = jnp.float32
BF16 = jnp.bfloat16


def iota(shape, dim):
    return lax.broadcasted_iota(jnp.int32, shape, dim)


def div(x, n):
    if n & (n - 1):
        return x // n
    return lax.shift_right_logical(x, jnp.int32(n.bit_length() - 1))


def mod(x, n):
    if n & (n - 1):
        return lax.rem(x, n)
    return x & (n - 1)


def three_parts(x, axis):
    head = x.astype(BF16)
    rest = x - head.astype(F32)
    body = rest.astype(BF16)
    return jnp.concatenate([head, body, (rest - body.astype(F32)).astype(BF16)], axis=axis)


def two_parts(x, axis):
    head = x.astype(BF16)
    return jnp.concatenate([head, (x - head.astype(F32)).astype(BF16)], axis=axis)


def kernel(
    sizes,
    temp_hbm,
    cond_hbm,
    mass_hbm,
    dyn_hbm,
    leak_hbm,
    panel_hbm,
    place_hbm,
    block_hbm,
    tier_hbm,
    sens_hbm,
    out_ref,
    power_ref,
    panel_ref,
    place_ref,
    block_ref,
    tier_ref,
    sens_ref,
    temp,
    cond,
    mass,
    dyn,
    leak,
    dyn_pick,
    leak_pick,
    note_send,
    note_recv,
    place_send,
    place_recv,
    fac,
    fac_send,
    fac_recv,
    early_send,
    early_recv,
    early_power,
    load_send,
    load_recv,
    dirs,
    faces,
    diag,
    inv,
    resid,
    column_gain,
    edge_send,
    edge_recv,
    edge_spare,
    plane_recv,
    plane_spare,
    rim_send,
    rim_recv,
    rim_spare,
    gain_send,
    gain_recv,
    gain_spare,
    face_send,
    face_recv,
    face_spare,
    nothing,
    in_sem,
    note_ssem,
    note_rsem,
    place_ssem,
    place_rsem,
    fac_ssem,
    fac_rsem,
    early_ssem,
    early_rsem,
    load_ssem,
    load_rsem,
    halo_ssem,
    halo_rsem,
    rim_ssem,
    rim_rsem,
    gain_ssem,
    gain_rsem,
    face_ssem,
    face_rsem,
):
    n_row, n_col, n_layer = sizes
    tiles = n_row * n_col
    tiers, rows, cols = temp.shape
    slots, cells = dyn.shape
    wide = cells // FOLDS
    halves = wide // LANES
    rows_of_tile = CAP * FOLDS
    named = 8 * tiles
    in_plane = (rows // SUB) * (cols // SUB)
    patches = tiers * in_plane
    bands = tiers * (rows // SUB)
    my_row = lax.axis_index("row")
    my_col = lax.axis_index("col")
    my_layer = lax.axis_index("layer")
    me = my_row * n_col + my_col

    loads = [
        pltpu.make_async_copy(src, dst, in_sem.at[i])
        for i, (src, dst) in enumerate(
            (
                (temp_hbm, temp),
                (panel_hbm, panel_ref),
                (place_hbm, place_ref),
                (block_hbm, block_ref),
                (tier_hbm, tier_ref),
                (sens_hbm, sens_ref),
                (dyn_hbm.at[0], dyn),
                (leak_hbm.at[0], leak),
                (cond_hbm, cond),
                (mass_hbm, mass),
            )
        )
    ]
    for load in loads:
        load.start()

    def far_first(step):
        if n_row & (n_row - 1) or n_col & (n_col - 1) or n_col == 1:
            return lax.rem(me + step, tiles)
        near = n_col // 2
        turn = mod(step, tiles // 2)
        over_row = n_row - 1 - div(turn, near)
        over_col = n_col - 1 - mod(turn, near) - near * div(step, tiles // 2)
        return lax.bitwise_xor(my_row, over_row) * n_col + lax.bitwise_xor(my_col, over_col)

    def each_peer(act):
        @pl.loop(0, tiles)
        def _(step):
            other = far_first(step)
            pl.when(other != me)(lambda: act(other))

    def device(other):
        return {"row": div(other, n_col), "col": mod(other, n_col)}

    sides = (
        (my_layer > 0, {"layer": my_layer - 1}, 0),
        (my_layer < n_layer - 1, {"layer": my_layer + 1}, 1),
        (my_row > 0, {"row": my_row - 1}, 2),
        (my_row < n_row - 1, {"row": my_row + 1}, 3),
        (my_col > 0, {"col": my_col - 1}, 4),
        (my_col < n_col - 1, {"col": my_col + 1}, 5),
    )

    def neighbour(d_row, d_col, d_layer):
        exists, where = [], {}
        for axis, mine, count, d in (
            ("row", my_row, n_row, d_row),
            ("col", my_col, n_col, d_col),
            ("layer", my_layer, n_layer, d_layer),
        ):
            if d:
                exists.append(mine > 0 if d < 0 else mine < count - 1)
                where[axis] = mine + d
        return functools.reduce(jnp.logical_and, exists), where

    rims_of = (
        [((a, b, 0), 0, 1, 8 + i) for i, (a, b) in enumerate(((-1, -1), (-1, 1), (1, -1), (1, 1)))]
        + [((a, 0, c), 0, 1, 12 + i) for i, (a, c) in enumerate(((-1, -1), (-1, 1), (1, -1), (1, 1)))]
        + [((0, b, c), 2, 1, 16 + i) for i, (b, c) in enumerate(((-1, -1), (-1, 1), (1, -1), (1, 1)))]
        + [((-1, 0, 0), 0, 2, 0), ((1, 0, 0), 0, 2, 2), ((0, -1, 0), 2, 2, 4), ((0, 1, 0), 2, 2, 6)]
    )
    slot_of = {step: slot for step, _, _, slot in rims_of}

    nothing[...] = jnp.zeros_like(nothing)
    barrier = pltpu.get_barrier_semaphore()

    each_peer(
        lambda other: pl.semaphore_signal(barrier, inc=1, device_id=device(other), device_id_type=MESH)
    )

    across = [neighbour(*step) for step, _, _, _ in rims_of if step[2]] + [neighbour(0, 0, -1), neighbour(0, 0, 1)]
    for exists, where in across:

        @pl.when(exists)
        def _(where=where):
            pl.semaphore_signal(barrier, inc=1, device_id=where, device_id_type=MESH)

    def remote(src, dst, ssem, rsem, other):
        return pltpu.make_async_remote_copy(
            src_ref=src,
            dst_ref=dst,
            send_sem=ssem,
            recv_sem=rsem,
            device_id=device(other),
            device_id_type=MESH,
        )

    def note_copy(other):
        return remote(note_send, note_recv.at[me], note_ssem, note_rsem, other)

    def place_copy(other):
        return remote(place_send.at[other], place_recv.at[me], place_ssem, place_rsem, other)

    def fac_copy(other):
        return remote(fac_send.at[other], fac_recv.at[me], fac_ssem, fac_rsem, other)

    def early_copy(other):
        return remote(early_send.at[other], early_recv.at[me], early_ssem, early_rsem, other)

    def load_copy(other):
        return remote(load_send.at[other], load_recv.at[me], load_ssem, load_rsem, other)

    def send(src, dst, ssem, rsem, where):
        pltpu.make_async_remote_copy(
            src_ref=src, dst_ref=dst, send_sem=ssem, recv_sem=rsem, device_id=where, device_id_type=MESH
        ).start()

    def bytes_of(ref, sem):
        return pltpu.make_async_copy(ref, ref, sem)

    def keep(src, dst, sem):
        pltpu.make_async_copy(src, dst, sem).start()

    loads[0].wait()
    band_sums = jnp.concatenate(
        [
            jnp.sum(temp[t, b * SUB : (b + 1) * SUB, :], axis=0, keepdims=True)
            for t in range(tiers)
            for b in range(rows // SUB)
        ],
        axis=0,
    )
    lane_b = iota((bands, LANES), 1)
    sub_b = iota((bands, LANES), 0)
    means = jnp.zeros((1, LANES), F32)
    per_band = cols // SUB
    for part in range(per_band):
        total = jnp.sum(jnp.where(div(lane_b, SUB) == part, band_sums, 0.0), axis=1, keepdims=True)
        means = means + jnp.sum(
            jnp.where(lane_b == sub_b * per_band + part, total, 0.0), axis=0, keepdims=True
        )
    means = means * (1.0 / (SUB * SUB))
    note_send[...] = means
    lane_s = iota((slots, slots), 1)
    sub_s = iota((slots, slots), 0)
    eye = lane_s == sub_s

    def to_col(row):
        return jnp.sum(jnp.where(eye, jnp.broadcast_to(row, (slots, slots)), 0.0), axis=1, keepdims=True)

    def to_row(col):
        return jnp.sum(jnp.where(eye, jnp.broadcast_to(col, (slots, slots)), 0.0), axis=0, keepdims=True)

    for load in loads[1:6]:
        load.wait()
    tgt_row = panel_ref[...].astype(F32)
    tgt_col = to_col(tgt_row)
    blk_row = block_ref[...].astype(F32)
    blk_col = to_col(blk_row)
    sub_col = to_col(place_ref[...].astype(F32))
    same_tile = tgt_col == tgt_row
    rank_col = jnp.sum(jnp.where(same_tile & (lane_s < sub_s), 1.0, 0.0), axis=1, keepdims=True)
    rank_row = jnp.sum(jnp.where(same_tile & (sub_s < lane_s), 1.0, 0.0), axis=0, keepdims=True)
    blocks = tier_ref.shape[1]
    of_block = blk_col == iota((slots, blocks), 1).astype(F32)
    tier_col = jnp.sum(jnp.where(of_block, tier_ref[...].astype(F32), 0.0), axis=1, keepdims=True)
    sens_col = jnp.sum(jnp.where(of_block, sens_ref[...], 0.0), axis=1, keepdims=True)
    pos_col = tier_col * in_plane + sub_col
    goes = (tgt_row * CAP + rank_row) == iota((tiles * CAP, slots), 0).astype(F32)
    pick = jnp.where(goes, 1.0, 0.0).astype(BF16)
    loads[6].wait()
    loads[7].wait()
    for src, dst in ((dyn, dyn_pick), (leak, leak_pick)):
        for fold in range(FOLDS):
            taken = jnp.dot(pick, src[:, fold * wide : (fold + 1) * wide], preferred_element_type=F32)
            for half in range(halves):
                dst[half, pl.ds(fold, tiles * CAP, stride=FOLDS), :] = taken[
                    :, half * LANES : (half + 1) * LANES
                ]
    for tile in range(tiles):
        for half in range(EARLY):
            at, lanes = slice(tile * rows_of_tile, (tile + 1) * rows_of_tile), slice(half * LANES, (half + 1) * LANES)
            early_send[tile, 0, :, lanes] = dyn_pick[half, at, :].astype(BF16)
            early_send[tile, 1, :, lanes] = leak_pick[half, at, :].astype(BF16)

    beyond = sum(exists.astype(jnp.int32) for exists, _ in across)
    pl.semaphore_wait(barrier, tiles - 1 + beyond)

    each_peer(lambda other: note_copy(other).start())
    keep(note_send, note_recv.at[me], note_rsem)
    each_peer(lambda other: early_copy(other).start())
    keep(early_send.at[me], early_recv.at[me], early_rsem)

    sub8 = iota((2 * tiers, 2 * cols), 0)
    lane8 = mod(iota((2 * tiers, 2 * cols), 1), cols)
    picks = [
        jnp.where(
            ((sub8 == t) & (lane8 == 0)) | ((sub8 == tiers + t) & (lane8 == cols - 1)), 1.0, 0.0
        ).astype(BF16)
        for t in range(tiers)
    ]

    sub16 = iota((4 * tiers, 2 * cols), 0)
    lane16 = mod(iota((4 * tiers, 2 * cols), 1), cols)
    both_picks = [
        jnp.where(
            ((sub16 == t) & (lane16 == 0))
            | ((sub16 == tiers + t) & (lane16 == cols - 1))
            | ((sub16 == 2 * tiers + t) & (lane16 == 1))
            | ((sub16 == 3 * tiers + t) & (lane16 == cols - 2)),
            1.0,
            0.0,
        ).astype(BF16)
        for t in range(tiers)
    ]

    def halo_ends(turn, field, side, lands):
        if side < 2:
            return field.at[0 if side == 0 else tiers - 1], plane_recv.at[turn, lands], 0
        return edge_send.at[turn, (side - 2) // 2], edge_recv.at[turn, lands - 2], 1

    def halo_start(turn, field, exists, where, side):
        @pl.when(exists)
        def _():
            src, dst, kind = halo_ends(turn, field, side, side ^ 1)
            send(src, dst, halo_ssem.at[kind], halo_rsem.at[turn, kind], where)

    def pack_rows(turn, field):
        for end in range(2):
            at = end * (rows - 1)
            for t in range(tiers):
                edge_send[turn, 0, end * tiers + t : end * tiers + t + 1, :] = field[t, at : at + 1, :]

    def columns_of(field, taking=picks):
        columns = jnp.zeros((taking[0].shape[0], rows), F32)
        for t in range(tiers):
            columns = columns + lax.dot_general(
                taking[t], two_parts(field(t), 1), (((1,), (1,)), ((), ())), preferred_element_type=F32
            )
        return columns

    def rows_of(first, last):
        return jnp.concatenate([first(t) for t in range(tiers)] + [last(t) for t in range(tiers)], axis=0)

    def start_halo(turn, field):
        def start(which):
            for exists, where, side in which:
                halo_start(turn, field, exists, where, side)

        pack_rows(turn, field)
        start(sides[2:4])
        start(sides[:2])
        edge_send[turn, 1] = columns_of(lambda t: field[t])
        start(sides[4:])

    def wait_plane(turn):
        bytes_of(plane_recv.at[turn], halo_rsem.at[turn, 0]).wait()

    def wait_halo(turn):
        wait_plane(turn)
        bytes_of(edge_recv.at[turn], halo_rsem.at[turn, 1]).wait()

    row_i = iota((rows, cols), 0)
    col_i = iota((rows, cols), 1)
    sub16 = mod(iota((8 * tiers, tiers * cols), 0), 4 * tiers)
    lane16 = iota((8 * tiers, tiers * cols), 1)
    put = jnp.where(
        ((mod(lane16, cols) == 0) & (sub16 == tiers + div(lane16, cols)))
        | ((mod(lane16, cols) == cols - 1) & (sub16 == 2 * tiers + div(lane16, cols))),
        1.0,
        0.0,
    ).astype(BF16)

    def inside(field, t):
        v = field[t]
        none = jnp.zeros_like(v)
        low = none if t == 0 else field[t - 1]
        high = none if t == tiers - 1 else field[t + 1]
        north = jnp.where(row_i == 0, 0.0, pltpu.roll(v, 1, 0))
        south = jnp.where(row_i == rows - 1, 0.0, pltpu.roll(v, rows - 1, 0))
        west = jnp.where(col_i == 0, 0.0, pltpu.roll(v, 1, 1))
        east = jnp.where(col_i == cols - 1, 0.0, pltpu.roll(v, cols - 1, 1))
        return v, (low, high, north, south, west, east)

    def rims(west, east, t=None):
        ends = jnp.concatenate([west, east], axis=0)
        into = put if t is None else put[:, t * cols : (t + 1) * cols]
        return lax.dot_general(
            two_parts(ends, 0), into, (((0,), (0,)), ((), ())), preferred_element_type=F32
        )

    def apply_inside(field, t):
        v, around = inside(field, t)
        value = diag[t] * v
        for k in range(6):
            if not (k == 0 and t == 0 or k == 1 and t == tiers - 1):
                value = value - faces[k, t] * around[k]
        return value

    def add_beyond(turn):
        rim = rims(edge_recv[turn, 2], edge_recv[turn, 3])
        resid[0] = resid[0] + faces[0, 0] * plane_recv[turn, 0]
        resid[tiers - 1] = resid[tiers - 1] + faces[1, tiers - 1] * plane_recv[turn, 1]
        for t in range(tiers):
            first, last = slice(0, 1), slice(rows - 1, rows)
            resid[t, first, :] = (
                resid[t, first, :] + faces[2, t, first, :] * edge_recv[turn, 0, tiers + t : tiers + t + 1, :]
            )
            resid[t, last, :] = (
                resid[t, last, :] + faces[3, t, last, :] * edge_recv[turn, 1, t : t + 1, :]
            )
            face = jnp.where(col_i == 0, faces[4, t], faces[5, t])
            resid[t] = resid[t] + face * rim[:, t * cols : (t + 1) * cols]

    name_r = iota((named, slots), 0).astype(F32)
    named_row = tgt_row * 8.0 + rank_row
    named_col = tgt_col * 8.0 + rank_col
    by_name = name_r == named_row

    def rename(row):
        return jnp.sum(jnp.where(by_name, row, 0.0), axis=1, keepdims=True)

    pos_r = rename(to_row(pos_col) + 1.0)
    blk_r = rename(blk_row + 1.0)
    sens_r = rename(to_row(sens_col))
    blk_n = jnp.sum(
        jnp.where(named_col == iota((slots, named), 1).astype(F32), blk_col + 1.0, 0.0), axis=0, keepdims=True
    )
    same_block = jnp.where((blk_r == blk_n) & (blk_r > 0.0), 1.0, 0.0)
    block_size = jnp.maximum(jnp.sum(same_block, axis=1, keepdims=True), 1.0)
    same_three = jnp.concatenate([same_block.astype(BF16)] * 3, axis=1)
    at_place = (iota((named, LANES), 1) + 1).astype(F32) == pos_r
    group = div(iota((8, LANES), 1), LANES // CAP) == iota((8, LANES), 0)

    def one_row(block):
        return jnp.sum(jnp.where(group, block, 0.0), axis=0, keepdims=True)

    for tile in range(tiles):
        place_send[tile] = one_row(jnp.broadcast_to(pos_r[tile * 8 : (tile + 1) * 8], (8, LANES)))
    each_peer(lambda other: place_copy(other).start())
    keep(place_send.at[me], place_recv.at[me], place_rsem)

    loads[8].wait()
    start_halo(0, temp)
    start_halo(1, cond)

    bytes_of(note_recv, note_rsem).wait()
    tile_means = jnp.concatenate([jnp.broadcast_to(note_recv[tile], (8, LANES)) for tile in range(tiles)], axis=0)
    at_slots = three_parts(jnp.where(at_place, tile_means, 0.0), 0)
    block_sum = jnp.sum(
        jnp.dot(same_three, at_slots, preferred_element_type=F32), axis=1, keepdims=True
    )
    fac[...] = jnp.broadcast_to(jnp.exp(sens_r * (block_sum / block_size)), (named, LANES))

    upper_rank = iota((8, LANES), 0) >= FOLDS
    def load_step(step):
        other = far_first(step)

        def factor_of(rank):
            return fac[pl.ds(other * 8 + rank, 8, stride=0), :]

        by = jnp.concatenate(
            [jnp.where(upper_rank, factor_of(rank + 1), factor_of(rank)) for rank in range(0, CAP, 2)], axis=0
        )
        at = pl.ds(pl.multiple_of(other * rows_of_tile, rows_of_tile), rows_of_tile)
        for half in range(EARLY, halves):
            load_send[other, :, (half - EARLY) * LANES : (half - EARLY + 1) * LANES] = (
                dyn_pick[half, at, :] + by * leak_pick[half, at, :]
            ).astype(BF16)

        @pl.when(other != me)
        def _():
            load_copy(other).start()

    pl.loop(0, tiles // 8)(load_step)
    for tile in range(tiles):
        fac_send[tile] = one_row(fac[tile * 8 : (tile + 1) * 8, :])
    each_peer(lambda other: fac_copy(other).start())
    keep(fac_send.at[me], fac_recv.at[me], fac_rsem)
    pl.loop(tiles // 8, tiles)(load_step)
    keep(load_send.at[me], load_recv.at[me], load_rsem)
    def missing(exists, blocks):
        @pl.when(jnp.logical_not(exists))
        def _():
            for recv, spare, at, ssem, rsem, none in blocks:
                keep(none, recv.at[at], rsem)
                keep(none, spare.at[at], ssem)

    none8 = nothing.at[:8, :]
    for exists, _, side in sides[:2]:
        missing(
            exists,
            [
                (plane_recv.at[turn], plane_spare.at[turn], side, halo_ssem.at[0], halo_rsem.at[turn, 0], nothing)
                for turn in range(4)
            ]
            + [(face_recv.at[side], face_spare.at[side], k, face_ssem, face_rsem, nothing) for k in range(3)],
        )
    for exists, _, side in sides[2:]:
        missing(
            exists,
            [
                (edge_recv.at[turn], edge_spare.at[turn], side - 2, halo_ssem.at[1], halo_rsem.at[turn, 1], none8)
                for turn in range(2)
            ]
            + [(gain_recv, gain_spare, 3 * (side - 2) + k, gain_ssem, gain_rsem, none8) for k in range(3)],
        )
    for step, _, count, slot in rims_of:
        missing(
            neighbour(*step)[0],
            [(rim_recv, rim_spare, slot + k, rim_ssem, rim_rsem, none8) for k in range(count)],
        )
    loads[9].wait()
    wait_halo(0)
    wait_halo(1)
    rim = rims(edge_recv[1, 2], edge_recv[1, 3])
    for t in range(tiers):
        c, (low, high, north, south, west, east) = inside(cond, t)
        here = rim[:, t * cols : (t + 1) * cols]
        low = plane_recv[1, 0] if t == 0 else low
        high = plane_recv[1, 1] if t == tiers - 1 else high
        north = jnp.where(row_i == 0, edge_recv[1, 0, tiers + t : tiers + t + 1, :], north)
        south = jnp.where(row_i == rows - 1, edge_recv[1, 1, t : t + 1, :], south)
        west = jnp.where(col_i == 0, here, west)
        east = jnp.where(col_i == cols - 1, here, east)
        total = mass[t]
        for k, beside in enumerate((low, high, north, south, west, east)):
            face = 0.5 * (c + beside)
            faces[k, t] = face
            total = total + face
        diag[t] = total
        inv[t] = 1.0 / total
    for t in range(tiers):
        resid[t] = mass[t] * temp[t] - apply_inside(temp, t)
    add_beyond(0)

    middle = (EIG_LOW + EIG_HIGH) / 2.0
    spread = (EIG_HIGH - EIG_LOW) / 2.0
    ratio = middle / spread
    weight_a = 1.0 / ratio
    weight_b = 1.0 / (2.0 * ratio - weight_a)
    weight_c = 1.0 / (2.0 * ratio - weight_b)
    keep_b, push_b = weight_b * weight_a, 2.0 * weight_b / spread
    keep_c, push_c = weight_c * weight_b, 2.0 * weight_c / spread

    for t in range(tiers):
        scaled = push_b * inv[t]
        for k in range(6):
            faces[k, t] = scaled * faces[k, t]
        inv[t] = inv[t] * (1.0 / middle)

    def layer_face(t):
        if t == 0 and t == tiers - 1:
            raise ValueError("one tier")
        return faces[0, t] if t == 0 else faces[1, t] if t == tiers - 1 else jnp.zeros((rows, cols), F32)

    first, last = slice(0, 1), slice(rows - 1, rows)
    side_face = [jnp.where(col_i == 0, faces[4, t], jnp.where(col_i == cols - 1, faces[5, t], 0.0)) for t in range(tiers)]
    ends_face = [jnp.where(row_i == 0, faces[2, t], jnp.where(row_i == rows - 1, faces[3, t], 0.0)) for t in range(tiers)]
    gain_send[0] = rows_of(lambda t: faces[2, t, first, :], lambda t: faces[3, t, last, :])
    gain_send[1] = rows_of(lambda t: layer_face(t)[first, :], lambda t: layer_face(t)[last, :])
    gain_send[2] = rows_of(lambda t: side_face[t][first, :], lambda t: side_face[t][last, :])
    gain_send[3] = columns_of(lambda t: side_face[t])
    gain_send[4] = columns_of(layer_face)
    gain_send[5] = columns_of(lambda t: ends_face[t])
    blank = jnp.zeros((rows, cols), F32)
    column_gain[0] = columns_of(lambda t: jnp.where(col_i == 0, faces[5, t], faces[4, t]))
    column_gain[1] = columns_of(lambda t: jnp.where(row_i == 0, 0.0, faces[2, t]))
    column_gain[2] = columns_of(lambda t: jnp.where(row_i == rows - 1, 0.0, faces[3, t]))
    column_gain[3] = columns_of(lambda t: faces[0, t] if t > 0 else blank)
    column_gain[4] = columns_of(lambda t: faces[1, t] if t < tiers - 1 else blank)
    for exists, where, side in sides[:2]:
        t = 0 if side == 0 else tiers - 1
        face_send[side, 0] = faces[side, t]
        face_send[side, 1] = ends_face[t]
        face_send[side, 2] = side_face[t]

        @pl.when(exists)
        def _(where=where, side=side):
            send(face_send.at[side], face_recv.at[side ^ 1], face_ssem, face_rsem, where)

    for exists, where, side in sides[2:]:
        lands = (side - 2) ^ 1

        @pl.when(exists)
        def _(where=where, side=side, lands=lands):
            send(
                gain_send.at[0:3] if side < 4 else gain_send.at[3:6],
                gain_recv.at[3 * lands : 3 * lands + 3],
                gain_ssem,
                gain_rsem,
                where,
            )

    sources = tiles * CAP * FOLDS
    sel_i = iota((FOLDS * patches, sources), 0)
    sel_j = iota((FOLDS * patches, sources), 1)
    sel_in = mod(sel_i, patches)
    sel_patch = mod(sel_in, bands) * per_band + div(sel_in, bands)
    fold_hit = div(sel_i, patches) == mod(sel_j, FOLDS)
    bytes_of(place_recv, place_rsem).wait()
    def by_source(ref):
        taken = jnp.concatenate([jnp.broadcast_to(ref[tile], (rows_of_tile, LANES)) for tile in range(tiles)], axis=0)
        rank = div(mod(iota(taken.shape, 0), rows_of_tile), FOLDS)
        return jnp.sum(jnp.where(iota(taken.shape, 1) == rank * (LANES // CAP), taken, 0.0), axis=1, keepdims=True)

    same = iota((sources, sources), 0) == iota((sources, sources), 1)
    code = jnp.sum(jnp.where(same, by_source(place_recv), 0.0), axis=0, keepdims=True)
    picker = jnp.where(fold_hit & (code == (sel_patch + 1).astype(F32)), 1.0, 0.0).astype(BF16)
    left = iota((bands, LANES), 1) < SUB

    def deposit(footprint, begin, end):
        for fold in range(FOLDS):
            for k in range(begin, end):
                lanes = slice((k - begin) * LANES, (k - begin + 1) * LANES)
                a = footprint[fold * patches : fold * patches + bands, lanes]
                b = footprint[fold * patches + bands : fold * patches + 2 * bands, lanes]
                at = 2 * (fold * halves + k)
                power_ref[pl.ds(at, bands, stride=SUB), :] = jnp.where(left, a, pltpu.roll(b, SUB, 1))
                power_ref[pl.ds(at + 1, bands, stride=SUB), :] = jnp.where(left, pltpu.roll(a, SUB, 1), b)

    bytes_of(fac_recv, fac_rsem).wait()
    factors = by_source(fac_recv)
    bytes_of(early_recv, early_rsem).wait()
    for half in range(EARLY):
        lanes = slice(half * LANES, (half + 1) * LANES)
        for tile in range(tiles):
            early_power[tile * rows_of_tile : (tile + 1) * rows_of_tile, lanes] = (
                early_recv[tile, 0, :, lanes].astype(F32)
                + factors[tile * rows_of_tile : (tile + 1) * rows_of_tile] * early_recv[tile, 1, :, lanes].astype(F32)
            ).astype(BF16)
    deposit(jnp.dot(picker, early_power[...], preferred_element_type=F32), 0, EARLY)
    bytes_of(load_recv, load_rsem).wait()
    deposit(
        jnp.dot(picker, load_recv[...].reshape(sources, wide - EARLY * LANES), preferred_element_type=F32), EARLY, halves
    )
    start, after = dirs.at[0], dirs.at[1]

    def begin_rows(t, begin, end):
        power_rows = power_ref[t * rows + begin : t * rows + end, :]
        start[t, begin:end, :] = (resid[t, begin:end, :] + power_rows) * inv[t, begin:end, :]

    for t in range(tiers):
        begin_rows(t, 0, 8)
        begin_rows(t, rows - 8, rows)

    def send_rims(which):
        for step, block, count, _ in which:
            exists, where = neighbour(*step)
            lands = slot_of[tuple(-d for d in step)]

            @pl.when(exists)
            def _(where=where, block=block, count=count, lands=lands):
                send(
                    rim_send.at[block : block + count],
                    rim_recv.at[lands : lands + count],
                    rim_ssem,
                    rim_rsem,
                    where,
                )

    def send_planes(turn, field):
        for exists, where, side in sides[:2]:
            halo_start(turn, field, exists, where, side)

    def around_sum(field, t):
        v, around = inside(field, t)
        value = None
        for k in range(6):
            if not (k == 0 and t == 0 or k == 1 and t == tiers - 1):
                term = faces[k, t] * around[k]
                value = term if value is None else value + term
        return v, value

    own_rows = rows_of(lambda t: start[t, first, :], lambda t: start[t, last, :])
    rim_send[0] = own_rows
    send_rims(rims_of[:8])
    stay = keep_b + push_b * (middle - 1.0)
    slab_lane = iota((8, cols), 1)

    def slab_row(t, begin, row, inward, shift):
        slab = slice(begin, begin + 8)
        v = start[t, slab, :]
        value = stay * v + faces[inward, t, slab, :] * pltpu.roll(v, shift, 0)
        value = value + faces[4, t, slab, :] * jnp.where(slab_lane == 0, 0.0, pltpu.roll(v, 1, 1))
        value = value + faces[5, t, slab, :] * jnp.where(slab_lane == cols - 1, 0.0, pltpu.roll(v, cols - 1, 1))
        if t > 0:
            value = value + faces[0, t, slab, :] * start[t - 1, slab, :]
        if t < tiers - 1:
            value = value + faces[1, t, slab, :] * start[t + 1, slab, :]
        return value[row : row + 1, :]

    rim_send[1] = rows_of(lambda t: slab_row(t, 0, 0, 3, 7), lambda t: slab_row(t, rows - 8, 7, 2, 1))
    send_rims(rims_of[12:14])
    for t in range(tiers):
        begin_rows(t, 8, rows - 8)
    send_planes(2, start)
    columns = columns_of(lambda t: start[t], both_picks)
    own_columns = columns[: 2 * tiers]
    rim_send[2] = own_columns
    rim_send[3] = (
        stay * own_columns
        + column_gain[0] * columns[2 * tiers :]
        + column_gain[1] * pltpu.roll(own_columns, 1, 1)
        + column_gain[2] * pltpu.roll(own_columns, rows - 1, 1)
        + column_gain[3] * pltpu.roll(own_columns, 1, 0)
        + column_gain[4] * pltpu.roll(own_columns, 2 * tiers - 1, 0)
    )
    send_rims(rims_of[14:])
    send_rims(rims_of[8:12])
    for t in range(tiers):
        v, value = around_sum(start, t)
        after[t] = stay * v + value
    send_planes(3, after)
    bytes_of(gain_recv, gain_rsem).wait()
    wait_plane(2)
    wait_plane(3)
    bytes_of(face_recv, face_rsem).wait()
    bytes_of(rim_recv, rim_rsem).wait()

    rim_a = rims(rim_recv[4], rim_recv[6])

    def beyond_rows(ref, t, scale, north, south, rim):
        ref[t, first, :] = ref[t, first, :] + scale * faces[2, t, first, :] * north
        ref[t, last, :] = ref[t, last, :] + scale * faces[3, t, last, :] * south
        face = jnp.where(col_i == 0, faces[4, t], faces[5, t])
        ref[t] = ref[t] + scale * face * rim[:, t * cols : (t + 1) * cols]

    second = resid
    for t in range(tiers):
        value = after[t]
        if t == 0:
            value = value + faces[0, t] * plane_recv[2, 0]
        if t == tiers - 1:
            value = value + faces[1, t] * plane_recv[2, 1]
        second[t] = value
        beyond_rows(
            second, t, 1.0, rim_recv[0, tiers + t : tiers + t + 1, :], rim_recv[2, t : t + 1, :], rim_a
        )

    for side, t in ((0, tiers - 1), (1, 0)):
        plane = plane_recv.at[3, side]
        rim = rims(rim_recv[16 + side], rim_recv[18 + side], t)
        plane[...] = (
            plane[...] + face_recv[side, 0] * start[0 if side == 0 else tiers - 1] + face_recv[side, 2] * rim
        )
        plane[first, :] = (
            plane[first, :] + face_recv[side, 1, first, :] * rim_recv[12 + side, tiers + t : tiers + t + 1, :]
        )
        plane[last, :] = plane[last, :] + face_recv[side, 1, last, :] * rim_recv[14 + side, t : t + 1, :]

    eight_s = iota((2 * tiers, cols), 0)
    eight_l = iota((2 * tiers, cols), 1)
    upper = eight_s >= tiers
    tier_s = mod(eight_s, tiers)

    def pair(a, b):
        return jnp.where(upper, a, b)

    def swap(x):
        return pltpu.roll(x, tiers, 0)

    def layer_part(down, up):
        return jnp.where(
            tier_s == 0, pltpu.roll(down, tiers + 1, 0), jnp.where(tier_s == tiers - 1, pltpu.roll(up, tiers - 1, 0), 0.0)
        )

    north_west, north_east, south_west, south_east = (rim_recv[8 + i] for i in range(4))

    def shell(own, at, layer_at, gain_at, side_part):
        return (
            pair(rim_recv[at + 1], rim_recv[at + 3])
            + pair(gain_recv[gain_at], gain_recv[gain_at + 3]) * swap(own)
            + pair(gain_recv[gain_at + 1], gain_recv[gain_at + 4])
            * layer_part(
                pair(rim_recv[layer_at], rim_recv[layer_at + 2]), pair(rim_recv[layer_at + 1], rim_recv[layer_at + 3])
            )
            + pair(gain_recv[gain_at + 2], gain_recv[gain_at + 5]) * side_part
        )

    row_shell = shell(
        own_rows,
        0,
        12,
        0,
        jnp.where(
            eight_l == 0,
            pltpu.roll(pair(north_west, south_west), 1, 1),
            pltpu.roll(pair(north_east, south_east), cols - 1, 1),
        ),
    )
    col_shell = shell(
        own_columns,
        4,
        16,
        6,
        jnp.where(
            eight_l == 0,
            pair(pltpu.roll(north_west, 1, 1), swap(north_east)),
            pair(swap(south_west), pltpu.roll(south_east, cols - 1, 1)),
        ),
    )
    rim_b = rims(col_shell, col_shell)

    lift = push_c / push_b
    old = 1.0 - lift * keep_b
    now = 1.0 + keep_c + lift - push_c
    for t in range(tiers):
        v, value = around_sum(second, t)
        if t == 0:
            value = value + faces[0, t] * plane_recv[3, 0]
        if t == tiers - 1:
            value = value + faces[1, t] * plane_recv[3, 1]
        out_ref[t] = temp[t] + old * start[t] + now * v + lift * value
        beyond_rows(
            out_ref, t, lift, row_shell[tiers + t : tiers + t + 1, :], row_shell[t : t + 1, :], rim_b
        )
    bytes_of(plane_recv, halo_ssem.at[0]).wait()
    bytes_of(edge_recv, halo_ssem.at[1]).wait()
    bytes_of(rim_recv, rim_ssem).wait()
    bytes_of(gain_recv, gain_ssem).wait()
    bytes_of(face_recv, face_ssem).wait()
    bytes_of(note_recv.at[1:], note_ssem).wait()
    bytes_of(place_recv.at[1:], place_ssem).wait()
    bytes_of(fac_recv.at[1:], fac_ssem).wait()
    bytes_of(early_recv.at[1:], early_ssem).wait()
    bytes_of(load_recv.at[1:], load_ssem).wait()


def hand_over(new, power, new_out, power_out, sem):
    moves = (pltpu.make_async_copy(power, power_out, sem.at[0]), pltpu.make_async_copy(new, new_out, sem.at[1]))
    for move in moves:
        move.start()
    for move in moves:
        move.wait()


def shards(sizes, temp, cond, mass, dyn, leak, panel, place, block, tier, sens):
    tiers, rows, cols = temp.shape
    slots, cells = dyn.shape[1:]
    tiles = sizes[0] * sizes[1]
    any_spec = pl.BlockSpec(memory_space=pl.ANY)
    vmem_spec = pl.BlockSpec(memory_space=pltpu.VMEM)
    grid = (tiers, rows, cols)
    dma = pltpu.SemaphoreType.DMA
    new, power = pl.pallas_call(
        functools.partial(kernel, sizes),
        out_shape=(
            pltpu.VMEM(grid, F32),
            pltpu.VMEM((tiers * rows, cols), F32),
        ),
        in_specs=[any_spec] * 10,
        out_specs=(vmem_spec, vmem_spec),
        scratch_shapes=[
            pltpu.VMEM((1, slots), jnp.int32),
            pltpu.VMEM((1, slots), jnp.int32),
            pltpu.VMEM((1, slots), jnp.int32),
            pltpu.VMEM(tier.shape, jnp.int32),
            pltpu.VMEM(sens.shape, F32),
            pltpu.VMEM(grid, F32),
            pltpu.VMEM(grid, F32),
            pltpu.VMEM(grid, F32),
            pltpu.VMEM((slots, cells), BF16),
            pltpu.VMEM((slots, cells), BF16),
            pltpu.VMEM((cells // FOLDS // LANES, tiles * CAP * FOLDS, LANES), F32),
            pltpu.VMEM((cells // FOLDS // LANES, tiles * CAP * FOLDS, LANES), F32),
            pltpu.VMEM((1, LANES), F32),
            pltpu.VMEM((tiles, 1, LANES), F32),
            pltpu.VMEM((tiles, 1, LANES), F32),
            pltpu.VMEM((tiles, 1, LANES), F32),
            pltpu.VMEM((8 * tiles, LANES), F32),
            pltpu.VMEM((tiles, 1, LANES), F32),
            pltpu.VMEM((tiles, 1, LANES), F32),
            pltpu.VMEM((tiles, 2, CAP * FOLDS, EARLY * LANES), BF16),
            pltpu.VMEM((tiles, 2, CAP * FOLDS, EARLY * LANES), BF16),
            pltpu.VMEM((tiles * CAP * FOLDS, EARLY * LANES), BF16),
            pltpu.VMEM((tiles, CAP * FOLDS, cells // FOLDS - EARLY * LANES), BF16),
            pltpu.VMEM((tiles, CAP * FOLDS, cells // FOLDS - EARLY * LANES), BF16),
            pltpu.VMEM((SWEEPS - 1,) + grid, F32),
            pltpu.VMEM((6,) + grid, F32),
            pltpu.VMEM(grid, F32),
            pltpu.VMEM(grid, F32),
            pltpu.VMEM(grid, F32),
            pltpu.VMEM((5, 2 * tiers, cols), F32),
            pltpu.VMEM((2, 2, 2 * tiers, cols), F32),
            pltpu.VMEM((2, 4, 2 * tiers, cols), F32),
            pltpu.VMEM((2, 4, 2 * tiers, cols), F32),
            pltpu.VMEM((4, 2, rows, cols), F32),
            pltpu.VMEM((4, 2, rows, cols), F32),
            pltpu.VMEM((4, 2 * tiers, cols), F32),
            pltpu.VMEM((20, 2 * tiers, cols), F32),
            pltpu.VMEM((20, 2 * tiers, cols), F32),
            pltpu.VMEM((6, 2 * tiers, cols), F32),
            pltpu.VMEM((12, 2 * tiers, cols), F32),
            pltpu.VMEM((12, 2 * tiers, cols), F32),
            pltpu.VMEM((2, 3, rows, cols), F32),
            pltpu.VMEM((2, 3, rows, cols), F32),
            pltpu.VMEM((2, 3, rows, cols), F32),
            pltpu.VMEM((rows, cols), F32),
            dma((10,)),
            dma(()),
            dma(()),
            dma(()),
            dma(()),
            dma(()),
            dma(()),
            dma(()),
            dma(()),
            dma(()),
            dma(()),
            dma((2,)),
            dma((4, 2)),
            dma(()),
            dma(()),
            dma(()),
            dma(()),
            dma(()),
            dma(()),
        ],
        compiler_params=pltpu.CompilerParams(
            collective_id=0, has_side_effects=True, vmem_limit_bytes=VMEM_BYTES
        ),
    )(
        *(
            pltpu.with_memory_space_constraint(given, pltpu.HBM)
            for given in (temp, cond, mass, dyn, leak, panel.reshape(1, slots), place, block, tier, sens)
        )
    )
    return pl.pallas_call(
        hand_over,
        out_shape=(jax.ShapeDtypeStruct(grid, F32),) * 2,
        in_specs=[vmem_spec] * 2,
        out_specs=(any_spec, any_spec),
        scratch_shapes=[dma((2,))],
        compiler_params=pltpu.CompilerParams(vmem_limit_bytes=VMEM_BYTES),
    )(new, power.reshape(grid))


def solution(mesh):
    sizes = (mesh.shape["row"], mesh.shape["col"], mesh.shape["layer"])
    owner = ("row", "col", "layer")
    return jax.shard_map(
        functools.partial(shards, sizes),
        mesh=mesh,
        in_specs=(P("layer", "row", "col"),) * 3
        + (P(owner, None, None),) * 3
        + (P(owner, None),) * 4,
        out_specs=(P("layer", "row", "col"), P("layer", "row", "col")),
        check_vma=False,
    )
```

```python
import functools
import jax
import jax.numpy as jnp
from jax import lax
from jax.experimental import pallas as pl
from jax.experimental.pallas import tpu as pltpu
from jax.sharding import PartitionSpec as P

SUB = 64
SWEEPS = 3
CAP = 4
EIG_LOW = 0.1
EIG_HIGH = 2.0
LANES = 128
FOLDS = 4
EARLY = 1
VMEM_BYTES = 40 << 20

MESH = pl.DeviceIdType.MESH
F32 = jnp.float32
BF16 = jnp.bfloat16


def iota(shape, dim):
    return lax.broadcasted_iota(jnp.int32, shape, dim)


def div(x, n):
    if n & (n - 1):
        return x // n
    return lax.shift_right_logical(x, jnp.int32(n.bit_length() - 1))


def mod(x, n):
    if n & (n - 1):
        return lax.rem(x, n)
    return x & (n - 1)


def three_parts(x, axis):
    head = x.astype(BF16)
    rest = x - head.astype(F32)
    body = rest.astype(BF16)
    return jnp.concatenate([head, body, (rest - body.astype(F32)).astype(BF16)], axis=axis)


def two_parts(x, axis):
    head = x.astype(BF16)
    return jnp.concatenate([head, (x - head.astype(F32)).astype(BF16)], axis=axis)


def kernel(
    sizes,
    temp_hbm,
    cond_hbm,
    mass_hbm,
    dyn_hbm,
    leak_hbm,
    panel_hbm,
    place_hbm,
    block_hbm,
    tier_hbm,
    sens_hbm,
    out_ref,
    power_ref,
    panel_ref,
    place_ref,
    block_ref,
    tier_ref,
    sens_ref,
    temp,
    cond,
    mass,
    dyn,
    leak,
    dyn_pick,
    leak_pick,
    note_send,
    note_recv,
    place_send,
    place_recv,
    fac,
    fac_send,
    fac_recv,
    early_send,
    early_recv,
    early_power,
    load_send,
    load_recv,
    dirs,
    faces,
    diag,
    inv,
    resid,
    column_gain,
    edge_send,
    edge_recv,
    edge_spare,
    plane_recv,
    plane_spare,
    rim_send,
    rim_recv,
    rim_spare,
    gain_send,
    gain_recv,
    gain_spare,
    face_send,
    face_recv,
    face_spare,
    nothing,
    in_sem,
    note_ssem,
    note_rsem,
    place_ssem,
    place_rsem,
    fac_ssem,
    fac_rsem,
    early_ssem,
    early_rsem,
    load_ssem,
    load_rsem,
    halo_ssem,
    halo_rsem,
    rim_ssem,
    rim_rsem,
    gain_ssem,
    gain_rsem,
    face_ssem,
    face_rsem,
):
    n_row, n_col, n_layer = sizes
    tiles = n_row * n_col
    tiers, rows, cols = temp.shape
    slots, cells = dyn.shape
    wide = cells // FOLDS
    halves = wide // LANES
    rows_of_tile = CAP * FOLDS
    named = 8 * tiles
    in_plane = (rows // SUB) * (cols // SUB)
    patches = tiers * in_plane
    bands = tiers * (rows // SUB)
    my_row = lax.axis_index("row")
    my_col = lax.axis_index("col")
    my_layer = lax.axis_index("layer")
    me = my_row * n_col + my_col

    loads = [
        pltpu.make_async_copy(src, dst, in_sem.at[i])
        for i, (src, dst) in enumerate(
            (
                (temp_hbm, temp),
                (panel_hbm, panel_ref),
                (place_hbm, place_ref),
                (block_hbm, block_ref),
                (tier_hbm, tier_ref),
                (sens_hbm, sens_ref),
                (dyn_hbm.at[0], dyn),
                (leak_hbm.at[0], leak),
                (cond_hbm, cond),
                (mass_hbm, mass),
            )
        )
    ]
    for load in loads:
        load.start()

    def far_first(step):
        if n_row & (n_row - 1) or n_col & (n_col - 1) or n_col == 1:
            return lax.rem(me + step, tiles)
        near = n_col // 2
        turn = mod(step, tiles // 2)
        over_row = n_row - 1 - div(turn, near)
        over_col = n_col - 1 - mod(turn, near) - near * div(step, tiles // 2)
        return lax.bitwise_xor(my_row, over_row) * n_col + lax.bitwise_xor(my_col, over_col)

    def low_first(step):
        if n_row & (n_row - 1) or n_col & (n_col - 1) or n_row == 1 or n_col == 1:
            return lax.rem(me + step, tiles)
        near = n_col // 2
        group, turn = div(step, tiles // 2), mod(step, tiles // 2)
        over, turn = div(turn, tiles // 4), mod(turn, tiles // 4)
        over_row = n_row // 2 - 1 - div(turn, near)
        over_col = n_col - 1 - mod(turn, near) - near * over
        row = group * (n_row // 2) + lax.bitwise_xor(mod(my_row, n_row // 2), over_row)
        return row * n_col + lax.bitwise_xor(my_col, over_col)

    def each_peer(act, order=far_first):
        @pl.loop(0, tiles)
        def _(step):
            other = order(step)
            pl.when(other != me)(lambda: act(other))

    def device(other):
        return {"row": div(other, n_col), "col": mod(other, n_col)}

    sides = (
        (my_layer > 0, {"layer": my_layer - 1}, 0),
        (my_layer < n_layer - 1, {"layer": my_layer + 1}, 1),
        (my_row > 0, {"row": my_row - 1}, 2),
        (my_row < n_row - 1, {"row": my_row + 1}, 3),
        (my_col > 0, {"col": my_col - 1}, 4),
        (my_col < n_col - 1, {"col": my_col + 1}, 5),
    )

    def neighbour(d_row, d_col, d_layer):
        exists, where = [], {}
        for axis, mine, count, d in (
            ("row", my_row, n_row, d_row),
            ("col", my_col, n_col, d_col),
            ("layer", my_layer, n_layer, d_layer),
        ):
            if d:
                exists.append(mine > 0 if d < 0 else mine < count - 1)
                where[axis] = mine + d
        return functools.reduce(jnp.logical_and, exists), where

    rims_of = (
        [((a, b, 0), 0, 1, 8 + i) for i, (a, b) in enumerate(((-1, -1), (-1, 1), (1, -1), (1, 1)))]
        + [((a, 0, c), 0, 1, 12 + i) for i, (a, c) in enumerate(((-1, -1), (-1, 1), (1, -1), (1, 1)))]
        + [((0, b, c), 2, 1, 16 + i) for i, (b, c) in enumerate(((-1, -1), (-1, 1), (1, -1), (1, 1)))]
        + [((-1, 0, 0), 0, 2, 0), ((1, 0, 0), 0, 2, 2), ((0, -1, 0), 2, 2, 4), ((0, 1, 0), 2, 2, 6)]
    )
    slot_of = {step: slot for step, _, _, slot in rims_of}

    nothing[...] = jnp.zeros_like(nothing)
    barrier = pltpu.get_barrier_semaphore()

    each_peer(
        lambda other: pl.semaphore_signal(barrier, inc=1, device_id=device(other), device_id_type=MESH)
    )

    across = [neighbour(*step) for step, _, _, _ in rims_of if step[2]] + [neighbour(0, 0, -1), neighbour(0, 0, 1)]
    for exists, where in across:

        @pl.when(exists)
        def _(where=where):
            pl.semaphore_signal(barrier, inc=1, device_id=where, device_id_type=MESH)

    def remote(src, dst, ssem, rsem, other):
        return pltpu.make_async_remote_copy(
            src_ref=src,
            dst_ref=dst,
            send_sem=ssem,
            recv_sem=rsem,
            device_id=device(other),
            device_id_type=MESH,
        )

    def note_copy(other):
        return remote(note_send, note_recv.at[me], note_ssem, note_rsem, other)

    def place_copy(other):
        return remote(place_send.at[other], place_recv.at[me], place_ssem, place_rsem, other)

    def fac_copy(other):
        return remote(fac_send.at[other], fac_recv.at[me], fac_ssem, fac_rsem, other)

    def early_copy(other):
        return remote(early_send.at[other], early_recv.at[me], early_ssem, early_rsem, other)

    def load_copy(other):
        return remote(load_send.at[other], load_recv.at[me], load_ssem, load_rsem, other)

    def send(src, dst, ssem, rsem, where):
        pltpu.make_async_remote_copy(
            src_ref=src, dst_ref=dst, send_sem=ssem, recv_sem=rsem, device_id=where, device_id_type=MESH
        ).start()

    def bytes_of(ref, sem):
        return pltpu.make_async_copy(ref, ref, sem)

    def keep(src, dst, sem):
        pltpu.make_async_copy(src, dst, sem).start()

    loads[0].wait()
    band_sums = jnp.concatenate(
        [
            jnp.sum(temp[t, b * SUB : (b + 1) * SUB, :], axis=0, keepdims=True)
            for t in range(tiers)
            for b in range(rows // SUB)
        ],
        axis=0,
    )
    lane_b = iota((bands, LANES), 1)
    sub_b = iota((bands, LANES), 0)
    means = jnp.zeros((1, LANES), F32)
    per_band = cols // SUB
    for part in range(per_band):
        total = jnp.sum(jnp.where(div(lane_b, SUB) == part, band_sums, 0.0), axis=1, keepdims=True)
        means = means + jnp.sum(
            jnp.where(lane_b == sub_b * per_band + part, total, 0.0), axis=0, keepdims=True
        )
    means = means * (1.0 / (SUB * SUB))
    note_send[...] = means
    lane_s = iota((slots, slots), 1)
    sub_s = iota((slots, slots), 0)
    eye = lane_s == sub_s

    def to_col(row):
        return jnp.sum(jnp.where(eye, jnp.broadcast_to(row, (slots, slots)), 0.0), axis=1, keepdims=True)

    def to_row(col):
        return jnp.sum(jnp.where(eye, jnp.broadcast_to(col, (slots, slots)), 0.0), axis=0, keepdims=True)

    for load in loads[1:6]:
        load.wait()
    tgt_row = panel_ref[...].astype(F32)
    tgt_col = to_col(tgt_row)
    blk_row = block_ref[...].astype(F32)
    blk_col = to_col(blk_row)
    sub_col = to_col(place_ref[...].astype(F32))
    same_tile = tgt_col == tgt_row
    rank_col = jnp.sum(jnp.where(same_tile & (lane_s < sub_s), 1.0, 0.0), axis=1, keepdims=True)
    rank_row = jnp.sum(jnp.where(same_tile & (sub_s < lane_s), 1.0, 0.0), axis=0, keepdims=True)
    blocks = tier_ref.shape[1]
    of_block = blk_col == iota((slots, blocks), 1).astype(F32)
    tier_col = jnp.sum(jnp.where(of_block, tier_ref[...].astype(F32), 0.0), axis=1, keepdims=True)
    sens_col = jnp.sum(jnp.where(of_block, sens_ref[...], 0.0), axis=1, keepdims=True)
    pos_col = tier_col * in_plane + sub_col
    goes = (tgt_row * CAP + rank_row) == iota((tiles * CAP, slots), 0).astype(F32)
    pick = jnp.where(goes, 1.0, 0.0).astype(BF16)
    loads[6].wait()
    loads[7].wait()
    for src, dst in ((dyn, dyn_pick), (leak, leak_pick)):
        for fold in range(FOLDS):
            taken = jnp.dot(pick, src[:, fold * wide : (fold + 1) * wide], preferred_element_type=F32)
            for half in range(halves):
                dst[half, pl.ds(fold, tiles * CAP, stride=FOLDS), :] = taken[
                    :, half * LANES : (half + 1) * LANES
                ]
    for tile in range(tiles):
        for half in range(EARLY):
            at, lanes = slice(tile * rows_of_tile, (tile + 1) * rows_of_tile), slice(half * LANES, (half + 1) * LANES)
            early_send[tile, 0, :, lanes] = dyn_pick[half, at, :].astype(BF16)
            early_send[tile, 1, :, lanes] = leak_pick[half, at, :].astype(BF16)

    beyond = sum(exists.astype(jnp.int32) for exists, _ in across)
    pl.semaphore_wait(barrier, tiles - 1 + beyond)

    each_peer(lambda other: note_copy(other).start())
    keep(note_send, note_recv.at[me], note_rsem)
    each_peer(lambda other: early_copy(other).start(), low_first)
    keep(early_send.at[me], early_recv.at[me], early_rsem)

    sub8 = iota((2 * tiers, 2 * cols), 0)
    lane8 = mod(iota((2 * tiers, 2 * cols), 1), cols)
    picks = [
        jnp.where(
            ((sub8 == t) & (lane8 == 0)) | ((sub8 == tiers + t) & (lane8 == cols - 1)), 1.0, 0.0
        ).astype(BF16)
        for t in range(tiers)
    ]

    sub16 = iota((4 * tiers, 2 * cols), 0)
    lane16 = mod(iota((4 * tiers, 2 * cols), 1), cols)
    both_picks = [
        jnp.where(
            ((sub16 == t) & (lane16 == 0))
            | ((sub16 == tiers + t) & (lane16 == cols - 1))
            | ((sub16 == 2 * tiers + t) & (lane16 == 1))
            | ((sub16 == 3 * tiers + t) & (lane16 == cols - 2)),
            1.0,
            0.0,
        ).astype(BF16)
        for t in range(tiers)
    ]

    def halo_ends(turn, field, side, lands):
        if side < 2:
            return field.at[0 if side == 0 else tiers - 1], plane_recv.at[turn, lands], 0
        return edge_send.at[turn, (side - 2) // 2], edge_recv.at[turn, lands - 2], 1

    def halo_start(turn, field, exists, where, side):
        @pl.when(exists)
        def _():
            src, dst, kind = halo_ends(turn, field, side, side ^ 1)
            send(src, dst, halo_ssem.at[kind], halo_rsem.at[turn, kind], where)

    def pack_rows(turn, field):
        for end in range(2):
            at = end * (rows - 1)
            for t in range(tiers):
                edge_send[turn, 0, end * tiers + t : end * tiers + t + 1, :] = field[t, at : at + 1, :]

    def columns_of(field, taking=picks):
        columns = jnp.zeros((taking[0].shape[0], rows), F32)
        for t in range(tiers):
            columns = columns + lax.dot_general(
                taking[t], two_parts(field(t), 1), (((1,), (1,)), ((), ())), preferred_element_type=F32
            )
        return columns

    def rows_of(first, last):
        return jnp.concatenate([first(t) for t in range(tiers)] + [last(t) for t in range(tiers)], axis=0)

    def start_halo(turn, field):
        def start(which):
            for exists, where, side in which:
                halo_start(turn, field, exists, where, side)

        pack_rows(turn, field)
        start(sides[2:4])
        start(sides[:2])
        edge_send[turn, 1] = columns_of(lambda t: field[t])
        start(sides[4:])

    def wait_plane(turn):
        bytes_of(plane_recv.at[turn], halo_rsem.at[turn, 0]).wait()

    def wait_halo(turn):
        wait_plane(turn)
        bytes_of(edge_recv.at[turn], halo_rsem.at[turn, 1]).wait()

    row_i = iota((rows, cols), 0)
    col_i = iota((rows, cols), 1)
    sub16 = mod(iota((8 * tiers, tiers * cols), 0), 4 * tiers)
    lane16 = iota((8 * tiers, tiers * cols), 1)
    put = jnp.where(
        ((mod(lane16, cols) == 0) & (sub16 == tiers + div(lane16, cols)))
        | ((mod(lane16, cols) == cols - 1) & (sub16 == 2 * tiers + div(lane16, cols))),
        1.0,
        0.0,
    ).astype(BF16)

    def inside(field, t):
        v = field[t]
        none = jnp.zeros_like(v)
        low = none if t == 0 else field[t - 1]
        high = none if t == tiers - 1 else field[t + 1]
        north = jnp.where(row_i == 0, 0.0, pltpu.roll(v, 1, 0))
        south = jnp.where(row_i == rows - 1, 0.0, pltpu.roll(v, rows - 1, 0))
        west = jnp.where(col_i == 0, 0.0, pltpu.roll(v, 1, 1))
        east = jnp.where(col_i == cols - 1, 0.0, pltpu.roll(v, cols - 1, 1))
        return v, (low, high, north, south, west, east)

    def rims(west, east, t=None):
        ends = jnp.concatenate([west, east], axis=0)
        into = put if t is None else put[:, t * cols : (t + 1) * cols]
        return lax.dot_general(
            two_parts(ends, 0), into, (((0,), (0,)), ((), ())), preferred_element_type=F32
        )

    def apply_inside(field, t):
        v, around = inside(field, t)
        value = diag[t] * v
        for k in range(6):
            if not (k == 0 and t == 0 or k == 1 and t == tiers - 1):
                value = value - faces[k, t] * around[k]
        return value

    def add_beyond(turn):
        rim = rims(edge_recv[turn, 2], edge_recv[turn, 3])
        resid[0] = resid[0] + faces[0, 0] * plane_recv[turn, 0]
        resid[tiers - 1] = resid[tiers - 1] + faces[1, tiers - 1] * plane_recv[turn, 1]
        for t in range(tiers):
            first, last = slice(0, 1), slice(rows - 1, rows)
            resid[t, first, :] = (
                resid[t, first, :] + faces[2, t, first, :] * edge_recv[turn, 0, tiers + t : tiers + t + 1, :]
            )
            resid[t, last, :] = (
                resid[t, last, :] + faces[3, t, last, :] * edge_recv[turn, 1, t : t + 1, :]
            )
            face = jnp.where(col_i == 0, faces[4, t], faces[5, t])
            resid[t] = resid[t] + face * rim[:, t * cols : (t + 1) * cols]

    name_r = iota((named, slots), 0).astype(F32)
    named_row = tgt_row * 8.0 + rank_row
    named_col = tgt_col * 8.0 + rank_col
    by_name = name_r == named_row

    def rename(row):
        return jnp.sum(jnp.where(by_name, row, 0.0), axis=1, keepdims=True)

    pos_r = rename(to_row(pos_col) + 1.0)
    blk_r = rename(blk_row + 1.0)
    sens_r = rename(to_row(sens_col))
    blk_n = jnp.sum(
        jnp.where(named_col == iota((slots, named), 1).astype(F32), blk_col + 1.0, 0.0), axis=0, keepdims=True
    )
    same_block = jnp.where((blk_r == blk_n) & (blk_r > 0.0), 1.0, 0.0)
    block_size = jnp.maximum(jnp.sum(same_block, axis=1, keepdims=True), 1.0)
    same_three = jnp.concatenate([same_block.astype(BF16)] * 3, axis=1)
    at_place = (iota((named, LANES), 1) + 1).astype(F32) == pos_r
    group = div(iota((8, LANES), 1), LANES // CAP) == iota((8, LANES), 0)

    def one_row(block):
        return jnp.sum(jnp.where(group, block, 0.0), axis=0, keepdims=True)

    for tile in range(tiles):
        place_send[tile] = one_row(jnp.broadcast_to(pos_r[tile * 8 : (tile + 1) * 8], (8, LANES)))
    each_peer(lambda other: place_copy(other).start())
    keep(place_send.at[me], place_recv.at[me], place_rsem)

    loads[8].wait()
    start_halo(0, temp)
    start_halo(1, cond)

    bytes_of(note_recv, note_rsem).wait()
    tile_means = jnp.concatenate([jnp.broadcast_to(note_recv[tile], (8, LANES)) for tile in range(tiles)], axis=0)
    at_slots = three_parts(jnp.where(at_place, tile_means, 0.0), 0)
    block_sum = jnp.sum(
        jnp.dot(same_three, at_slots, preferred_element_type=F32), axis=1, keepdims=True
    )
    fac[...] = jnp.broadcast_to(jnp.exp(sens_r * (block_sum / block_size)), (named, LANES))

    upper_rank = iota((8, LANES), 0) >= FOLDS
    def load_step(step):
        other = low_first(step)

        def factor_of(rank):
            return fac[pl.ds(other * 8 + rank, 8, stride=0), :]

        by = jnp.concatenate(
            [jnp.where(upper_rank, factor_of(rank + 1), factor_of(rank)) for rank in range(0, CAP, 2)], axis=0
        )
        at = pl.ds(pl.multiple_of(other * rows_of_tile, rows_of_tile), rows_of_tile)
        for half in range(EARLY, halves):
            load_send[other, :, (half - EARLY) * LANES : (half - EARLY + 1) * LANES] = (
                dyn_pick[half, at, :] + by * leak_pick[half, at, :]
            ).astype(BF16)

        @pl.when(other != me)
        def _():
            load_copy(other).start()

    pl.loop(0, tiles // 8)(load_step)
    for tile in range(tiles):
        fac_send[tile] = one_row(fac[tile * 8 : (tile + 1) * 8, :])
    each_peer(lambda other: fac_copy(other).start(), low_first)
    keep(fac_send.at[me], fac_recv.at[me], fac_rsem)
    pl.loop(tiles // 8, tiles)(load_step)
    keep(load_send.at[me], load_recv.at[me], load_rsem)
    def missing(exists, blocks):
        @pl.when(jnp.logical_not(exists))
        def _():
            for recv, spare, at, ssem, rsem, none in blocks:
                keep(none, recv.at[at], rsem)
                keep(none, spare.at[at], ssem)

    none8 = nothing.at[:8, :]
    for exists, _, side in sides[:2]:
        missing(
            exists,
            [
                (plane_recv.at[turn], plane_spare.at[turn], side, halo_ssem.at[0], halo_rsem.at[turn, 0], nothing)
                for turn in range(4)
            ]
            + [(face_recv.at[side], face_spare.at[side], k, face_ssem, face_rsem, nothing) for k in range(3)],
        )
    for exists, _, side in sides[2:]:
        missing(
            exists,
            [
                (edge_recv.at[turn], edge_spare.at[turn], side - 2, halo_ssem.at[1], halo_rsem.at[turn, 1], none8)
                for turn in range(2)
            ]
            + [(gain_recv, gain_spare, 3 * (side - 2) + k, gain_ssem, gain_rsem, none8) for k in range(3)],
        )
    for step, _, count, slot in rims_of:
        missing(
            neighbour(*step)[0],
            [(rim_recv, rim_spare, slot + k, rim_ssem, rim_rsem, none8) for k in range(count)],
        )
    loads[9].wait()
    wait_halo(0)
    wait_halo(1)
    rim = rims(edge_recv[1, 2], edge_recv[1, 3])
    for t in range(tiers):
        c, (low, high, north, south, west, east) = inside(cond, t)
        here = rim[:, t * cols : (t + 1) * cols]
        low = plane_recv[1, 0] if t == 0 else low
        high = plane_recv[1, 1] if t == tiers - 1 else high
        north = jnp.where(row_i == 0, edge_recv[1, 0, tiers + t : tiers + t + 1, :], north)
        south = jnp.where(row_i == rows - 1, edge_recv[1, 1, t : t + 1, :], south)
        west = jnp.where(col_i == 0, here, west)
        east = jnp.where(col_i == cols - 1, here, east)
        total = mass[t]
        for k, beside in enumerate((low, high, north, south, west, east)):
            face = 0.5 * (c + beside)
            faces[k, t] = face
            total = total + face
        diag[t] = total
        inv[t] = 1.0 / total
    for t in range(tiers):
        resid[t] = mass[t] * temp[t] - apply_inside(temp, t)
    add_beyond(0)

    middle = (EIG_LOW + EIG_HIGH) / 2.0
    spread = (EIG_HIGH - EIG_LOW) / 2.0
    ratio = middle / spread
    weight_a = 1.0 / ratio
    weight_b = 1.0 / (2.0 * ratio - weight_a)
    weight_c = 1.0 / (2.0 * ratio - weight_b)
    keep_b, push_b = weight_b * weight_a, 2.0 * weight_b / spread
    keep_c, push_c = weight_c * weight_b, 2.0 * weight_c / spread

    for t in range(tiers):
        scaled = push_b * inv[t]
        for k in range(6):
            faces[k, t] = scaled * faces[k, t]
        inv[t] = inv[t] * (1.0 / middle)

    def layer_face(t):
        if t == 0 and t == tiers - 1:
            raise ValueError("one tier")
        return faces[0, t] if t == 0 else faces[1, t] if t == tiers - 1 else jnp.zeros((rows, cols), F32)

    first, last = slice(0, 1), slice(rows - 1, rows)
    side_face = [jnp.where(col_i == 0, faces[4, t], jnp.where(col_i == cols - 1, faces[5, t], 0.0)) for t in range(tiers)]
    ends_face = [jnp.where(row_i == 0, faces[2, t], jnp.where(row_i == rows - 1, faces[3, t], 0.0)) for t in range(tiers)]
    gain_send[0] = rows_of(lambda t: faces[2, t, first, :], lambda t: faces[3, t, last, :])
    gain_send[1] = rows_of(lambda t: layer_face(t)[first, :], lambda t: layer_face(t)[last, :])
    gain_send[2] = rows_of(lambda t: side_face[t][first, :], lambda t: side_face[t][last, :])
    gain_send[3] = columns_of(lambda t: side_face[t])
    gain_send[4] = columns_of(layer_face)
    gain_send[5] = columns_of(lambda t: ends_face[t])
    blank = jnp.zeros((rows, cols), F32)
    column_gain[0] = columns_of(lambda t: jnp.where(col_i == 0, faces[5, t], faces[4, t]))
    column_gain[1] = columns_of(lambda t: jnp.where(row_i == 0, 0.0, faces[2, t]))
    column_gain[2] = columns_of(lambda t: jnp.where(row_i == rows - 1, 0.0, faces[3, t]))
    column_gain[3] = columns_of(lambda t: faces[0, t] if t > 0 else blank)
    column_gain[4] = columns_of(lambda t: faces[1, t] if t < tiers - 1 else blank)
    for exists, where, side in sides[:2]:
        t = 0 if side == 0 else tiers - 1
        face_send[side, 0] = faces[side, t]
        face_send[side, 1] = ends_face[t]
        face_send[side, 2] = side_face[t]

        @pl.when(exists)
        def _(where=where, side=side):
            send(face_send.at[side], face_recv.at[side ^ 1], face_ssem, face_rsem, where)

    for exists, where, side in sides[2:]:
        lands = (side - 2) ^ 1

        @pl.when(exists)
        def _(where=where, side=side, lands=lands):
            send(
                gain_send.at[0:3] if side < 4 else gain_send.at[3:6],
                gain_recv.at[3 * lands : 3 * lands + 3],
                gain_ssem,
                gain_rsem,
                where,
            )

    sources = tiles * CAP * FOLDS
    sel_i = iota((FOLDS * patches, sources), 0)
    sel_j = iota((FOLDS * patches, sources), 1)
    sel_in = mod(sel_i, patches)
    sel_patch = mod(sel_in, bands) * per_band + div(sel_in, bands)
    fold_hit = div(sel_i, patches) == mod(sel_j, FOLDS)
    bytes_of(place_recv, place_rsem).wait()
    def by_source(ref):
        taken = jnp.concatenate([jnp.broadcast_to(ref[tile], (rows_of_tile, LANES)) for tile in range(tiles)], axis=0)
        rank = div(mod(iota(taken.shape, 0), rows_of_tile), FOLDS)
        return jnp.sum(jnp.where(iota(taken.shape, 1) == rank * (LANES // CAP), taken, 0.0), axis=1, keepdims=True)

    same = iota((sources, sources), 0) == iota((sources, sources), 1)
    code = jnp.sum(jnp.where(same, by_source(place_recv), 0.0), axis=0, keepdims=True)
    picker = jnp.where(fold_hit & (code == (sel_patch + 1).astype(F32)), 1.0, 0.0).astype(BF16)
    left = iota((bands, LANES), 1) < SUB

    def deposit(footprint, begin, end):
        for fold in range(FOLDS):
            for k in range(begin, end):
                lanes = slice((k - begin) * LANES, (k - begin + 1) * LANES)
                a = footprint[fold * patches : fold * patches + bands, lanes]
                b = footprint[fold * patches + bands : fold * patches + 2 * bands, lanes]
                at = 2 * (fold * halves + k)
                power_ref[pl.ds(at, bands, stride=SUB), :] = jnp.where(left, a, pltpu.roll(b, SUB, 1))
                power_ref[pl.ds(at + 1, bands, stride=SUB), :] = jnp.where(left, pltpu.roll(a, SUB, 1), b)

    bytes_of(fac_recv, fac_rsem).wait()
    factors = by_source(fac_recv)
    bytes_of(early_recv, early_rsem).wait()
    for half in range(EARLY):
        lanes = slice(half * LANES, (half + 1) * LANES)
        for tile in range(tiles):
            early_power[tile * rows_of_tile : (tile + 1) * rows_of_tile, lanes] = (
                early_recv[tile, 0, :, lanes].astype(F32)
                + factors[tile * rows_of_tile : (tile + 1) * rows_of_tile] * early_recv[tile, 1, :, lanes].astype(F32)
            ).astype(BF16)
    deposit(jnp.dot(picker, early_power[...], preferred_element_type=F32), 0, EARLY)
    bytes_of(load_recv, load_rsem).wait()
    deposit(
        jnp.dot(picker, load_recv[...].reshape(sources, wide - EARLY * LANES), preferred_element_type=F32), EARLY, halves
    )
    start, after = dirs.at[0], dirs.at[1]

    def begin_rows(t, begin, end):
        power_rows = power_ref[t * rows + begin : t * rows + end, :]
        start[t, begin:end, :] = (resid[t, begin:end, :] + power_rows) * inv[t, begin:end, :]

    for t in range(tiers):
        begin_rows(t, 0, 8)
        begin_rows(t, rows - 8, rows)

    def send_rims(which):
        for step, block, count, _ in which:
            exists, where = neighbour(*step)
            lands = slot_of[tuple(-d for d in step)]

            @pl.when(exists)
            def _(where=where, block=block, count=count, lands=lands):
                send(
                    rim_send.at[block : block + count],
                    rim_recv.at[lands : lands + count],
                    rim_ssem,
                    rim_rsem,
                    where,
                )

    def send_planes(turn, field):
        for exists, where, side in sides[:2]:
            halo_start(turn, field, exists, where, side)

    def around_sum(field, t):
        v, around = inside(field, t)
        value = None
        for k in range(6):
            if not (k == 0 and t == 0 or k == 1 and t == tiers - 1):
                term = faces[k, t] * around[k]
                value = term if value is None else value + term
        return v, value

    own_rows = rows_of(lambda t: start[t, first, :], lambda t: start[t, last, :])
    rim_send[0] = own_rows
    send_rims(rims_of[:8])
    stay = keep_b + push_b * (middle - 1.0)
    slab_lane = iota((8, cols), 1)

    def slab_row(t, begin, row, inward, shift):
        slab = slice(begin, begin + 8)
        v = start[t, slab, :]
        value = stay * v + faces[inward, t, slab, :] * pltpu.roll(v, shift, 0)
        value = value + faces[4, t, slab, :] * jnp.where(slab_lane == 0, 0.0, pltpu.roll(v, 1, 1))
        value = value + faces[5, t, slab, :] * jnp.where(slab_lane == cols - 1, 0.0, pltpu.roll(v, cols - 1, 1))
        if t > 0:
            value = value + faces[0, t, slab, :] * start[t - 1, slab, :]
        if t < tiers - 1:
            value = value + faces[1, t, slab, :] * start[t + 1, slab, :]
        return value[row : row + 1, :]

    rim_send[1] = rows_of(lambda t: slab_row(t, 0, 0, 3, 7), lambda t: slab_row(t, rows - 8, 7, 2, 1))
    send_rims(rims_of[12:14])
    for t in range(tiers):
        begin_rows(t, 8, rows - 8)
    send_planes(2, start)
    columns = columns_of(lambda t: start[t], both_picks)
    own_columns = columns[: 2 * tiers]
    rim_send[2] = own_columns
    rim_send[3] = (
        stay * own_columns
        + column_gain[0] * columns[2 * tiers :]
        + column_gain[1] * pltpu.roll(own_columns, 1, 1)
        + column_gain[2] * pltpu.roll(own_columns, rows - 1, 1)
        + column_gain[3] * pltpu.roll(own_columns, 1, 0)
        + column_gain[4] * pltpu.roll(own_columns, 2 * tiers - 1, 0)
    )
    send_rims(rims_of[14:])
    send_rims(rims_of[8:12])
    for t in range(tiers):
        v, value = around_sum(start, t)
        after[t] = stay * v + value
    send_planes(3, after)
    bytes_of(gain_recv, gain_rsem).wait()
    wait_plane(2)
    wait_plane(3)
    bytes_of(face_recv, face_rsem).wait()
    bytes_of(rim_recv, rim_rsem).wait()

    rim_a = rims(rim_recv[4], rim_recv[6])

    def beyond_rows(ref, t, scale, north, south, rim):
        ref[t, first, :] = ref[t, first, :] + scale * faces[2, t, first, :] * north
        ref[t, last, :] = ref[t, last, :] + scale * faces[3, t, last, :] * south
        face = jnp.where(col_i == 0, faces[4, t], faces[5, t])
        ref[t] = ref[t] + scale * face * rim[:, t * cols : (t + 1) * cols]

    second = resid
    for t in range(tiers):
        value = after[t]
        if t == 0:
            value = value + faces[0, t] * plane_recv[2, 0]
        if t == tiers - 1:
            value = value + faces[1, t] * plane_recv[2, 1]
        second[t] = value
        beyond_rows(
            second, t, 1.0, rim_recv[0, tiers + t : tiers + t + 1, :], rim_recv[2, t : t + 1, :], rim_a
        )

    for side, t in ((0, tiers - 1), (1, 0)):
        plane = plane_recv.at[3, side]
        rim = rims(rim_recv[16 + side], rim_recv[18 + side], t)
        plane[...] = (
            plane[...] + face_recv[side, 0] * start[0 if side == 0 else tiers - 1] + face_recv[side, 2] * rim
        )
        plane[first, :] = (
            plane[first, :] + face_recv[side, 1, first, :] * rim_recv[12 + side, tiers + t : tiers + t + 1, :]
        )
        plane[last, :] = plane[last, :] + face_recv[side, 1, last, :] * rim_recv[14 + side, t : t + 1, :]

    eight_s = iota((2 * tiers, cols), 0)
    eight_l = iota((2 * tiers, cols), 1)
    upper = eight_s >= tiers
    tier_s = mod(eight_s, tiers)

    def pair(a, b):
        return jnp.where(upper, a, b)

    def swap(x):
        return pltpu.roll(x, tiers, 0)

    def layer_part(down, up):
        return jnp.where(
            tier_s == 0, pltpu.roll(down, tiers + 1, 0), jnp.where(tier_s == tiers - 1, pltpu.roll(up, tiers - 1, 0), 0.0)
        )

    north_west, north_east, south_west, south_east = (rim_recv[8 + i] for i in range(4))

    def shell(own, at, layer_at, gain_at, side_part):
        return (
            pair(rim_recv[at + 1], rim_recv[at + 3])
            + pair(gain_recv[gain_at], gain_recv[gain_at + 3]) * swap(own)
            + pair(gain_recv[gain_at + 1], gain_recv[gain_at + 4])
            * layer_part(
                pair(rim_recv[layer_at], rim_recv[layer_at + 2]), pair(rim_recv[layer_at + 1], rim_recv[layer_at + 3])
            )
            + pair(gain_recv[gain_at + 2], gain_recv[gain_at + 5]) * side_part
        )

    row_shell = shell(
        own_rows,
        0,
        12,
        0,
        jnp.where(
            eight_l == 0,
            pltpu.roll(pair(north_west, south_west), 1, 1),
            pltpu.roll(pair(north_east, south_east), cols - 1, 1),
        ),
    )
    col_shell = shell(
        own_columns,
        4,
        16,
        6,
        jnp.where(
            eight_l == 0,
            pair(pltpu.roll(north_west, 1, 1), swap(north_east)),
            pair(swap(south_west), pltpu.roll(south_east, cols - 1, 1)),
        ),
    )
    rim_b = rims(col_shell, col_shell)

    lift = push_c / push_b
    old = 1.0 - lift * keep_b
    now = 1.0 + keep_c + lift - push_c
    for t in range(tiers):
        v, value = around_sum(second, t)
        if t == 0:
            value = value + faces[0, t] * plane_recv[3, 0]
        if t == tiers - 1:
            value = value + faces[1, t] * plane_recv[3, 1]
        out_ref[t] = temp[t] + old * start[t] + now * v + lift * value
        beyond_rows(
            out_ref, t, lift, row_shell[tiers + t : tiers + t + 1, :], row_shell[t : t + 1, :], rim_b
        )
    bytes_of(plane_recv, halo_ssem.at[0]).wait()
    bytes_of(edge_recv, halo_ssem.at[1]).wait()
    bytes_of(rim_recv, rim_ssem).wait()
    bytes_of(gain_recv, gain_ssem).wait()
    bytes_of(face_recv, face_ssem).wait()
    bytes_of(note_recv.at[1:], note_ssem).wait()
    bytes_of(place_recv.at[1:], place_ssem).wait()
    bytes_of(fac_recv.at[1:], fac_ssem).wait()
    bytes_of(early_recv.at[1:], early_ssem).wait()
    bytes_of(load_recv.at[1:], load_ssem).wait()


def hand_over(new, power, new_out, power_out, sem):
    moves = (pltpu.make_async_copy(power, power_out, sem.at[0]), pltpu.make_async_copy(new, new_out, sem.at[1]))
    for move in moves:
        move.start()
    for move in moves:
        move.wait()


def shards(sizes, temp, cond, mass, dyn, leak, panel, place, block, tier, sens):
    tiers, rows, cols = temp.shape
    slots, cells = dyn.shape[1:]
    tiles = sizes[0] * sizes[1]
    any_spec = pl.BlockSpec(memory_space=pl.ANY)
    vmem_spec = pl.BlockSpec(memory_space=pltpu.VMEM)
    grid = (tiers, rows, cols)
    dma = pltpu.SemaphoreType.DMA
    new, power = pl.pallas_call(
        functools.partial(kernel, sizes),
        out_shape=(
            pltpu.VMEM(grid, F32),
            pltpu.VMEM((tiers * rows, cols), F32),
        ),
        in_specs=[any_spec] * 10,
        out_specs=(vmem_spec, vmem_spec),
        scratch_shapes=[
            pltpu.VMEM((1, slots), jnp.int32),
            pltpu.VMEM((1, slots), jnp.int32),
            pltpu.VMEM((1, slots), jnp.int32),
            pltpu.VMEM(tier.shape, jnp.int32),
            pltpu.VMEM(sens.shape, F32),
            pltpu.VMEM(grid, F32),
            pltpu.VMEM(grid, F32),
            pltpu.VMEM(grid, F32),
            pltpu.VMEM((slots, cells), BF16),
            pltpu.VMEM((slots, cells), BF16),
            pltpu.VMEM((cells // FOLDS // LANES, tiles * CAP * FOLDS, LANES), F32),
            pltpu.VMEM((cells // FOLDS // LANES, tiles * CAP * FOLDS, LANES), F32),
            pltpu.VMEM((1, LANES), F32),
            pltpu.VMEM((tiles, 1, LANES), F32),
            pltpu.VMEM((tiles, 1, LANES), F32),
            pltpu.VMEM((tiles, 1, LANES), F32),
            pltpu.VMEM((8 * tiles, LANES), F32),
            pltpu.VMEM((tiles, 1, LANES), F32),
            pltpu.VMEM((tiles, 1, LANES), F32),
            pltpu.VMEM((tiles, 2, CAP * FOLDS, EARLY * LANES), BF16),
            pltpu.VMEM((tiles, 2, CAP * FOLDS, EARLY * LANES), BF16),
            pltpu.VMEM((tiles * CAP * FOLDS, EARLY * LANES), BF16),
            pltpu.VMEM((tiles, CAP * FOLDS, cells // FOLDS - EARLY * LANES), BF16),
            pltpu.VMEM((tiles, CAP * FOLDS, cells // FOLDS - EARLY * LANES), BF16),
            pltpu.VMEM((SWEEPS - 1,) + grid, F32),
            pltpu.VMEM((6,) + grid, F32),
            pltpu.VMEM(grid, F32),
            pltpu.VMEM(grid, F32),
            pltpu.VMEM(grid, F32),
            pltpu.VMEM((5, 2 * tiers, cols), F32),
            pltpu.VMEM((2, 2, 2 * tiers, cols), F32),
            pltpu.VMEM((2, 4, 2 * tiers, cols), F32),
            pltpu.VMEM((2, 4, 2 * tiers, cols), F32),
            pltpu.VMEM((4, 2, rows, cols), F32),
            pltpu.VMEM((4, 2, rows, cols), F32),
            pltpu.VMEM((4, 2 * tiers, cols), F32),
            pltpu.VMEM((20, 2 * tiers, cols), F32),
            pltpu.VMEM((20, 2 * tiers, cols), F32),
            pltpu.VMEM((6, 2 * tiers, cols), F32),
            pltpu.VMEM((12, 2 * tiers, cols), F32),
            pltpu.VMEM((12, 2 * tiers, cols), F32),
            pltpu.VMEM((2, 3, rows, cols), F32),
            pltpu.VMEM((2, 3, rows, cols), F32),
            pltpu.VMEM((2, 3, rows, cols), F32),
            pltpu.VMEM((rows, cols), F32),
            dma((10,)),
            dma(()),
            dma(()),
            dma(()),
            dma(()),
            dma(()),
            dma(()),
            dma(()),
            dma(()),
            dma(()),
            dma(()),
            dma((2,)),
            dma((4, 2)),
            dma(()),
            dma(()),
            dma(()),
            dma(()),
            dma(()),
            dma(()),
        ],
        compiler_params=pltpu.CompilerParams(
            collective_id=0, has_side_effects=True, vmem_limit_bytes=VMEM_BYTES
        ),
    )(
        *(
            pltpu.with_memory_space_constraint(given, pltpu.HBM)
            for given in (temp, cond, mass, dyn, leak, panel.reshape(1, slots), place, block, tier, sens)
        )
    )
    return pl.pallas_call(
        hand_over,
        out_shape=(jax.ShapeDtypeStruct(grid, F32),) * 2,
        in_specs=[vmem_spec] * 2,
        out_specs=(any_spec, any_spec),
        scratch_shapes=[dma((2,))],
        compiler_params=pltpu.CompilerParams(vmem_limit_bytes=VMEM_BYTES),
    )(new, power.reshape(grid))


def solution(mesh):
    sizes = (mesh.shape["row"], mesh.shape["col"], mesh.shape["layer"])
    owner = ("row", "col", "layer")
    return jax.shard_map(
        functools.partial(shards, sizes),
        mesh=mesh,
        in_specs=(P("layer", "row", "col"),) * 3
        + (P(owner, None, None),) * 3
        + (P(owner, None),) * 4,
        out_specs=(P("layer", "row", "col"), P("layer", "row", "col")),
        check_vma=False,
    )
```

```python
import functools
import jax
import jax.numpy as jnp
from jax import lax
from jax.experimental import pallas as pl
from jax.experimental.pallas import tpu as pltpu
from jax.sharding import PartitionSpec as P

SUB = 64
SWEEPS = 3
CAP = 4
EIG_LOW = 0.1
EIG_HIGH = 2.0
LANES = 128
FOLDS = 4
EARLY = 1
VMEM_BYTES = 40 << 20

MESH = pl.DeviceIdType.MESH
F32 = jnp.float32
BF16 = jnp.bfloat16


def iota(shape, dim):
    return lax.broadcasted_iota(jnp.int32, shape, dim)


def div(x, n):
    if n & (n - 1):
        return x // n
    return lax.shift_right_logical(x, jnp.int32(n.bit_length() - 1))


def mod(x, n):
    if n & (n - 1):
        return lax.rem(x, n)
    return x & (n - 1)


def three_parts(x, axis):
    head = x.astype(BF16)
    rest = x - head.astype(F32)
    body = rest.astype(BF16)
    return jnp.concatenate([head, body, (rest - body.astype(F32)).astype(BF16)], axis=axis)


def two_parts(x, axis):
    head = x.astype(BF16)
    return jnp.concatenate([head, (x - head.astype(F32)).astype(BF16)], axis=axis)


def kernel(
    sizes,
    temp_hbm,
    cond_hbm,
    mass_hbm,
    dyn_hbm,
    leak_hbm,
    panel_hbm,
    place_hbm,
    block_hbm,
    tier_hbm,
    sens_hbm,
    out_ref,
    power_ref,
    panel_ref,
    place_ref,
    block_ref,
    tier_ref,
    sens_ref,
    temp,
    cond,
    mass,
    dyn,
    leak,
    dyn_pick,
    leak_pick,
    note_send,
    note_recv,
    place_send,
    place_recv,
    fac,
    fac_send,
    fac_recv,
    early_send,
    early_recv,
    early_power,
    load_send,
    load_recv,
    dirs,
    faces,
    diag,
    inv,
    resid,
    column_gain,
    edge_send,
    edge_recv,
    edge_spare,
    plane_recv,
    plane_spare,
    rim_send,
    rim_recv,
    rim_spare,
    gain_send,
    gain_recv,
    gain_spare,
    face_send,
    face_recv,
    face_spare,
    nothing,
    sent,
    in_sem,
    out_sem,
    note_rsem,
    place_rsem,
    fac_rsem,
    early_rsem,
    load_rsem,
    halo_rsem,
    rim_rsem,
    gain_rsem,
    face_rsem,
):
    n_row, n_col, n_layer = sizes
    tiles = n_row * n_col
    tiers, rows, cols = temp.shape
    slots, cells = dyn.shape
    wide = cells // FOLDS
    halves = wide // LANES
    rows_of_tile = CAP * FOLDS
    named = 8 * tiles
    in_plane = (rows // SUB) * (cols // SUB)
    patches = tiers * in_plane
    bands = tiers * (rows // SUB)
    my_row = lax.axis_index("row")
    my_col = lax.axis_index("col")
    my_layer = lax.axis_index("layer")
    me = my_row * n_col + my_col

    loads = [
        pltpu.make_async_copy(src, dst, in_sem.at[i])
        for i, (src, dst) in enumerate(
            (
                (temp_hbm, temp),
                (panel_hbm, panel_ref),
                (place_hbm, place_ref),
                (block_hbm, block_ref),
                (tier_hbm, tier_ref),
                (sens_hbm, sens_ref),
                (dyn_hbm.at[0], dyn),
                (leak_hbm.at[0], leak),
                (cond_hbm, cond),
                (mass_hbm, mass),
            )
        )
    ]
    for load in loads:
        load.start()

    def far_first(step):
        if n_row & (n_row - 1) or n_col & (n_col - 1) or n_col == 1:
            return lax.rem(me + step, tiles)
        near = n_col // 2
        turn = mod(step, tiles // 2)
        over_row = n_row - 1 - div(turn, near)
        over_col = n_col - 1 - mod(turn, near) - near * div(step, tiles // 2)
        return lax.bitwise_xor(my_row, over_row) * n_col + lax.bitwise_xor(my_col, over_col)

    def low_first(step):
        if n_row & (n_row - 1) or n_col & (n_col - 1) or n_row == 1 or n_col == 1:
            return lax.rem(me + step, tiles)
        near = n_col // 2
        group, turn = div(step, tiles // 2), mod(step, tiles // 2)
        over, turn = div(turn, tiles // 4), mod(turn, tiles // 4)
        over_row = n_row // 2 - 1 - div(turn, near)
        over_col = n_col - 1 - mod(turn, near) - near * over
        row = group * (n_row // 2) + lax.bitwise_xor(mod(my_row, n_row // 2), over_row)
        return row * n_col + lax.bitwise_xor(my_col, over_col)

    def each_peer(act, order=far_first):
        @pl.loop(0, tiles)
        def _(step):
            other = order(step)
            pl.when(other != me)(lambda: act(other))

    def device(other):
        return {"row": div(other, n_col), "col": mod(other, n_col)}

    sides = (
        (my_layer > 0, {"layer": my_layer - 1}, 0),
        (my_layer < n_layer - 1, {"layer": my_layer + 1}, 1),
        (my_row > 0, {"row": my_row - 1}, 2),
        (my_row < n_row - 1, {"row": my_row + 1}, 3),
        (my_col > 0, {"col": my_col - 1}, 4),
        (my_col < n_col - 1, {"col": my_col + 1}, 5),
    )

    def neighbour(d_row, d_col, d_layer):
        exists, where = [], {}
        for axis, mine, count, d in (
            ("row", my_row, n_row, d_row),
            ("col", my_col, n_col, d_col),
            ("layer", my_layer, n_layer, d_layer),
        ):
            if d:
                exists.append(mine > 0 if d < 0 else mine < count - 1)
                where[axis] = mine + d
        return functools.reduce(jnp.logical_and, exists), where

    rims_of = (
        [((a, b, 0), 0, 1, 8 + i) for i, (a, b) in enumerate(((-1, -1), (-1, 1), (1, -1), (1, 1)))]
        + [((a, 0, c), 0, 1, 12 + i) for i, (a, c) in enumerate(((-1, -1), (-1, 1), (1, -1), (1, 1)))]
        + [((0, b, c), 2, 1, 16 + i) for i, (b, c) in enumerate(((-1, -1), (-1, 1), (1, -1), (1, 1)))]
        + [((-1, 0, 0), 0, 2, 0), ((1, 0, 0), 0, 2, 2), ((0, -1, 0), 2, 2, 4), ((0, 1, 0), 2, 2, 6)]
    )
    slot_of = {step: slot for step, _, _, slot in rims_of}

    nothing[...] = jnp.zeros_like(nothing)
    barrier = pltpu.get_barrier_semaphore()

    each_peer(
        lambda other: pl.semaphore_signal(barrier, inc=1, device_id=device(other), device_id_type=MESH)
    )

    across = [neighbour(*step) for step, _, _, _ in rims_of if step[2]] + [neighbour(0, 0, -1), neighbour(0, 0, 1)]
    for exists, where in across:

        @pl.when(exists)
        def _(where=where):
            pl.semaphore_signal(barrier, inc=1, device_id=where, device_id_type=MESH)

    def remote(src, dst, ssem, rsem, other):
        return pltpu.make_async_remote_copy(
            src_ref=src,
            dst_ref=dst,
            send_sem=ssem,
            recv_sem=rsem,
            device_id=device(other),
            device_id_type=MESH,
        )

    def note_copy(other):
        return remote(note_send, note_recv.at[me], out_sem, note_rsem, other)

    def place_copy(other):
        return remote(place_send.at[other], place_recv.at[me], out_sem, place_rsem, other)

    def fac_copy(other):
        return remote(fac_send.at[other], fac_recv.at[me], out_sem, fac_rsem, other)

    def early_copy(other):
        return remote(early_send.at[other], early_recv.at[me], out_sem, early_rsem, other)

    def load_copy(other):
        return remote(load_send.at[other], load_recv.at[me], out_sem, load_rsem, other)

    def send(src, dst, ssem, rsem, where):
        pltpu.make_async_remote_copy(
            src_ref=src, dst_ref=dst, send_sem=ssem, recv_sem=rsem, device_id=where, device_id_type=MESH
        ).start()

    def bytes_of(ref, sem):
        return pltpu.make_async_copy(ref, ref, sem)

    def keep(src, dst, sem):
        pltpu.make_async_copy(src, dst, sem).start()

    loads[0].wait()
    band_sums = jnp.concatenate(
        [
            jnp.sum(temp[t, b * SUB : (b + 1) * SUB, :], axis=0, keepdims=True)
            for t in range(tiers)
            for b in range(rows // SUB)
        ],
        axis=0,
    )
    lane_b = iota((bands, LANES), 1)
    sub_b = iota((bands, LANES), 0)
    means = jnp.zeros((1, LANES), F32)
    per_band = cols // SUB
    for part in range(per_band):
        total = jnp.sum(jnp.where(div(lane_b, SUB) == part, band_sums, 0.0), axis=1, keepdims=True)
        means = means + jnp.sum(
            jnp.where(lane_b == sub_b * per_band + part, total, 0.0), axis=0, keepdims=True
        )
    means = means * (1.0 / (SUB * SUB))
    note_send[...] = means
    lane_s = iota((slots, slots), 1)
    sub_s = iota((slots, slots), 0)
    eye = lane_s == sub_s

    def to_col(row):
        return jnp.sum(jnp.where(eye, jnp.broadcast_to(row, (slots, slots)), 0.0), axis=1, keepdims=True)

    def to_row(col):
        return jnp.sum(jnp.where(eye, jnp.broadcast_to(col, (slots, slots)), 0.0), axis=0, keepdims=True)

    for load in loads[1:6]:
        load.wait()
    tgt_row = panel_ref[...].astype(F32)
    tgt_col = to_col(tgt_row)
    blk_row = block_ref[...].astype(F32)
    blk_col = to_col(blk_row)
    sub_col = to_col(place_ref[...].astype(F32))
    same_tile = tgt_col == tgt_row
    rank_col = jnp.sum(jnp.where(same_tile & (lane_s < sub_s), 1.0, 0.0), axis=1, keepdims=True)
    rank_row = jnp.sum(jnp.where(same_tile & (sub_s < lane_s), 1.0, 0.0), axis=0, keepdims=True)
    blocks = tier_ref.shape[1]
    of_block = blk_col == iota((slots, blocks), 1).astype(F32)
    tier_col = jnp.sum(jnp.where(of_block, tier_ref[...].astype(F32), 0.0), axis=1, keepdims=True)
    sens_col = jnp.sum(jnp.where(of_block, sens_ref[...], 0.0), axis=1, keepdims=True)
    pos_col = tier_col * in_plane + sub_col
    goes = (tgt_row * CAP + rank_row) == iota((tiles * CAP, slots), 0).astype(F32)
    pick = jnp.where(goes, 1.0, 0.0).astype(BF16)
    loads[6].wait()
    loads[7].wait()
    for src, dst in ((dyn, dyn_pick), (leak, leak_pick)):
        for fold in range(FOLDS):
            taken = jnp.dot(pick, src[:, fold * wide : (fold + 1) * wide], preferred_element_type=F32)
            for half in range(halves):
                dst[half, pl.ds(fold, tiles * CAP, stride=FOLDS), :] = taken[
                    :, half * LANES : (half + 1) * LANES
                ]
    for tile in range(tiles):
        for half in range(EARLY):
            at, lanes = slice(tile * rows_of_tile, (tile + 1) * rows_of_tile), slice(half * LANES, (half + 1) * LANES)
            early_send[tile, 0, :, lanes] = dyn_pick[half, at, :].astype(BF16)
            early_send[tile, 1, :, lanes] = leak_pick[half, at, :].astype(BF16)

    beyond = sum(exists.astype(jnp.int32) for exists, _ in across)
    pl.semaphore_wait(barrier, tiles - 1 + beyond)

    each_peer(lambda other: note_copy(other).start())
    keep(note_send, note_recv.at[me], note_rsem)
    each_peer(lambda other: early_copy(other).start(), low_first)
    keep(early_send.at[me], early_recv.at[me], early_rsem)

    sub8 = iota((2 * tiers, 2 * cols), 0)
    lane8 = mod(iota((2 * tiers, 2 * cols), 1), cols)
    picks = [
        jnp.where(
            ((sub8 == t) & (lane8 == 0)) | ((sub8 == tiers + t) & (lane8 == cols - 1)), 1.0, 0.0
        ).astype(BF16)
        for t in range(tiers)
    ]

    sub16 = iota((4 * tiers, 2 * cols), 0)
    lane16 = mod(iota((4 * tiers, 2 * cols), 1), cols)
    both_picks = [
        jnp.where(
            ((sub16 == t) & (lane16 == 0))
            | ((sub16 == tiers + t) & (lane16 == cols - 1))
            | ((sub16 == 2 * tiers + t) & (lane16 == 1))
            | ((sub16 == 3 * tiers + t) & (lane16 == cols - 2)),
            1.0,
            0.0,
        ).astype(BF16)
        for t in range(tiers)
    ]

    def halo_ends(turn, field, side, lands):
        if side < 2:
            return field.at[0 if side == 0 else tiers - 1], plane_recv.at[turn, lands], 0
        return edge_send.at[turn, (side - 2) // 2], edge_recv.at[turn, lands - 2], 1

    def halo_start(turn, field, exists, where, side):
        @pl.when(exists)
        def _():
            src, dst, kind = halo_ends(turn, field, side, side ^ 1)
            send(src, dst, out_sem, halo_rsem.at[turn, kind], where)

    def pack_rows(turn, field):
        for end in range(2):
            at = end * (rows - 1)
            for t in range(tiers):
                edge_send[turn, 0, end * tiers + t : end * tiers + t + 1, :] = field[t, at : at + 1, :]

    def columns_of(field, taking=picks):
        columns = jnp.zeros((taking[0].shape[0], rows), F32)
        for t in range(tiers):
            columns = columns + lax.dot_general(
                taking[t], two_parts(field(t), 1), (((1,), (1,)), ((), ())), preferred_element_type=F32
            )
        return columns

    def rows_of(first, last):
        return jnp.concatenate([first(t) for t in range(tiers)] + [last(t) for t in range(tiers)], axis=0)

    def start_halo(turn, field):
        def start(which):
            for exists, where, side in which:
                halo_start(turn, field, exists, where, side)

        pack_rows(turn, field)
        start(sides[2:4])
        start(sides[:2])
        edge_send[turn, 1] = columns_of(lambda t: field[t])
        start(sides[4:])

    def wait_plane(turn):
        bytes_of(plane_recv.at[turn], halo_rsem.at[turn, 0]).wait()

    def wait_halo(turn):
        wait_plane(turn)
        bytes_of(edge_recv.at[turn], halo_rsem.at[turn, 1]).wait()

    row_i = iota((rows, cols), 0)
    col_i = iota((rows, cols), 1)
    sub16 = mod(iota((8 * tiers, tiers * cols), 0), 4 * tiers)
    lane16 = iota((8 * tiers, tiers * cols), 1)
    put = jnp.where(
        ((mod(lane16, cols) == 0) & (sub16 == tiers + div(lane16, cols)))
        | ((mod(lane16, cols) == cols - 1) & (sub16 == 2 * tiers + div(lane16, cols))),
        1.0,
        0.0,
    ).astype(BF16)

    def inside(field, t):
        v = field[t]
        none = jnp.zeros_like(v)
        low = none if t == 0 else field[t - 1]
        high = none if t == tiers - 1 else field[t + 1]
        north = jnp.where(row_i == 0, 0.0, pltpu.roll(v, 1, 0))
        south = jnp.where(row_i == rows - 1, 0.0, pltpu.roll(v, rows - 1, 0))
        west = jnp.where(col_i == 0, 0.0, pltpu.roll(v, 1, 1))
        east = jnp.where(col_i == cols - 1, 0.0, pltpu.roll(v, cols - 1, 1))
        return v, (low, high, north, south, west, east)

    def rims(west, east, t=None):
        ends = jnp.concatenate([west, east], axis=0)
        into = put if t is None else put[:, t * cols : (t + 1) * cols]
        return lax.dot_general(
            two_parts(ends, 0), into, (((0,), (0,)), ((), ())), preferred_element_type=F32
        )

    def apply_inside(field, t):
        v, around = inside(field, t)
        value = diag[t] * v
        for k in range(6):
            if not (k == 0 and t == 0 or k == 1 and t == tiers - 1):
                value = value - faces[k, t] * around[k]
        return value

    def add_beyond(turn):
        rim = rims(edge_recv[turn, 2], edge_recv[turn, 3])
        resid[0] = resid[0] + faces[0, 0] * plane_recv[turn, 0]
        resid[tiers - 1] = resid[tiers - 1] + faces[1, tiers - 1] * plane_recv[turn, 1]
        for t in range(tiers):
            first, last = slice(0, 1), slice(rows - 1, rows)
            resid[t, first, :] = (
                resid[t, first, :] + faces[2, t, first, :] * edge_recv[turn, 0, tiers + t : tiers + t + 1, :]
            )
            resid[t, last, :] = (
                resid[t, last, :] + faces[3, t, last, :] * edge_recv[turn, 1, t : t + 1, :]
            )
            face = jnp.where(col_i == 0, faces[4, t], faces[5, t])
            resid[t] = resid[t] + face * rim[:, t * cols : (t + 1) * cols]

    name_r = iota((named, slots), 0).astype(F32)
    named_row = tgt_row * 8.0 + rank_row
    named_col = tgt_col * 8.0 + rank_col
    by_name = name_r == named_row

    def rename(row):
        return jnp.sum(jnp.where(by_name, row, 0.0), axis=1, keepdims=True)

    pos_r = rename(to_row(pos_col) + 1.0)
    blk_r = rename(blk_row + 1.0)
    sens_r = rename(to_row(sens_col))
    blk_n = jnp.sum(
        jnp.where(named_col == iota((slots, named), 1).astype(F32), blk_col + 1.0, 0.0), axis=0, keepdims=True
    )
    same_block = jnp.where((blk_r == blk_n) & (blk_r > 0.0), 1.0, 0.0)
    block_size = jnp.maximum(jnp.sum(same_block, axis=1, keepdims=True), 1.0)
    same_three = jnp.concatenate([same_block.astype(BF16)] * 3, axis=1)
    at_place = (iota((named, LANES), 1) + 1).astype(F32) == pos_r
    group = div(iota((8, LANES), 1), LANES // CAP) == iota((8, LANES), 0)

    def one_row(block):
        return jnp.sum(jnp.where(group, block, 0.0), axis=0, keepdims=True)

    for tile in range(tiles):
        place_send[tile] = one_row(jnp.broadcast_to(pos_r[tile * 8 : (tile + 1) * 8], (8, LANES)))
    each_peer(lambda other: place_copy(other).start())
    keep(place_send.at[me], place_recv.at[me], place_rsem)

    loads[8].wait()
    start_halo(0, temp)
    start_halo(1, cond)

    bytes_of(note_recv, note_rsem).wait()
    tile_means = jnp.concatenate([jnp.broadcast_to(note_recv[tile], (8, LANES)) for tile in range(tiles)], axis=0)
    at_slots = three_parts(jnp.where(at_place, tile_means, 0.0), 0)
    block_sum = jnp.sum(
        jnp.dot(same_three, at_slots, preferred_element_type=F32), axis=1, keepdims=True
    )
    fac[...] = jnp.broadcast_to(jnp.exp(sens_r * (block_sum / block_size)), (named, LANES))

    upper_rank = iota((8, LANES), 0) >= FOLDS
    def load_step(step):
        other = low_first(step)

        def factor_of(rank):
            return fac[pl.ds(other * 8 + rank, 8, stride=0), :]

        by = jnp.concatenate(
            [jnp.where(upper_rank, factor_of(rank + 1), factor_of(rank)) for rank in range(0, CAP, 2)], axis=0
        )
        at = pl.ds(pl.multiple_of(other * rows_of_tile, rows_of_tile), rows_of_tile)
        for half in range(EARLY, halves):
            load_send[other, :, (half - EARLY) * LANES : (half - EARLY + 1) * LANES] = (
                dyn_pick[half, at, :] + by * leak_pick[half, at, :]
            ).astype(BF16)

        @pl.when(other != me)
        def _():
            load_copy(other).start()

    pl.loop(0, tiles // 8)(load_step)
    for tile in range(tiles):
        fac_send[tile] = one_row(fac[tile * 8 : (tile + 1) * 8, :])
    each_peer(lambda other: fac_copy(other).start(), low_first)
    keep(fac_send.at[me], fac_recv.at[me], fac_rsem)
    pl.loop(tiles // 8, tiles)(load_step)
    keep(load_send.at[me], load_recv.at[me], load_rsem)
    def missing(exists, blocks):
        @pl.when(jnp.logical_not(exists))
        def _():
            for recv, spare, at, ssem, rsem, none in blocks:
                keep(none, recv.at[at], rsem)
                keep(none, spare.at[at], ssem)

    none8 = nothing.at[:8, :]
    for exists, _, side in sides[:2]:
        missing(
            exists,
            [
                (plane_recv.at[turn], plane_spare.at[turn], side, out_sem, halo_rsem.at[turn, 0], nothing)
                for turn in range(4)
            ]
            + [(face_recv.at[side], face_spare.at[side], k, out_sem, face_rsem, nothing) for k in range(3)],
        )
    for exists, _, side in sides[2:]:
        missing(
            exists,
            [
                (edge_recv.at[turn], edge_spare.at[turn], side - 2, out_sem, halo_rsem.at[turn, 1], none8)
                for turn in range(2)
            ]
            + [(gain_recv, gain_spare, 3 * (side - 2) + k, out_sem, gain_rsem, none8) for k in range(3)],
        )
    for step, _, count, slot in rims_of:
        missing(
            neighbour(*step)[0],
            [(rim_recv, rim_spare, slot + k, out_sem, rim_rsem, none8) for k in range(count)],
        )
    loads[9].wait()
    wait_halo(0)
    wait_halo(1)
    rim = rims(edge_recv[1, 2], edge_recv[1, 3])
    for t in range(tiers):
        c, (low, high, north, south, west, east) = inside(cond, t)
        here = rim[:, t * cols : (t + 1) * cols]
        low = plane_recv[1, 0] if t == 0 else low
        high = plane_recv[1, 1] if t == tiers - 1 else high
        north = jnp.where(row_i == 0, edge_recv[1, 0, tiers + t : tiers + t + 1, :], north)
        south = jnp.where(row_i == rows - 1, edge_recv[1, 1, t : t + 1, :], south)
        west = jnp.where(col_i == 0, here, west)
        east = jnp.where(col_i == cols - 1, here, east)
        total = mass[t]
        for k, beside in enumerate((low, high, north, south, west, east)):
            face = 0.5 * (c + beside)
            faces[k, t] = face
            total = total + face
        diag[t] = total
        inv[t] = 1.0 / total
    for t in range(tiers):
        resid[t] = mass[t] * temp[t] - apply_inside(temp, t)
    add_beyond(0)

    middle = (EIG_LOW + EIG_HIGH) / 2.0
    spread = (EIG_HIGH - EIG_LOW) / 2.0
    ratio = middle / spread
    weight_a = 1.0 / ratio
    weight_b = 1.0 / (2.0 * ratio - weight_a)
    weight_c = 1.0 / (2.0 * ratio - weight_b)
    keep_b, push_b = weight_b * weight_a, 2.0 * weight_b / spread
    keep_c, push_c = weight_c * weight_b, 2.0 * weight_c / spread

    for t in range(tiers):
        scaled = push_b * inv[t]
        for k in range(6):
            faces[k, t] = scaled * faces[k, t]
        inv[t] = inv[t] * (1.0 / middle)

    def layer_face(t):
        if t == 0 and t == tiers - 1:
            raise ValueError("one tier")
        return faces[0, t] if t == 0 else faces[1, t] if t == tiers - 1 else jnp.zeros((rows, cols), F32)

    first, last = slice(0, 1), slice(rows - 1, rows)
    side_face = [jnp.where(col_i == 0, faces[4, t], jnp.where(col_i == cols - 1, faces[5, t], 0.0)) for t in range(tiers)]
    ends_face = [jnp.where(row_i == 0, faces[2, t], jnp.where(row_i == rows - 1, faces[3, t], 0.0)) for t in range(tiers)]
    gain_send[0] = rows_of(lambda t: faces[2, t, first, :], lambda t: faces[3, t, last, :])
    gain_send[1] = rows_of(lambda t: layer_face(t)[first, :], lambda t: layer_face(t)[last, :])
    gain_send[2] = rows_of(lambda t: side_face[t][first, :], lambda t: side_face[t][last, :])
    gain_send[3] = columns_of(lambda t: side_face[t])
    gain_send[4] = columns_of(layer_face)
    gain_send[5] = columns_of(lambda t: ends_face[t])
    blank = jnp.zeros((rows, cols), F32)
    column_gain[0] = columns_of(lambda t: jnp.where(col_i == 0, faces[5, t], faces[4, t]))
    column_gain[1] = columns_of(lambda t: jnp.where(row_i == 0, 0.0, faces[2, t]))
    column_gain[2] = columns_of(lambda t: jnp.where(row_i == rows - 1, 0.0, faces[3, t]))
    column_gain[3] = columns_of(lambda t: faces[0, t] if t > 0 else blank)
    column_gain[4] = columns_of(lambda t: faces[1, t] if t < tiers - 1 else blank)
    for exists, where, side in sides[:2]:
        t = 0 if side == 0 else tiers - 1
        face_send[side, 0] = faces[side, t]
        face_send[side, 1] = ends_face[t]
        face_send[side, 2] = side_face[t]

        @pl.when(exists)
        def _(where=where, side=side):
            send(face_send.at[side], face_recv.at[side ^ 1], out_sem, face_rsem, where)

    for exists, where, side in sides[2:]:
        lands = (side - 2) ^ 1

        @pl.when(exists)
        def _(where=where, side=side, lands=lands):
            send(
                gain_send.at[0:3] if side < 4 else gain_send.at[3:6],
                gain_recv.at[3 * lands : 3 * lands + 3],
                out_sem,
                gain_rsem,
                where,
            )

    sources = tiles * CAP * FOLDS
    sel_i = iota((FOLDS * patches, sources), 0)
    sel_j = iota((FOLDS * patches, sources), 1)
    sel_in = mod(sel_i, patches)
    sel_patch = mod(sel_in, bands) * per_band + div(sel_in, bands)
    fold_hit = div(sel_i, patches) == mod(sel_j, FOLDS)
    bytes_of(place_recv, place_rsem).wait()
    def by_source(ref):
        taken = jnp.concatenate([jnp.broadcast_to(ref[tile], (rows_of_tile, LANES)) for tile in range(tiles)], axis=0)
        rank = div(mod(iota(taken.shape, 0), rows_of_tile), FOLDS)
        return jnp.sum(jnp.where(iota(taken.shape, 1) == rank * (LANES // CAP), taken, 0.0), axis=1, keepdims=True)

    same = iota((sources, sources), 0) == iota((sources, sources), 1)
    code = jnp.sum(jnp.where(same, by_source(place_recv), 0.0), axis=0, keepdims=True)
    picker = jnp.where(fold_hit & (code == (sel_patch + 1).astype(F32)), 1.0, 0.0).astype(BF16)
    left = iota((bands, LANES), 1) < SUB

    def deposit(footprint, begin, end):
        for fold in range(FOLDS):
            for k in range(begin, end):
                lanes = slice((k - begin) * LANES, (k - begin + 1) * LANES)
                a = footprint[fold * patches : fold * patches + bands, lanes]
                b = footprint[fold * patches + bands : fold * patches + 2 * bands, lanes]
                at = 2 * (fold * halves + k)
                power_ref[pl.ds(at, bands, stride=SUB), :] = jnp.where(left, a, pltpu.roll(b, SUB, 1))
                power_ref[pl.ds(at + 1, bands, stride=SUB), :] = jnp.where(left, pltpu.roll(a, SUB, 1), b)

    bytes_of(fac_recv, fac_rsem).wait()
    factors = by_source(fac_recv)
    bytes_of(early_recv, early_rsem).wait()
    for half in range(EARLY):
        lanes = slice(half * LANES, (half + 1) * LANES)
        for tile in range(tiles):
            early_power[tile * rows_of_tile : (tile + 1) * rows_of_tile, lanes] = (
                early_recv[tile, 0, :, lanes].astype(F32)
                + factors[tile * rows_of_tile : (tile + 1) * rows_of_tile] * early_recv[tile, 1, :, lanes].astype(F32)
            ).astype(BF16)
    deposit(jnp.dot(picker, early_power[...], preferred_element_type=F32), 0, EARLY)
    bytes_of(load_recv, load_rsem).wait()
    deposit(
        jnp.dot(picker, load_recv[...].reshape(sources, wide - EARLY * LANES), preferred_element_type=F32), EARLY, halves
    )
    start, after = dirs.at[0], dirs.at[1]

    def begin_rows(t, begin, end):
        power_rows = power_ref[t * rows + begin : t * rows + end, :]
        start[t, begin:end, :] = (resid[t, begin:end, :] + power_rows) * inv[t, begin:end, :]

    for t in range(tiers):
        begin_rows(t, 0, 8)
        begin_rows(t, rows - 8, rows)

    def send_rims(which):
        for step, block, count, _ in which:
            exists, where = neighbour(*step)
            lands = slot_of[tuple(-d for d in step)]

            @pl.when(exists)
            def _(where=where, block=block, count=count, lands=lands):
                send(
                    rim_send.at[block : block + count],
                    rim_recv.at[lands : lands + count],
                    out_sem,
                    rim_rsem,
                    where,
                )

    def send_planes(turn, field):
        for exists, where, side in sides[:2]:
            halo_start(turn, field, exists, where, side)

    def around_sum(field, t):
        v, around = inside(field, t)
        value = None
        for k in range(6):
            if not (k == 0 and t == 0 or k == 1 and t == tiers - 1):
                term = faces[k, t] * around[k]
                value = term if value is None else value + term
        return v, value

    own_rows = rows_of(lambda t: start[t, first, :], lambda t: start[t, last, :])
    rim_send[0] = own_rows
    send_rims(rims_of[:8])
    stay = keep_b + push_b * (middle - 1.0)
    slab_lane = iota((8, cols), 1)

    def slab_row(t, begin, row, inward, shift):
        slab = slice(begin, begin + 8)
        v = start[t, slab, :]
        value = stay * v + faces[inward, t, slab, :] * pltpu.roll(v, shift, 0)
        value = value + faces[4, t, slab, :] * jnp.where(slab_lane == 0, 0.0, pltpu.roll(v, 1, 1))
        value = value + faces[5, t, slab, :] * jnp.where(slab_lane == cols - 1, 0.0, pltpu.roll(v, cols - 1, 1))
        if t > 0:
            value = value + faces[0, t, slab, :] * start[t - 1, slab, :]
        if t < tiers - 1:
            value = value + faces[1, t, slab, :] * start[t + 1, slab, :]
        return value[row : row + 1, :]

    rim_send[1] = rows_of(lambda t: slab_row(t, 0, 0, 3, 7), lambda t: slab_row(t, rows - 8, 7, 2, 1))
    send_rims(rims_of[12:14])
    for t in range(tiers):
        begin_rows(t, 8, rows - 8)
    send_planes(2, start)
    columns = columns_of(lambda t: start[t], both_picks)
    own_columns = columns[: 2 * tiers]
    rim_send[2] = own_columns
    rim_send[3] = (
        stay * own_columns
        + column_gain[0] * columns[2 * tiers :]
        + column_gain[1] * pltpu.roll(own_columns, 1, 1)
        + column_gain[2] * pltpu.roll(own_columns, rows - 1, 1)
        + column_gain[3] * pltpu.roll(own_columns, 1, 0)
        + column_gain[4] * pltpu.roll(own_columns, 2 * tiers - 1, 0)
    )
    send_rims(rims_of[14:])
    send_rims(rims_of[8:12])
    for t in range(tiers):
        v, value = around_sum(start, t)
        after[t] = stay * v + value
    send_planes(3, after)
    bytes_of(gain_recv, gain_rsem).wait()
    wait_plane(2)
    wait_plane(3)
    bytes_of(face_recv, face_rsem).wait()
    bytes_of(rim_recv, rim_rsem).wait()

    rim_a = rims(rim_recv[4], rim_recv[6])

    def beyond_rows(ref, t, scale, north, south, rim):
        ref[t, first, :] = ref[t, first, :] + scale * faces[2, t, first, :] * north
        ref[t, last, :] = ref[t, last, :] + scale * faces[3, t, last, :] * south
        face = jnp.where(col_i == 0, faces[4, t], faces[5, t])
        ref[t] = ref[t] + scale * face * rim[:, t * cols : (t + 1) * cols]

    second = resid
    for t in range(tiers):
        value = after[t]
        if t == 0:
            value = value + faces[0, t] * plane_recv[2, 0]
        if t == tiers - 1:
            value = value + faces[1, t] * plane_recv[2, 1]
        second[t] = value
        beyond_rows(
            second, t, 1.0, rim_recv[0, tiers + t : tiers + t + 1, :], rim_recv[2, t : t + 1, :], rim_a
        )

    for side, t in ((0, tiers - 1), (1, 0)):
        plane = plane_recv.at[3, side]
        rim = rims(rim_recv[16 + side], rim_recv[18 + side], t)
        plane[...] = (
            plane[...] + face_recv[side, 0] * start[0 if side == 0 else tiers - 1] + face_recv[side, 2] * rim
        )
        plane[first, :] = (
            plane[first, :] + face_recv[side, 1, first, :] * rim_recv[12 + side, tiers + t : tiers + t + 1, :]
        )
        plane[last, :] = plane[last, :] + face_recv[side, 1, last, :] * rim_recv[14 + side, t : t + 1, :]

    eight_s = iota((2 * tiers, cols), 0)
    eight_l = iota((2 * tiers, cols), 1)
    upper = eight_s >= tiers
    tier_s = mod(eight_s, tiers)

    def pair(a, b):
        return jnp.where(upper, a, b)

    def swap(x):
        return pltpu.roll(x, tiers, 0)

    def layer_part(down, up):
        return jnp.where(
            tier_s == 0, pltpu.roll(down, tiers + 1, 0), jnp.where(tier_s == tiers - 1, pltpu.roll(up, tiers - 1, 0), 0.0)
        )

    north_west, north_east, south_west, south_east = (rim_recv[8 + i] for i in range(4))

    def shell(own, at, layer_at, gain_at, side_part):
        return (
            pair(rim_recv[at + 1], rim_recv[at + 3])
            + pair(gain_recv[gain_at], gain_recv[gain_at + 3]) * swap(own)
            + pair(gain_recv[gain_at + 1], gain_recv[gain_at + 4])
            * layer_part(
                pair(rim_recv[layer_at], rim_recv[layer_at + 2]), pair(rim_recv[layer_at + 1], rim_recv[layer_at + 3])
            )
            + pair(gain_recv[gain_at + 2], gain_recv[gain_at + 5]) * side_part
        )

    row_shell = shell(
        own_rows,
        0,
        12,
        0,
        jnp.where(
            eight_l == 0,
            pltpu.roll(pair(north_west, south_west), 1, 1),
            pltpu.roll(pair(north_east, south_east), cols - 1, 1),
        ),
    )
    col_shell = shell(
        own_columns,
        4,
        16,
        6,
        jnp.where(
            eight_l == 0,
            pair(pltpu.roll(north_west, 1, 1), swap(north_east)),
            pair(swap(south_west), pltpu.roll(south_east, cols - 1, 1)),
        ),
    )
    rim_b = rims(col_shell, col_shell)

    lift = push_c / push_b
    old = 1.0 - lift * keep_b
    now = 1.0 + keep_c + lift - push_c
    for t in range(tiers):
        v, value = around_sum(second, t)
        if t == 0:
            value = value + faces[0, t] * plane_recv[3, 0]
        if t == tiers - 1:
            value = value + faces[1, t] * plane_recv[3, 1]
        out_ref[t] = temp[t] + old * start[t] + now * v + lift * value
        beyond_rows(
            out_ref, t, lift, row_shell[tiers + t : tiers + t + 1, :], row_shell[t : t + 1, :], rim_b
        )
    bytes_of(sent, out_sem).wait()


def hand_over(new, power, new_out, power_out, sem):
    moves = (pltpu.make_async_copy(power, power_out, sem.at[0]), pltpu.make_async_copy(new, new_out, sem.at[1]))
    for move in moves:
        move.start()
    for move in moves:
        move.wait()


def shards(sizes, temp, cond, mass, dyn, leak, panel, place, block, tier, sens):
    tiers, rows, cols = temp.shape
    slots, cells = dyn.shape[1:]
    tiles = sizes[0] * sizes[1]
    any_spec = pl.BlockSpec(memory_space=pl.ANY)
    vmem_spec = pl.BlockSpec(memory_space=pltpu.VMEM)
    grid = (tiers, rows, cols)
    peer_rows = 3 + CAP * (cells + EARLY * FOLDS * LANES) // (2 * LANES)
    sent_rows = (tiles - 1) * peer_rows + 14 * rows * cols // LANES + 40 * 2 * tiers * cols // LANES
    dma = pltpu.SemaphoreType.DMA
    new, power = pl.pallas_call(
        functools.partial(kernel, sizes),
        out_shape=(
            pltpu.VMEM(grid, F32),
            pltpu.VMEM((tiers * rows, cols), F32),
        ),
        in_specs=[any_spec] * 10,
        out_specs=(vmem_spec, vmem_spec),
        scratch_shapes=[
            pltpu.VMEM((1, slots), jnp.int32),
            pltpu.VMEM((1, slots), jnp.int32),
            pltpu.VMEM((1, slots), jnp.int32),
            pltpu.VMEM(tier.shape, jnp.int32),
            pltpu.VMEM(sens.shape, F32),
            pltpu.VMEM(grid, F32),
            pltpu.VMEM(grid, F32),
            pltpu.VMEM(grid, F32),
            pltpu.VMEM((slots, cells), BF16),
            pltpu.VMEM((slots, cells), BF16),
            pltpu.VMEM((cells // FOLDS // LANES, tiles * CAP * FOLDS, LANES), F32),
            pltpu.VMEM((cells // FOLDS // LANES, tiles * CAP * FOLDS, LANES), F32),
            pltpu.VMEM((1, LANES), F32),
            pltpu.VMEM((tiles, 1, LANES), F32),
            pltpu.VMEM((tiles, 1, LANES), F32),
            pltpu.VMEM((tiles, 1, LANES), F32),
            pltpu.VMEM((8 * tiles, LANES), F32),
            pltpu.VMEM((tiles, 1, LANES), F32),
            pltpu.VMEM((tiles, 1, LANES), F32),
            pltpu.VMEM((tiles, 2, CAP * FOLDS, EARLY * LANES), BF16),
            pltpu.VMEM((tiles, 2, CAP * FOLDS, EARLY * LANES), BF16),
            pltpu.VMEM((tiles * CAP * FOLDS, EARLY * LANES), BF16),
            pltpu.VMEM((tiles, CAP * FOLDS, cells // FOLDS - EARLY * LANES), BF16),
            pltpu.VMEM((tiles, CAP * FOLDS, cells // FOLDS - EARLY * LANES), BF16),
            pltpu.VMEM((SWEEPS - 1,) + grid, F32),
            pltpu.VMEM((6,) + grid, F32),
            pltpu.VMEM(grid, F32),
            pltpu.VMEM(grid, F32),
            pltpu.VMEM(grid, F32),
            pltpu.VMEM((5, 2 * tiers, cols), F32),
            pltpu.VMEM((2, 2, 2 * tiers, cols), F32),
            pltpu.VMEM((2, 4, 2 * tiers, cols), F32),
            pltpu.VMEM((2, 4, 2 * tiers, cols), F32),
            pltpu.VMEM((4, 2, rows, cols), F32),
            pltpu.VMEM((4, 2, rows, cols), F32),
            pltpu.VMEM((4, 2 * tiers, cols), F32),
            pltpu.VMEM((20, 2 * tiers, cols), F32),
            pltpu.VMEM((20, 2 * tiers, cols), F32),
            pltpu.VMEM((6, 2 * tiers, cols), F32),
            pltpu.VMEM((12, 2 * tiers, cols), F32),
            pltpu.VMEM((12, 2 * tiers, cols), F32),
            pltpu.VMEM((2, 3, rows, cols), F32),
            pltpu.VMEM((2, 3, rows, cols), F32),
            pltpu.VMEM((2, 3, rows, cols), F32),
            pltpu.VMEM((rows, cols), F32),
            pltpu.VMEM((sent_rows, 1, LANES), F32),
            dma((10,)),
            dma(()),
            dma(()),
            dma(()),
            dma(()),
            dma(()),
            dma(()),
            dma((4, 2)),
            dma(()),
            dma(()),
            dma(()),
        ],
        compiler_params=pltpu.CompilerParams(
            collective_id=0, has_side_effects=True, vmem_limit_bytes=VMEM_BYTES
        ),
    )(
        *(
            pltpu.with_memory_space_constraint(given, pltpu.HBM)
            for given in (temp, cond, mass, dyn, leak, panel.reshape(1, slots), place, block, tier, sens)
        )
    )
    return pl.pallas_call(
        hand_over,
        out_shape=(jax.ShapeDtypeStruct(grid, F32),) * 2,
        in_specs=[vmem_spec] * 2,
        out_specs=(any_spec, any_spec),
        scratch_shapes=[dma((2,))],
        compiler_params=pltpu.CompilerParams(vmem_limit_bytes=VMEM_BYTES),
    )(new, power.reshape(grid))


def solution(mesh):
    sizes = (mesh.shape["row"], mesh.shape["col"], mesh.shape["layer"])
    owner = ("row", "col", "layer")
    return jax.shard_map(
        functools.partial(shards, sizes),
        mesh=mesh,
        in_specs=(P("layer", "row", "col"),) * 3
        + (P(owner, None, None),) * 3
        + (P(owner, None),) * 4,
        out_specs=(P("layer", "row", "col"), P("layer", "row", "col")),
        check_vma=False,
    )
```

```python
import functools
import jax
import jax.numpy as jnp
from jax import lax
from jax.experimental import pallas as pl
from jax.experimental.pallas import tpu as pltpu
from jax.sharding import PartitionSpec as P

SUB = 64
SWEEPS = 3
CAP = 4
EIG_LOW = 0.1
EIG_HIGH = 2.0
LANES = 128
FOLDS = 4
EARLY = 1
VMEM_BYTES = 40 << 20

MESH = pl.DeviceIdType.MESH
F32 = jnp.float32
BF16 = jnp.bfloat16


def iota(shape, dim):
    return lax.broadcasted_iota(jnp.int32, shape, dim)


def div(x, n):
    if n & (n - 1):
        return x // n
    return lax.shift_right_logical(x, jnp.int32(n.bit_length() - 1))


def mod(x, n):
    if n & (n - 1):
        return lax.rem(x, n)
    return x & (n - 1)


def three_parts(x, axis):
    head = x.astype(BF16)
    rest = x - head.astype(F32)
    body = rest.astype(BF16)
    return jnp.concatenate([head, body, (rest - body.astype(F32)).astype(BF16)], axis=axis)


def two_parts(x, axis):
    head = x.astype(BF16)
    return jnp.concatenate([head, (x - head.astype(F32)).astype(BF16)], axis=axis)


def kernel(
    sizes,
    temp_hbm,
    cond_hbm,
    mass_hbm,
    dyn_hbm,
    leak_hbm,
    panel_hbm,
    place_hbm,
    block_hbm,
    tier_hbm,
    sens_hbm,
    out_ref,
    power_ref,
    panel_ref,
    place_ref,
    block_ref,
    tier_ref,
    sens_ref,
    temp,
    cond,
    mass,
    dyn,
    leak,
    dyn_pick,
    leak_pick,
    note_send,
    note_recv,
    place_send,
    place_recv,
    fac,
    fac_send,
    fac_recv,
    early_send,
    early_recv,
    early_power,
    load_send,
    load_recv,
    dirs,
    faces,
    diag,
    inv,
    resid,
    column_gain,
    edge_send,
    edge_recv,
    edge_spare,
    plane_recv,
    plane_spare,
    rim_send,
    rim_recv,
    rim_spare,
    gain_send,
    gain_recv,
    gain_spare,
    face_send,
    face_recv,
    face_spare,
    nothing,
    sent,
    in_sem,
    out_sem,
    note_rsem,
    place_rsem,
    fac_rsem,
    early_rsem,
    load_rsem,
    halo_rsem,
    rim_rsem,
    gain_rsem,
    face_rsem,
):
    n_row, n_col, n_layer = sizes
    tiles = n_row * n_col
    tiers, rows, cols = temp.shape
    slots, cells = dyn.shape
    wide = cells // FOLDS
    halves = wide // LANES
    rows_of_tile = CAP * FOLDS
    named = 8 * tiles
    in_plane = (rows // SUB) * (cols // SUB)
    patches = tiers * in_plane
    bands = tiers * (rows // SUB)
    my_row = lax.axis_index("row")
    my_col = lax.axis_index("col")
    my_layer = lax.axis_index("layer")
    me = my_row * n_col + my_col

    loads = [
        pltpu.make_async_copy(src, dst, in_sem.at[i])
        for i, (src, dst) in enumerate(
            (
                (temp_hbm, temp),
                (panel_hbm, panel_ref),
                (place_hbm, place_ref),
                (block_hbm, block_ref),
                (tier_hbm, tier_ref),
                (sens_hbm, sens_ref),
                (dyn_hbm.at[0], dyn),
                (leak_hbm.at[0], leak),
                (cond_hbm, cond),
                (mass_hbm, mass),
            )
        )
    ]
    for load in loads:
        load.start()

    def far_first(step):
        if n_row & (n_row - 1) or n_col & (n_col - 1) or n_col == 1:
            return lax.rem(me + step, tiles)
        near = n_col // 2
        turn = mod(step, tiles // 2)
        over_row = n_row - 1 - div(turn, near)
        over_col = n_col - 1 - mod(turn, near) - near * div(step, tiles // 2)
        return lax.bitwise_xor(my_row, over_row) * n_col + lax.bitwise_xor(my_col, over_col)

    def low_first(step):
        if n_row & (n_row - 1) or n_col & (n_col - 1) or n_row == 1 or n_col == 1:
            return lax.rem(me + step, tiles)
        near = n_col // 2
        group, turn = div(step, tiles // 2), mod(step, tiles // 2)
        over, turn = div(turn, tiles // 4), mod(turn, tiles // 4)
        over_row = n_row // 2 - 1 - div(turn, near)
        over_col = n_col - 1 - mod(turn, near) - near * over
        row = group * (n_row // 2) + lax.bitwise_xor(mod(my_row, n_row // 2), over_row)
        return row * n_col + lax.bitwise_xor(my_col, over_col)

    def each_peer(act, order=far_first):
        @pl.loop(0, tiles)
        def _(step):
            other = order(step)
            pl.when(other != me)(lambda: act(other))

    def device(other):
        return {"row": div(other, n_col), "col": mod(other, n_col)}

    sides = (
        (my_layer > 0, {"layer": my_layer - 1}, 0),
        (my_layer < n_layer - 1, {"layer": my_layer + 1}, 1),
        (my_row > 0, {"row": my_row - 1}, 2),
        (my_row < n_row - 1, {"row": my_row + 1}, 3),
        (my_col > 0, {"col": my_col - 1}, 4),
        (my_col < n_col - 1, {"col": my_col + 1}, 5),
    )

    def neighbour(d_row, d_col, d_layer):
        exists, where = [], {}
        for axis, mine, count, d in (
            ("row", my_row, n_row, d_row),
            ("col", my_col, n_col, d_col),
            ("layer", my_layer, n_layer, d_layer),
        ):
            if d:
                exists.append(mine > 0 if d < 0 else mine < count - 1)
                where[axis] = mine + d
        return functools.reduce(jnp.logical_and, exists), where

    rims_of = (
        [((a, b, 0), 0, 1, 8 + i) for i, (a, b) in enumerate(((-1, -1), (-1, 1), (1, -1), (1, 1)))]
        + [((a, 0, c), 0, 1, 12 + i) for i, (a, c) in enumerate(((-1, -1), (-1, 1), (1, -1), (1, 1)))]
        + [((0, b, c), 2, 1, 16 + i) for i, (b, c) in enumerate(((-1, -1), (-1, 1), (1, -1), (1, 1)))]
        + [((-1, 0, 0), 0, 2, 0), ((1, 0, 0), 0, 2, 2), ((0, -1, 0), 2, 2, 4), ((0, 1, 0), 2, 2, 6)]
    )
    slot_of = {step: slot for step, _, _, slot in rims_of}

    nothing[...] = jnp.zeros_like(nothing)
    barrier = pltpu.get_barrier_semaphore()

    each_peer(
        lambda other: pl.semaphore_signal(barrier, inc=1, device_id=device(other), device_id_type=MESH)
    )

    across = [neighbour(*step) for step, _, _, _ in rims_of if step[2]] + [neighbour(0, 0, -1), neighbour(0, 0, 1)]
    for exists, where in across:

        @pl.when(exists)
        def _(where=where):
            pl.semaphore_signal(barrier, inc=1, device_id=where, device_id_type=MESH)

    def remote(src, dst, ssem, rsem, other):
        return pltpu.make_async_remote_copy(
            src_ref=src,
            dst_ref=dst,
            send_sem=ssem,
            recv_sem=rsem,
            device_id=device(other),
            device_id_type=MESH,
        )

    def note_copy(other):
        return remote(note_send, note_recv.at[me], out_sem, note_rsem, other)

    def place_copy(other):
        return remote(place_send.at[other], place_recv.at[me], out_sem, place_rsem, other)

    def fac_copy(other):
        return remote(fac_send.at[other], fac_recv.at[me], out_sem, fac_rsem, other)

    def early_copy(other):
        return remote(early_send.at[other], early_recv.at[me], out_sem, early_rsem, other)

    def load_copy(other):
        return remote(load_send.at[other], load_recv.at[me], out_sem, load_rsem, other)

    def send(src, dst, ssem, rsem, where):
        pltpu.make_async_remote_copy(
            src_ref=src, dst_ref=dst, send_sem=ssem, recv_sem=rsem, device_id=where, device_id_type=MESH
        ).start()

    def bytes_of(ref, sem):
        return pltpu.make_async_copy(ref, ref, sem)

    def keep(src, dst, sem):
        pltpu.make_async_copy(src, dst, sem).start()

    loads[0].wait()
    band_sums = jnp.concatenate(
        [
            jnp.sum(temp[t, b * SUB : (b + 1) * SUB, :], axis=0, keepdims=True)
            for t in range(tiers)
            for b in range(rows // SUB)
        ],
        axis=0,
    )
    lane_b = iota((bands, LANES), 1)
    sub_b = iota((bands, LANES), 0)
    means = jnp.zeros((1, LANES), F32)
    per_band = cols // SUB
    for part in range(per_band):
        total = jnp.sum(jnp.where(div(lane_b, SUB) == part, band_sums, 0.0), axis=1, keepdims=True)
        means = means + jnp.sum(
            jnp.where(lane_b == sub_b * per_band + part, total, 0.0), axis=0, keepdims=True
        )
    means = means * (1.0 / (SUB * SUB))
    note_send[...] = means
    lane_s = iota((slots, slots), 1)
    sub_s = iota((slots, slots), 0)
    eye = lane_s == sub_s

    def to_col(row):
        return jnp.sum(jnp.where(eye, jnp.broadcast_to(row, (slots, slots)), 0.0), axis=1, keepdims=True)

    def to_row(col):
        return jnp.sum(jnp.where(eye, jnp.broadcast_to(col, (slots, slots)), 0.0), axis=0, keepdims=True)

    for load in loads[1:6]:
        load.wait()
    tgt_row = panel_ref[...].astype(F32)
    tgt_col = to_col(tgt_row)
    blk_row = block_ref[...].astype(F32)
    blk_col = to_col(blk_row)
    sub_col = to_col(place_ref[...].astype(F32))
    same_tile = tgt_col == tgt_row
    rank_col = jnp.sum(jnp.where(same_tile & (lane_s < sub_s), 1.0, 0.0), axis=1, keepdims=True)
    rank_row = jnp.sum(jnp.where(same_tile & (sub_s < lane_s), 1.0, 0.0), axis=0, keepdims=True)
    blocks = tier_ref.shape[1]
    of_block = blk_col == iota((slots, blocks), 1).astype(F32)
    tier_col = jnp.sum(jnp.where(of_block, tier_ref[...].astype(F32), 0.0), axis=1, keepdims=True)
    sens_col = jnp.sum(jnp.where(of_block, sens_ref[...], 0.0), axis=1, keepdims=True)
    pos_col = tier_col * in_plane + sub_col
    goes = (tgt_row * CAP + rank_row) == iota((tiles * CAP, slots), 0).astype(F32)
    pick = jnp.where(goes, 1.0, 0.0).astype(BF16)
    loads[6].wait()
    loads[7].wait()
    for src, dst in ((dyn, dyn_pick), (leak, leak_pick)):
        for fold in range(FOLDS):
            taken = jnp.dot(pick, src[:, fold * wide : (fold + 1) * wide], preferred_element_type=F32)
            for half in range(halves):
                dst[half, pl.ds(fold, tiles * CAP, stride=FOLDS), :] = taken[
                    :, half * LANES : (half + 1) * LANES
                ]
    for tile in range(tiles):
        for half in range(EARLY):
            at, lanes = slice(tile * rows_of_tile, (tile + 1) * rows_of_tile), slice(half * LANES, (half + 1) * LANES)
            early_send[tile, 0, :, lanes] = dyn_pick[half, at, :].astype(BF16)
            early_send[tile, 1, :, lanes] = leak_pick[half, at, :].astype(BF16)

    beyond = sum(exists.astype(jnp.int32) for exists, _ in across)
    pl.semaphore_wait(barrier, tiles - 1 + beyond)

    each_peer(lambda other: note_copy(other).start())
    keep(note_send, note_recv.at[me], note_rsem)
    each_peer(lambda other: early_copy(other).start(), low_first)
    keep(early_send.at[me], early_recv.at[me], early_rsem)

    sub8 = iota((2 * tiers, 2 * cols), 0)
    lane8 = mod(iota((2 * tiers, 2 * cols), 1), cols)
    picks = [
        jnp.where(
            ((sub8 == t) & (lane8 == 0)) | ((sub8 == tiers + t) & (lane8 == cols - 1)), 1.0, 0.0
        ).astype(BF16)
        for t in range(tiers)
    ]

    sub16 = iota((4 * tiers, 2 * cols), 0)
    lane16 = mod(iota((4 * tiers, 2 * cols), 1), cols)
    both_picks = [
        jnp.where(
            ((sub16 == t) & (lane16 == 0))
            | ((sub16 == tiers + t) & (lane16 == cols - 1))
            | ((sub16 == 2 * tiers + t) & (lane16 == 1))
            | ((sub16 == 3 * tiers + t) & (lane16 == cols - 2)),
            1.0,
            0.0,
        ).astype(BF16)
        for t in range(tiers)
    ]

    def halo_ends(turn, field, side, lands):
        if side < 2:
            return field.at[0 if side == 0 else tiers - 1], plane_recv.at[turn, lands], 0
        return edge_send.at[turn, (side - 2) // 2], edge_recv.at[turn, lands - 2], 1

    def halo_start(turn, field, exists, where, side):
        @pl.when(exists)
        def _():
            src, dst, kind = halo_ends(turn, field, side, side ^ 1)
            send(src, dst, out_sem, halo_rsem.at[turn, kind], where)

    def pack_rows(turn, field):
        for end in range(2):
            at = end * (rows - 1)
            for t in range(tiers):
                edge_send[turn, 0, end * tiers + t : end * tiers + t + 1, :] = field[t, at : at + 1, :]

    def columns_of(field, taking=picks):
        columns = jnp.zeros((taking[0].shape[0], rows), F32)
        for t in range(tiers):
            columns = columns + lax.dot_general(
                taking[t], two_parts(field(t), 1), (((1,), (1,)), ((), ())), preferred_element_type=F32
            )
        return columns

    def rows_of(first, last):
        return jnp.concatenate([first(t) for t in range(tiers)] + [last(t) for t in range(tiers)], axis=0)

    def start_halo(turn, field):
        def start(which):
            for exists, where, side in which:
                halo_start(turn, field, exists, where, side)

        pack_rows(turn, field)
        start(sides[2:4])
        start(sides[:2])
        edge_send[turn, 1] = columns_of(lambda t: field[t])
        start(sides[4:])

    def wait_plane(turn):
        bytes_of(plane_recv.at[turn], halo_rsem.at[turn, 0]).wait()

    def wait_halo(turn):
        wait_plane(turn)
        bytes_of(edge_recv.at[turn], halo_rsem.at[turn, 1]).wait()

    row_i = iota((rows, cols), 0)
    col_i = iota((rows, cols), 1)
    sub16 = mod(iota((8 * tiers, tiers * cols), 0), 4 * tiers)
    lane16 = iota((8 * tiers, tiers * cols), 1)
    put = jnp.where(
        ((mod(lane16, cols) == 0) & (sub16 == tiers + div(lane16, cols)))
        | ((mod(lane16, cols) == cols - 1) & (sub16 == 2 * tiers + div(lane16, cols))),
        1.0,
        0.0,
    ).astype(BF16)

    def inside(field, t):
        v = field[t]
        none = jnp.zeros_like(v)
        low = none if t == 0 else field[t - 1]
        high = none if t == tiers - 1 else field[t + 1]
        north = jnp.where(row_i == 0, 0.0, pltpu.roll(v, 1, 0))
        south = jnp.where(row_i == rows - 1, 0.0, pltpu.roll(v, rows - 1, 0))
        west = jnp.where(col_i == 0, 0.0, pltpu.roll(v, 1, 1))
        east = jnp.where(col_i == cols - 1, 0.0, pltpu.roll(v, cols - 1, 1))
        return v, (low, high, north, south, west, east)

    def rims(west, east, t=None):
        ends = jnp.concatenate([west, east], axis=0)
        into = put if t is None else put[:, t * cols : (t + 1) * cols]
        return lax.dot_general(
            two_parts(ends, 0), into, (((0,), (0,)), ((), ())), preferred_element_type=F32
        )

    def apply_inside(field, t):
        v, around = inside(field, t)
        value = diag[t] * v
        for k in range(6):
            if not (k == 0 and t == 0 or k == 1 and t == tiers - 1):
                value = value - faces[k, t] * around[k]
        return value

    def add_beyond(turn):
        rim = rims(edge_recv[turn, 2], edge_recv[turn, 3])
        resid[0] = resid[0] + faces[0, 0] * plane_recv[turn, 0]
        resid[tiers - 1] = resid[tiers - 1] + faces[1, tiers - 1] * plane_recv[turn, 1]
        for t in range(tiers):
            first, last = slice(0, 1), slice(rows - 1, rows)
            resid[t, first, :] = (
                resid[t, first, :] + faces[2, t, first, :] * edge_recv[turn, 0, tiers + t : tiers + t + 1, :]
            )
            resid[t, last, :] = (
                resid[t, last, :] + faces[3, t, last, :] * edge_recv[turn, 1, t : t + 1, :]
            )
            face = jnp.where(col_i == 0, faces[4, t], faces[5, t])
            resid[t] = resid[t] + face * rim[:, t * cols : (t + 1) * cols]

    name_r = iota((named, slots), 0).astype(F32)
    named_row = tgt_row * 8.0 + rank_row
    named_col = tgt_col * 8.0 + rank_col
    by_name = name_r == named_row

    def rename(row):
        return jnp.sum(jnp.where(by_name, row, 0.0), axis=1, keepdims=True)

    pos_r = rename(to_row(pos_col) + 1.0)
    blk_r = rename(blk_row + 1.0)
    sens_r = rename(to_row(sens_col))
    blk_n = jnp.sum(
        jnp.where(named_col == iota((slots, named), 1).astype(F32), blk_col + 1.0, 0.0), axis=0, keepdims=True
    )
    same_block = jnp.where((blk_r == blk_n) & (blk_r > 0.0), 1.0, 0.0)
    block_size = jnp.maximum(jnp.sum(same_block, axis=1, keepdims=True), 1.0)
    same_three = jnp.concatenate([same_block.astype(BF16)] * 3, axis=1)
    at_place = (iota((named, LANES), 1) + 1).astype(F32) == pos_r
    group = div(iota((8, LANES), 1), LANES // CAP) == iota((8, LANES), 0)

    def one_row(block):
        return jnp.sum(jnp.where(group, block, 0.0), axis=0, keepdims=True)

    for tile in range(tiles):
        place_send[tile] = one_row(jnp.broadcast_to(pos_r[tile * 8 : (tile + 1) * 8], (8, LANES)))
    each_peer(lambda other: place_copy(other).start())
    keep(place_send.at[me], place_recv.at[me], place_rsem)

    loads[8].wait()
    start_halo(0, temp)
    start_halo(1, cond)

    bytes_of(note_recv, note_rsem).wait()
    tile_means = jnp.concatenate([jnp.broadcast_to(note_recv[tile], (8, LANES)) for tile in range(tiles)], axis=0)
    at_slots = three_parts(jnp.where(at_place, tile_means, 0.0), 0)
    block_sum = jnp.sum(
        jnp.dot(same_three, at_slots, preferred_element_type=F32), axis=1, keepdims=True
    )
    fac[:named, :] = jnp.broadcast_to(jnp.exp(sens_r * (block_sum / block_size)), (named, LANES))

    upper_rank = iota((8, LANES), 0) >= FOLDS
    def load_step(step):
        other = low_first(step)

        def factor_of(rank):
            return fac[pl.ds(other * 8 + rank, 8, stride=0), :]

        by = jnp.concatenate(
            [jnp.where(upper_rank, factor_of(rank + 1), factor_of(rank)) for rank in range(0, CAP, 2)], axis=0
        )
        at = pl.ds(pl.multiple_of(other * rows_of_tile, rows_of_tile), rows_of_tile)
        for half in range(EARLY, halves):
            load_send[other, :, (half - EARLY) * LANES : (half - EARLY + 1) * LANES] = (
                dyn_pick[half, at, :] + by * leak_pick[half, at, :]
            ).astype(BF16)

        @pl.when(other != me)
        def _():
            load_copy(other).start()

    pl.loop(0, tiles // 8)(load_step)
    for tile in range(tiles):
        fac_send[tile] = one_row(fac[tile * 8 : (tile + 1) * 8, :])
    each_peer(lambda other: fac_copy(other).start(), low_first)
    keep(fac_send.at[me], fac_recv.at[me], fac_rsem)
    pl.loop(tiles // 8, tiles)(load_step)
    keep(load_send.at[me], load_recv.at[me], load_rsem)
    def missing(exists, blocks):
        @pl.when(jnp.logical_not(exists))
        def _():
            for recv, spare, at, ssem, rsem, none in blocks:
                keep(none, recv.at[at], rsem)
                keep(none, spare.at[at], ssem)

    none8 = nothing.at[:8, :]
    for exists, _, side in sides[:2]:
        missing(
            exists,
            [
                (plane_recv.at[turn], plane_spare.at[turn], side, out_sem, halo_rsem.at[turn, 0], nothing)
                for turn in range(4)
            ]
            + [(face_recv.at[side], face_spare.at[side], k, out_sem, face_rsem, nothing) for k in range(3)],
        )
    for exists, _, side in sides[2:]:
        missing(
            exists,
            [
                (edge_recv.at[turn], edge_spare.at[turn], side - 2, out_sem, halo_rsem.at[turn, 1], none8)
                for turn in range(2)
            ]
            + [(gain_recv, gain_spare, 3 * (side - 2) + k, out_sem, gain_rsem, none8) for k in range(3)],
        )
    for step, _, count, slot in rims_of:
        missing(
            neighbour(*step)[0],
            [(rim_recv, rim_spare, slot + k, out_sem, rim_rsem, none8) for k in range(count)],
        )
    loads[9].wait()
    wait_halo(0)
    wait_halo(1)
    rim = rims(edge_recv[1, 2], edge_recv[1, 3])
    for t in range(tiers):
        c, (low, high, north, south, west, east) = inside(cond, t)
        here = rim[:, t * cols : (t + 1) * cols]
        low = plane_recv[1, 0] if t == 0 else low
        high = plane_recv[1, 1] if t == tiers - 1 else high
        north = jnp.where(row_i == 0, edge_recv[1, 0, tiers + t : tiers + t + 1, :], north)
        south = jnp.where(row_i == rows - 1, edge_recv[1, 1, t : t + 1, :], south)
        west = jnp.where(col_i == 0, here, west)
        east = jnp.where(col_i == cols - 1, here, east)
        total = mass[t]
        for k, beside in enumerate((low, high, north, south, west, east)):
            face = 0.5 * (c + beside)
            faces[k, t] = face
            total = total + face
        diag[t] = total
        inv[t] = 1.0 / total
    for t in range(tiers):
        resid[t] = mass[t] * temp[t] - apply_inside(temp, t)
    add_beyond(0)

    middle = (EIG_LOW + EIG_HIGH) / 2.0
    spread = (EIG_HIGH - EIG_LOW) / 2.0
    ratio = middle / spread
    weight_a = 1.0 / ratio
    weight_b = 1.0 / (2.0 * ratio - weight_a)
    weight_c = 1.0 / (2.0 * ratio - weight_b)
    keep_b, push_b = weight_b * weight_a, 2.0 * weight_b / spread
    keep_c, push_c = weight_c * weight_b, 2.0 * weight_c / spread

    for t in range(tiers):
        scaled = push_b * inv[t]
        for k in range(6):
            faces[k, t] = scaled * faces[k, t]
        inv[t] = inv[t] * (1.0 / middle)

    def layer_face(t):
        if t == 0 and t == tiers - 1:
            raise ValueError("one tier")
        return faces[0, t] if t == 0 else faces[1, t] if t == tiers - 1 else jnp.zeros((rows, cols), F32)

    first, last = slice(0, 1), slice(rows - 1, rows)
    side_face = [jnp.where(col_i == 0, faces[4, t], jnp.where(col_i == cols - 1, faces[5, t], 0.0)) for t in range(tiers)]
    ends_face = [jnp.where(row_i == 0, faces[2, t], jnp.where(row_i == rows - 1, faces[3, t], 0.0)) for t in range(tiers)]
    gain_send[0] = rows_of(lambda t: faces[2, t, first, :], lambda t: faces[3, t, last, :])
    gain_send[1] = rows_of(lambda t: layer_face(t)[first, :], lambda t: layer_face(t)[last, :])
    gain_send[2] = rows_of(lambda t: side_face[t][first, :], lambda t: side_face[t][last, :])
    gain_send[3] = columns_of(lambda t: side_face[t])
    gain_send[4] = columns_of(layer_face)
    gain_send[5] = columns_of(lambda t: ends_face[t])
    blank = jnp.zeros((rows, cols), F32)
    column_gain[0] = columns_of(lambda t: jnp.where(col_i == 0, faces[5, t], faces[4, t]))
    column_gain[1] = columns_of(lambda t: jnp.where(row_i == 0, 0.0, faces[2, t]))
    column_gain[2] = columns_of(lambda t: jnp.where(row_i == rows - 1, 0.0, faces[3, t]))
    column_gain[3] = columns_of(lambda t: faces[0, t] if t > 0 else blank)
    column_gain[4] = columns_of(lambda t: faces[1, t] if t < tiers - 1 else blank)
    for exists, where, side in sides[:2]:
        t = 0 if side == 0 else tiers - 1
        face_send[side, 0] = faces[side, t]
        face_send[side, 1] = ends_face[t]
        face_send[side, 2] = side_face[t]

        @pl.when(exists)
        def _(where=where, side=side):
            send(face_send.at[side], face_recv.at[side ^ 1], out_sem, face_rsem, where)

    for exists, where, side in sides[2:]:
        lands = (side - 2) ^ 1

        @pl.when(exists)
        def _(where=where, side=side, lands=lands):
            send(
                gain_send.at[0:3] if side < 4 else gain_send.at[3:6],
                gain_recv.at[3 * lands : 3 * lands + 3],
                out_sem,
                gain_rsem,
                where,
            )

    sources = tiles * CAP * FOLDS
    sel_i = iota((FOLDS * patches, sources), 0)
    sel_j = iota((FOLDS * patches, sources), 1)
    sel_in = mod(sel_i, patches)
    sel_patch = mod(sel_in, bands) * per_band + div(sel_in, bands)
    fold_hit = div(sel_i, patches) == mod(sel_j, FOLDS)
    bytes_of(place_recv, place_rsem).wait()
    def by_source(ref):
        taken = jnp.concatenate([jnp.broadcast_to(ref[tile], (rows_of_tile, LANES)) for tile in range(tiles)], axis=0)
        rank = div(mod(iota(taken.shape, 0), rows_of_tile), FOLDS)
        return jnp.sum(jnp.where(iota(taken.shape, 1) == rank * (LANES // CAP), taken, 0.0), axis=1, keepdims=True)

    same = iota((sources, sources), 0) == iota((sources, sources), 1)
    code = jnp.sum(jnp.where(same, by_source(place_recv), 0.0), axis=0, keepdims=True)
    picker = jnp.where(fold_hit & (code == (sel_patch + 1).astype(F32)), 1.0, 0.0).astype(BF16)
    left = iota((bands, LANES), 1) < SUB

    def deposit(footprint, begin, end):
        for fold in range(FOLDS):
            for k in range(begin, end):
                lanes = slice((k - begin) * LANES, (k - begin + 1) * LANES)
                a = footprint[fold * patches : fold * patches + bands, lanes]
                b = footprint[fold * patches + bands : fold * patches + 2 * bands, lanes]
                at = 2 * (fold * halves + k)
                power_ref[pl.ds(at, bands, stride=SUB), :] = jnp.where(left, a, pltpu.roll(b, SUB, 1))
                power_ref[pl.ds(at + 1, bands, stride=SUB), :] = jnp.where(left, pltpu.roll(a, SUB, 1), b)

    bytes_of(fac_recv, fac_rsem).wait()
    factors = by_source(fac_recv)
    bytes_of(early_recv, early_rsem).wait()
    for half in range(EARLY):
        lanes = slice(half * LANES, (half + 1) * LANES)
        for tile in range(tiles):
            early_power[tile * rows_of_tile : (tile + 1) * rows_of_tile, lanes] = (
                early_recv[tile, 0, :, lanes].astype(F32)
                + factors[tile * rows_of_tile : (tile + 1) * rows_of_tile] * early_recv[tile, 1, :, lanes].astype(F32)
            ).astype(BF16)
    deposit(jnp.dot(picker, early_power[...], preferred_element_type=F32), 0, EARLY)
    bytes_of(load_recv, load_rsem).wait()
    deposit(
        jnp.dot(picker, load_recv[...].reshape(sources, wide - EARLY * LANES), preferred_element_type=F32), EARLY, halves
    )
    start, after = dirs.at[0], dirs.at[1]

    def begin_rows(t, begin, end):
        power_rows = power_ref[t * rows + begin : t * rows + end, :]
        start[t, begin:end, :] = (resid[t, begin:end, :] + power_rows) * inv[t, begin:end, :]

    for t in range(tiers):
        begin_rows(t, 0, 8)
        begin_rows(t, rows - 8, rows)

    def send_rims(which):
        for step, block, count, _ in which:
            exists, where = neighbour(*step)
            lands = slot_of[tuple(-d for d in step)]

            @pl.when(exists)
            def _(where=where, block=block, count=count, lands=lands):
                send(
                    rim_send.at[block : block + count],
                    rim_recv.at[lands : lands + count],
                    out_sem,
                    rim_rsem,
                    where,
                )

    def send_planes(turn, field):
        for exists, where, side in sides[:2]:
            halo_start(turn, field, exists, where, side)

    def around_sum(field, t):
        v, around = inside(field, t)
        value = None
        for k in range(6):
            if not (k == 0 and t == 0 or k == 1 and t == tiers - 1):
                term = faces[k, t] * around[k]
                value = term if value is None else value + term
        return v, value

    own_rows = rows_of(lambda t: start[t, first, :], lambda t: start[t, last, :])
    rim_send[0] = own_rows
    send_rims(rims_of[:8])
    stay = keep_b + push_b * (middle - 1.0)
    slab_lane = iota((8, cols), 1)

    def slab_row(t, begin, row, inward, shift):
        slab = slice(begin, begin + 8)
        v = start[t, slab, :]
        value = stay * v + faces[inward, t, slab, :] * pltpu.roll(v, shift, 0)
        value = value + faces[4, t, slab, :] * jnp.where(slab_lane == 0, 0.0, pltpu.roll(v, 1, 1))
        value = value + faces[5, t, slab, :] * jnp.where(slab_lane == cols - 1, 0.0, pltpu.roll(v, cols - 1, 1))
        if t > 0:
            value = value + faces[0, t, slab, :] * start[t - 1, slab, :]
        if t < tiers - 1:
            value = value + faces[1, t, slab, :] * start[t + 1, slab, :]
        return value[row : row + 1, :]

    rim_send[1] = rows_of(lambda t: slab_row(t, 0, 0, 3, 7), lambda t: slab_row(t, rows - 8, 7, 2, 1))
    send_rims(rims_of[12:14])
    for t in range(tiers):
        begin_rows(t, 8, rows - 8)
    send_planes(2, start)
    columns = columns_of(lambda t: start[t], both_picks)
    own_columns = columns[: 2 * tiers]
    rim_send[2] = own_columns
    rim_send[3] = (
        stay * own_columns
        + column_gain[0] * columns[2 * tiers :]
        + column_gain[1] * pltpu.roll(own_columns, 1, 1)
        + column_gain[2] * pltpu.roll(own_columns, rows - 1, 1)
        + column_gain[3] * pltpu.roll(own_columns, 1, 0)
        + column_gain[4] * pltpu.roll(own_columns, 2 * tiers - 1, 0)
    )
    send_rims(rims_of[14:])
    send_rims(rims_of[8:12])
    for t in range(tiers):
        v, value = around_sum(start, t)
        after[t] = stay * v + value
    send_planes(3, after)
    bytes_of(gain_recv, gain_rsem).wait()
    wait_plane(2)
    wait_plane(3)
    bytes_of(face_recv, face_rsem).wait()
    bytes_of(rim_recv, rim_rsem).wait()

    rim_a = rims(rim_recv[4], rim_recv[6])

    def beyond_rows(ref, t, scale, north, south, rim):
        ref[t, first, :] = ref[t, first, :] + scale * faces[2, t, first, :] * north
        ref[t, last, :] = ref[t, last, :] + scale * faces[3, t, last, :] * south
        face = jnp.where(col_i == 0, faces[4, t], faces[5, t])
        ref[t] = ref[t] + scale * face * rim[:, t * cols : (t + 1) * cols]

    second = resid
    for t in range(tiers):
        value = after[t]
        if t == 0:
            value = value + faces[0, t] * plane_recv[2, 0]
        if t == tiers - 1:
            value = value + faces[1, t] * plane_recv[2, 1]
        second[t] = value
        beyond_rows(
            second, t, 1.0, rim_recv[0, tiers + t : tiers + t + 1, :], rim_recv[2, t : t + 1, :], rim_a
        )

    for side, t in ((0, tiers - 1), (1, 0)):
        plane = plane_recv.at[3, side]
        rim = rims(rim_recv[16 + side], rim_recv[18 + side], t)
        plane[...] = (
            plane[...] + face_recv[side, 0] * start[0 if side == 0 else tiers - 1] + face_recv[side, 2] * rim
        )
        plane[first, :] = (
            plane[first, :] + face_recv[side, 1, first, :] * rim_recv[12 + side, tiers + t : tiers + t + 1, :]
        )
        plane[last, :] = plane[last, :] + face_recv[side, 1, last, :] * rim_recv[14 + side, t : t + 1, :]

    eight_s = iota((2 * tiers, cols), 0)
    eight_l = iota((2 * tiers, cols), 1)
    upper = eight_s >= tiers
    tier_s = mod(eight_s, tiers)

    def pair(a, b):
        return jnp.where(upper, a, b)

    def swap(x):
        return pltpu.roll(x, tiers, 0)

    def layer_part(down, up):
        return jnp.where(
            tier_s == 0, pltpu.roll(down, tiers + 1, 0), jnp.where(tier_s == tiers - 1, pltpu.roll(up, tiers - 1, 0), 0.0)
        )

    north_west, north_east, south_west, south_east = (rim_recv[8 + i] for i in range(4))

    def shell(own, at, layer_at, gain_at, side_part):
        return (
            pair(rim_recv[at + 1], rim_recv[at + 3])
            + pair(gain_recv[gain_at], gain_recv[gain_at + 3]) * swap(own)
            + pair(gain_recv[gain_at + 1], gain_recv[gain_at + 4])
            * layer_part(
                pair(rim_recv[layer_at], rim_recv[layer_at + 2]), pair(rim_recv[layer_at + 1], rim_recv[layer_at + 3])
            )
            + pair(gain_recv[gain_at + 2], gain_recv[gain_at + 5]) * side_part
        )

    row_shell = shell(
        own_rows,
        0,
        12,
        0,
        jnp.where(
            eight_l == 0,
            pltpu.roll(pair(north_west, south_west), 1, 1),
            pltpu.roll(pair(north_east, south_east), cols - 1, 1),
        ),
    )
    col_shell = shell(
        own_columns,
        4,
        16,
        6,
        jnp.where(
            eight_l == 0,
            pair(pltpu.roll(north_west, 1, 1), swap(north_east)),
            pair(swap(south_west), pltpu.roll(south_east, cols - 1, 1)),
        ),
    )
    rim_b = rims(col_shell, col_shell)

    lift = push_c / push_b
    old = 1.0 - lift * keep_b
    now = 1.0 + keep_c + lift - push_c
    for t in range(tiers):
        v, value = around_sum(second, t)
        if t == 0:
            value = value + faces[0, t] * plane_recv[3, 0]
        if t == tiers - 1:
            value = value + faces[1, t] * plane_recv[3, 1]
        out_ref[t] = temp[t] + old * start[t] + now * v + lift * value
        beyond_rows(
            out_ref, t, lift, row_shell[tiers + t : tiers + t + 1, :], row_shell[t : t + 1, :], rim_b
        )
    bytes_of(sent, out_sem).wait()


def hand_over(new, power, new_out, power_out, sem):
    moves = (pltpu.make_async_copy(power, power_out, sem.at[0]), pltpu.make_async_copy(new, new_out, sem.at[1]))
    for move in moves:
        move.start()
    for move in moves:
        move.wait()


def shards(sizes, temp, cond, mass, dyn, leak, panel, place, block, tier, sens):
    tiers, rows, cols = temp.shape
    slots, cells = dyn.shape[1:]
    tiles = sizes[0] * sizes[1]
    any_spec = pl.BlockSpec(memory_space=pl.ANY)
    vmem_spec = pl.BlockSpec(memory_space=pltpu.VMEM)
    grid = (tiers, rows, cols)
    peer_rows = 3 + CAP * (cells + EARLY * FOLDS * LANES) // (2 * LANES)
    sent_rows = (tiles - 1) * peer_rows + 14 * rows * cols // LANES + 40 * 2 * tiers * cols // LANES
    dma = pltpu.SemaphoreType.DMA
    new, power = pl.pallas_call(
        functools.partial(kernel, sizes),
        out_shape=(
            pltpu.VMEM(grid, F32),
            pltpu.VMEM((tiers * rows, cols), F32),
        ),
        in_specs=[any_spec] * 10,
        out_specs=(vmem_spec, vmem_spec),
        scratch_shapes=[
            pltpu.VMEM((1, slots), jnp.int32),
            pltpu.VMEM((1, slots), jnp.int32),
            pltpu.VMEM((1, slots), jnp.int32),
            pltpu.VMEM(tier.shape, jnp.int32),
            pltpu.VMEM(sens.shape, F32),
            pltpu.VMEM(grid, F32),
            pltpu.VMEM(grid, F32),
            pltpu.VMEM(grid, F32),
            pltpu.VMEM((slots, cells), BF16),
            pltpu.VMEM((slots, cells), BF16),
            pltpu.VMEM((cells // FOLDS // LANES, tiles * CAP * FOLDS, LANES), F32),
            pltpu.VMEM((cells // FOLDS // LANES, tiles * CAP * FOLDS, LANES), F32),
            pltpu.VMEM((1, LANES), F32),
            pltpu.VMEM((tiles, 1, LANES), F32),
            pltpu.VMEM((tiles, 1, LANES), F32),
            pltpu.VMEM((tiles, 1, LANES), F32),
            pltpu.VMEM((8 * tiles + 8, LANES), F32),
            pltpu.VMEM((tiles, 1, LANES), F32),
            pltpu.VMEM((tiles, 1, LANES), F32),
            pltpu.VMEM((tiles, 2, CAP * FOLDS, EARLY * LANES), BF16),
            pltpu.VMEM((tiles, 2, CAP * FOLDS, EARLY * LANES), BF16),
            pltpu.VMEM((tiles * CAP * FOLDS, EARLY * LANES), BF16),
            pltpu.VMEM((tiles, CAP * FOLDS, cells // FOLDS - EARLY * LANES), BF16),
            pltpu.VMEM((tiles, CAP * FOLDS, cells // FOLDS - EARLY * LANES), BF16),
            pltpu.VMEM((SWEEPS - 1,) + grid, F32),
            pltpu.VMEM((6,) + grid, F32),
            pltpu.VMEM(grid, F32),
            pltpu.VMEM(grid, F32),
            pltpu.VMEM(grid, F32),
            pltpu.VMEM((5, 2 * tiers, cols), F32),
            pltpu.VMEM((2, 2, 2 * tiers, cols), F32),
            pltpu.VMEM((2, 4, 2 * tiers, cols), F32),
            pltpu.VMEM((2, 4, 2 * tiers, cols), F32),
            pltpu.VMEM((4, 2, rows, cols), F32),
            pltpu.VMEM((4, 2, rows, cols), F32),
            pltpu.VMEM((4, 2 * tiers, cols), F32),
            pltpu.VMEM((20, 2 * tiers, cols), F32),
            pltpu.VMEM((20, 2 * tiers, cols), F32),
            pltpu.VMEM((6, 2 * tiers, cols), F32),
            pltpu.VMEM((12, 2 * tiers, cols), F32),
            pltpu.VMEM((12, 2 * tiers, cols), F32),
            pltpu.VMEM((2, 3, rows, cols), F32),
            pltpu.VMEM((2, 3, rows, cols), F32),
            pltpu.VMEM((2, 3, rows, cols), F32),
            pltpu.VMEM((rows, cols), F32),
            pltpu.VMEM((sent_rows, 1, LANES), F32),
            dma((10,)),
            dma(()),
            dma(()),
            dma(()),
            dma(()),
            dma(()),
            dma(()),
            dma((4, 2)),
            dma(()),
            dma(()),
            dma(()),
        ],
        compiler_params=pltpu.CompilerParams(
            collective_id=0, has_side_effects=True, vmem_limit_bytes=VMEM_BYTES
        ),
    )(
        *(
            pltpu.with_memory_space_constraint(given, pltpu.HBM)
            for given in (temp, cond, mass, dyn, leak, panel.reshape(1, slots), place, block, tier, sens)
        )
    )
    return pl.pallas_call(
        hand_over,
        out_shape=(jax.ShapeDtypeStruct(grid, F32),) * 2,
        in_specs=[vmem_spec] * 2,
        out_specs=(any_spec, any_spec),
        scratch_shapes=[dma((2,))],
        compiler_params=pltpu.CompilerParams(vmem_limit_bytes=VMEM_BYTES),
    )(new, power.reshape(grid))


def solution(mesh):
    sizes = (mesh.shape["row"], mesh.shape["col"], mesh.shape["layer"])
    owner = ("row", "col", "layer")
    return jax.shard_map(
        functools.partial(shards, sizes),
        mesh=mesh,
        in_specs=(P("layer", "row", "col"),) * 3
        + (P(owner, None, None),) * 3
        + (P(owner, None),) * 4,
        out_specs=(P("layer", "row", "col"), P("layer", "row", "col")),
        check_vma=False,
    )
```
